32 devices in a mesh: grp: 2 (over y), col: 4 (over z), row: 2 (over x), limb: 2 (over core).
Axes of the slice: x: 2, y: 2, z: 4, core: 2. Of those that a mesh axis runs over, the one named last changes fastest.
Arguments:
- database: bfloat16 [8192, 8192], P(('grp', 'row'), 'col'), parts along dimension 0, may hold values from -128 to 127, as said below
- lwe_matrix: bfloat16 [8192, 2, 512], P('col', 'limb'), may hold values from -0.0008544922 to 0.0008544922
- secret_ct: float32 [2, 2, 2, 512, 4096], P(None, None, 'limb', 'col', 'row'), may hold values from -6 to 6
Outputs:
- encrypted_product: float32 [4, 2, 4096], P('grp', None, 'row'), parts along dimension 0
The draws below stay inside these ranges and needn't reach their ends.
There are 2 independent parts, one for each index of `grp`. The reference program is written for one: setup_inputs(seed, part) draws one part's arguments, and reference() takes and returns one part's arrays. A program takes and returns all parts, laid end to end along the dimension named above; an argument that names none is the same for every part. Nothing has to cross between parts.
Inputs may be any that keep to these rules, and one draw needn't show every extreme that they name: `database`: whole numbers.
All inputs are finite; a program needn't handle non-finite values.
Results may differ from the reference program's by a relative error of at most 0.0003.
Values sent between devices are 32-bit elements; how exact they have to be, the bound alone decides.
A program may use at most 64 MiB of HBM per device.

```python
import math
import jax
import jax.numpy as jnp
from jax import lax

DEGREE = 4096
HALF = 512
COLUMNS = 8192
N_ROW = 2


def draw_database(key, part):
    values = jax.random.randint(key, (DEGREE, COLUMNS), -128, 128)
    return values.astype(jnp.float32).astype(jnp.bfloat16)


def level_of(stream_key, extent, shards, smallest, largest):
    def one(axis_at, blocks):
        heights = jax.random.uniform(jax.random.fold_in(jax.random.fold_in(stream_key, 6), axis_at), (blocks,), jnp.float32, smallest / len(shards), largest / len(shards))
        return jnp.repeat(jnp.exp(heights), extent[axis_at] // blocks).reshape((-1,) + (1,) * (len(extent) - axis_at - 1))

    factor_of = one(*shards[0])
    for cut in shards[1:]:
        factor_of = factor_of * one(*cut)
    return factor_of


def noise(stream_key, extent, scale, reach, pieces=(), held_as=jnp.bfloat16):
    gain = level_of(stream_key, extent, pieces, -0.22, 0.18) if pieces else 1.0
    result = jax.random.normal(stream_key, extent, jnp.float32) * scale * gain
    return jnp.minimum(jnp.maximum(result, -reach), reach).astype(held_as)


def setup_inputs(seed: int = 0, part: int = 0) -> dict:
    seeds = jax.random.split(jax.random.key(seed), 4)
    part_splits = jax.random.split(jax.random.fold_in(seeds[3], part), 4)
    return {
        "database": draw_database(jax.random.fold_in(jax.random.fold_in(seeds[3], part), 71), part),
        "lwe_matrix": noise(seeds[1], (COLUMNS, 2, HALF), (COLUMNS * 5461) ** -0.5, 0.0008544922, ((0, 4), (1, 2))),
        "secret_ct": noise(seeds[2], (2, 2, 2, HALF, DEGREE), 1.0, 6.0, ((2, 2), (3, 4), (4, 2)), jnp.float32),
    }


def reference(database, lwe_matrix, secret_ct):
    hint_full = jnp.dot(database, lwe_matrix.reshape(COLUMNS, 2 * HALF), preferred_element_type=jnp.float32)
    row_index = jnp.arange(DEGREE).astype(hint_full.dtype)
    twist_factor = jnp.exp(-1j * jnp.pi * row_index / DEGREE)
    spectrum = jnp.fft.fft(hint_full * twist_factor[:, None], axis=0) / math.sqrt(DEGREE)
    spectrum = spectrum.reshape(DEGREE // N_ROW, N_ROW, 2 * HALF).transpose(1, 0, 2).reshape(DEGREE, 2 * HALF)
    real_part = jnp.real(spectrum).T
    imag_part = jnp.imag(spectrum).T
    cipher = secret_ct.reshape(2, 2, 2 * HALF, DEGREE)
    out_real = lax.optimization_barrier(jnp.sum(real_part * cipher[:, 0] - imag_part * cipher[:, 1], axis=1))
    out_imag = lax.optimization_barrier(jnp.sum(real_part * cipher[:, 1] + imag_part * cipher[:, 0], axis=1))
    return jnp.stack([out_real, out_imag], axis=1) / math.sqrt(2 * HALF)
```

```python
import functools
import math

import jax
import jax.numpy as jnp
import numpy as np
from jax import lax
from jax.experimental import pallas as pl
from jax.experimental.pallas import tpu as pltpu
from jax.sharding import PartitionSpec as P

MESH = pl.DeviceIdType.MESH
UNIT = 8
LANES = 128
BLOCK = 256
EARLY = 2
LAG = 2


def fft(values):
    count = len(values)
    if count == 1:
        return values
    even, odd = fft(values[0::2]), fft(values[1::2])
    low, high = [], []
    for k in range(count // 2):
        (er, ei), (r, i) = even[k], odd[k]
        if k == 0:
            tr, ti = r, i
        elif 4 * k == count:
            tr, ti = i, -r
        elif 8 * k == count:
            half = math.sqrt(0.5)
            tr, ti = (r + i) * half, (i - r) * half
        elif 8 * k == 3 * count:
            half = math.sqrt(0.5)
            tr, ti = (i - r) * half, -(r + i) * half
        else:
            c, s = math.cos(2 * math.pi * k / count), math.sin(2 * math.pi * k / count)
            tr, ti = r * c + i * s, i * c - r * s
        low.append((er + tr, ei + ti))
        high.append((er - tr, ei - ti))
    return low + high


def swap_bits(blocks):
    blocks = list(blocks)
    lane = lax.broadcasted_iota(jnp.int32, blocks[0].shape, 1)
    step = 1
    while step < len(blocks):
        clear = (lane & step) == 0
        for b in range(len(blocks)):
            if not b & step:
                x, y = blocks[b], blocks[b + step]
                blocks[b] = jnp.where(clear, x, pltpu.roll(y, step, 1))
                blocks[b + step] = jnp.where(clear, pltpu.roll(x, LANES - step, 1), y)
        step *= 2
    return blocks


def kernel(cols, rows, grps, shared, l_hbm, d_hbm, s_hbm, turn_hbm, twiddle_hbm, w_hbm, out_ref,
           l_buf, lt, d_buf, part, from_left, from_right, land, cipher, turn, twiddle, w, acc,
           half_sum, half_in, z_in, whole_sum,
           load_sem, d_sem, send_sem, recv_sem, row_send, row_recv, s_send, s_recv, y_send, y_recv,
           limb_send, limb_recv, z_send, z_recv):
    me, row = lax.axis_index("col"), lax.axis_index("row")
    grp, limb = lax.axis_index("grp"), lax.axis_index("limb")
    units, row_dev = part.shape[1], part.shape[3]
    slow = row_dev // LANES
    blocks = d_buf.shape[0]
    first, last = me == 0, me == cols - 1
    end = first | last
    beside = jnp.where(first, 1, cols - 2)
    giver = ((me == 1) | (me == cols - 2)) if shared else None
    late = units - shared if shared else 0
    steps = max(shared + units, units + late)

    loads = [
        pltpu.make_async_copy(l_hbm, l_buf, load_sem.at[0]),
        pltpu.make_async_copy(turn_hbm.at[row], turn, load_sem.at[1]),
        pltpu.make_async_copy(twiddle_hbm, twiddle, load_sem.at[2]),
        pltpu.make_async_copy(w_hbm, w, load_sem.at[3]),
        pltpu.make_async_copy(s_hbm, cipher.at[:, :, pl.ds(0, units)], load_sem.at[4]),
    ]

    def d_load(b):
        return pltpu.make_async_copy(d_hbm.at[pl.ds(b * BLOCK, BLOCK)], d_buf.at[b], d_sem.at[b])

    loads[0].start()
    for b in range(blocks):
        d_load(b).start()
    for load in loads[1:]:
        load.start()

    barrier = pltpu.get_barrier_semaphore()
    greeted = 0
    peers = [{"col": lax.rem(me + step, cols)} for step in range(1, cols)]
    peers += [{"row": lax.rem(row + step, rows)} for step in range(1, rows)]
    peers += [{"limb": 1 - limb}]
    if shared:
        peers += [{"grp": 1 - grp}]
    for peer in peers:
        pl.semaphore_signal(barrier, inc=1, device_id=peer, device_id_type=MESH)
        greeted += 1

    acc[...] = jnp.zeros_like(acc)
    loads[0].wait()
    for c in range(0, l_buf.shape[0], BLOCK):
        lt[:, c : c + BLOCK] = l_buf[c : c + BLOCK, :].T
    pl.semaphore_wait(barrier, greeted)

    def remote(src, dst, send, recv, where):
        return pltpu.make_async_remote_copy(
            src_ref=src, dst_ref=dst, send_sem=send, recv_sem=recv, device_id=where, device_id_type=MESH
        )

    def hop(d, t, side, lanes=None):
        landing, lane = (from_left, 0) if side > 0 else (from_right, 1)
        src, dst = part.at[d, t], landing.at[d, t]
        if lanes is not None:
            src, dst = part.at[d, t, :, lanes], landing.at[d, t, :, lanes]
        return remote(src, dst, send_sem.at[lane, d, t], recv_sem.at[lane, d, t], {"col": me + side})

    def across(u, step):
        return remote(
            land.at[row, u], land.at[row, u], row_send.at[step - 1, u], row_recv.at[step - 1, u],
            {"row": lax.rem(row + step, rows)},
        )

    def give(u):
        there = jnp.where(me == 1, 0, cols - 1)
        return remote(
            s_hbm.at[grp, :, u], cipher.at[grp, :, units + u], s_send.at[u], s_recv.at[u], {"col": there}
        )

    def swap(u):
        here = cipher.at[grp, :, units + u]
        return remote(here, here, y_send.at[u], y_recv.at[u], {"grp": 1 - grp})

    if shared:
        @pl.when(giver)
        def _():
            @pl.loop(0, shared)
            def _(u):
                give(u).start()

    far = lambda side: range(cols - 1, 0, -1) if side > 0 else range(cols - 1)
    near = lambda side: (1 if side > 0 else cols - 2) if shared else None

    @pl.loop(0, blocks)
    def _(b):
        d_load(b).wait()
        lanes = pl.ds(pl.multiple_of(b * BLOCK, BLOCK), BLOCK)
        part[:, :, :, lanes] = lax.dot_general(
            lt[...], d_buf[b], (((1,), (1,)), ((), ())), preferred_element_type=jnp.float32
        ).reshape(cols, units, UNIT, BLOCK)
        for there, side in ((first, 1), (last, -1)):
            @pl.when(there)
            def _():
                for t in range(min(EARLY, units)):
                    for d in far(side):
                        if d != near(side):
                            hop(d, t, side, lanes).start()

    for there, side in ((first, 1), (last, -1)):
        @pl.when(there)
        def _():
            @pl.loop(min(EARLY, units), units)
            def _(t):
                for d in far(side):
                    if d != near(side):
                        hop(d, t, side).start()

            if shared:
                @pl.loop(shared, units)
                def _(t):
                    hop(near(side), t, side).start()

    for load in loads[1:]:
        load.wait()

    def consume(u):
        real, imag = [], []
        for s in range(slow):
            lanes = slice(s * LANES, (s + 1) * LANES)
            x = [land[m, u, :, lanes] for m in range(rows)]
            real.append(sum(x[m] * turn[m, 0, s : s + 1] for m in range(rows)))
            imag.append(sum(x[m] * turn[m, 1, s : s + 1] for m in range(rows)))
        both = jnp.concatenate([jnp.concatenate(real, 0), jnp.concatenate(imag, 0)], 1)
        high = both.astype(jnp.bfloat16)
        low = (both - high.astype(jnp.float32)).astype(jnp.bfloat16)
        mixed = jnp.dot(
            jnp.concatenate([high, low, high], 1), w[...], preferred_element_type=jnp.float32
        )
        spread = []
        for s in range(slow):
            r = mixed[s * UNIT : (s + 1) * UNIT, :LANES]
            i = mixed[s * UNIT : (s + 1) * UNIT, LANES:]
            c, n = twiddle[0, s : s + 1], twiddle[1, s : s + 1]
            spread.append((r * c - i * n, r * n + i * c) if s else (r, i))
        for v, (r, i) in enumerate(fft(spread)):
            lanes = slice(v * LANES, (v + 1) * LANES)
            for k in range(2):
                a, b = cipher[k, 0, u, :, lanes], cipher[k, 1, u, :, lanes]
                acc[k, 0, :, lanes] += r * a - i * b
                acc[k, 1, :, lanes] += r * b + i * a

    def place(i):
        at_end = jnp.where(i < shared, units + i, i - shared)
        inside = jnp.where(i < units - late, i, i - late)
        busy = jnp.where(
            end, (i >= 0) & (i < shared + units),
            (i >= 0) & ((i < units - late) | ((i >= units) & (i < units + late))),
        )
        return busy, jnp.where(end, at_end, inside)

    @pl.loop(0, steps + LAG)
    def _(i):
        @pl.when(jnp.logical_not(end) & (i < units))
        def _():
            for d in range(cols - 1, 1, -1):
                @pl.when(d > me)
                def _():
                    hop(d, i, 1).wait_recv()
                    part[d, i] += from_left[d, i]
                    hop(d, i, 1).start()
            for d in range(cols - 2):
                @pl.when(d < me)
                def _():
                    hop(d, i, -1).wait_recv()
                    part[d, i] += from_right[d, i]
                    hop(d, i, -1).start()

        busy, u = place(i)

        @pl.when(busy)
        def _():
            lent = u >= units
            d = jnp.where(lent, beside, me)
            t = jnp.where(lent, u - units, u)
            kept = t < shared

            @pl.when((me > 0) & jnp.logical_not(lent | ((me == 1) & kept)))
            def _():
                hop(me, t, 1).wait_recv()
                part[me, t] += from_left[me, t]

            @pl.when((me < cols - 1) & jnp.logical_not(lent | ((me == cols - 2) & kept)))
            def _():
                hop(me, t, -1).wait_recv()
                part[me, t] += from_right[me, t]

            moved = swap_bits(
                [part[d, t, :, b * LANES : (b + 1) * LANES] for b in range(slow)]
            )
            for s in range(slow):
                land[row, u, :, s * LANES : (s + 1) * LANES] = moved[s]
            for step in range(1, rows):
                across(u, step).start()
            if shared:
                @pl.when(lent)
                def _():
                    give(t).wait_recv()
                    swap(t).start()

        ready, v = place(i - LAG)

        @pl.when(ready)
        def _():
            for step in range(1, rows):
                across(v, step).wait_recv()
            if shared:
                @pl.when(v >= units)
                def _():
                    swap(v - units).wait_recv()
            consume(v)

    width = half_sum.shape[2]
    for k in range(2):
        for p in range(2):
            total = jnp.sum(acc[k, p], axis=0, keepdims=True)
            for q in range(4):
                r = (2 * k + p) * 2 + q % 2
                half_sum[q // 2, r : r + 1, :] = total[:, q * width : (q + 1) * width]
    other = {"limb": 1 - limb}
    trade = remote(half_sum.at[1 - limb], half_in, limb_send.at[0], limb_recv.at[0], other)
    trade.start()
    trade.wait_recv()
    z_in[me] = half_sum[limb] + half_in[...]

    def spread_to(step, peer):
        return remote(
            z_in.at[me], z_in.at[me], z_send.at[step], z_recv.at[step], {"col": peer}
        )

    for step in range(1, cols):
        spread_to(step, lax.rem(me + step, cols)).start()
    for step in range(1, cols):
        spread_to(step, lax.rem(me + step, cols)).wait_recv()
    total = z_in[0]
    for c in range(1, cols):
        total = total + z_in[c]
    whole_sum[limb] = total
    gather = remote(whole_sum.at[limb], whole_sum.at[limb], limb_send.at[1], limb_recv.at[1], other)
    gather.start()
    gather.wait_recv()
    for k in range(2):
        for p in range(2):
            for q in range(4):
                r = (2 * k + p) * 2 + q % 2
                out_ref[k, p : p + 1, q * width : (q + 1) * width] = whole_sum[q // 2, r : r + 1, :]

    for there, side in ((first, 1), (last, -1)):
        @pl.when(there)
        def _():
            @pl.loop(0, units)
            def _(t):
                for d in far(side):
                    if d != near(side):
                        hop(d, t, side).wait_send()

            if shared:
                @pl.loop(shared, units)
                def _(t):
                    hop(near(side), t, side).wait_send()

    @pl.when(jnp.logical_not(end))
    def _():
        @pl.loop(0, units)
        def _(t):
            for d in range(cols - 1, 1, -1):
                @pl.when(d > me)
                def _():
                    hop(d, t, 1).wait_send()
            for d in range(cols - 2):
                @pl.when(d < me)
                def _():
                    hop(d, t, -1).wait_send()

    if shared:
        @pl.when(giver)
        def _():
            @pl.loop(0, shared)
            def _(u):
                give(u).wait_send()

        @pl.when(end)
        def _():
            @pl.loop(0, shared)
            def _(u):
                swap(u).wait_send()
                for step in range(1, rows):
                    across(units + u, step).wait_send()

    @pl.loop(0, units)
    def _(u):
        for step in range(1, rows):
            across(u, step).wait_send()

    trade.wait_send()
    gather.wait_send()
    for step in range(1, cols):
        spread_to(step, lax.rem(me + step, cols)).wait_send()


def tables(rows, row_dev, half):
    slow = row_dev // LANES
    degree = rows * row_dev
    scale = 1.0 / (math.sqrt(degree) * math.sqrt(2 * half))
    lane = np.arange(LANES)
    at = LANES // slow * (lane % slow) + lane // slow
    n = np.arange(slow)[:, None] + slow * at[None, :]
    a, m = np.arange(rows)[:, None, None, None], np.arange(rows)[None, :, None, None]
    turn = -np.pi * ((n + m * row_dev) * (2 * a + 1) % (2 * degree)) / degree
    turn = np.exp(1j * turn) * scale
    turn = np.stack([turn.real, turn.imag], 2).astype(np.float32)
    twiddle = np.exp(-2j * np.pi * np.arange(slow)[:, None] * lane[None, :] / row_dev)
    twiddle = np.stack([twiddle.real, twiddle.imag], 0).astype(np.float32)
    w = np.exp(-2j * np.pi * (at[:, None] * lane[None, :] % LANES) / LANES)
    w = np.block([[w.real, w.imag], [-w.imag, w.real]]).astype(np.float32)
    high = w.astype(jnp.bfloat16)
    low = (w - high.astype(np.float32)).astype(jnp.bfloat16)
    return turn, twiddle, np.concatenate([high, high, low], 0)


def body(database, lwe_matrix, secret_ct):
    rows, cols = lax.axis_size("row"), lax.axis_size("col")
    grps = lax.axis_size("grp")
    row_dev, depth = database.shape
    half = lwe_matrix.shape[2]
    own = half // cols
    units = own // UNIT
    slow = row_dev // LANES
    shared = units * 5 // 8 if cols > 3 and grps == 2 else 0
    places = units + shared
    blocks = row_dev // BLOCK
    turn, twiddle, w = tables(rows, row_dev, half)
    dma = pltpu.SemaphoreType.DMA
    flow = pltpu.VMEM((cols, units, UNIT, row_dev), jnp.float32)
    lots = max(shared, 1)
    hbm = pl.BlockSpec(memory_space=pl.ANY)
    return pl.pallas_call(
        functools.partial(kernel, cols, rows, grps, shared),
        out_shape=jax.ShapeDtypeStruct((2, 2, row_dev), jnp.float32),
        in_specs=[hbm] * 6,
        out_specs=pl.BlockSpec(memory_space=pltpu.VMEM),
        scratch_shapes=[
            pltpu.VMEM((depth, half), lwe_matrix.dtype),
            pltpu.VMEM((half, depth), lwe_matrix.dtype),
            pltpu.VMEM((blocks, BLOCK, depth), database.dtype),
            flow,
            flow,
            flow,
            pltpu.VMEM((rows, places, UNIT, row_dev), jnp.float32),
            pltpu.VMEM((2, 2, places, UNIT, row_dev), jnp.float32),
            pltpu.VMEM(turn.shape[1:], jnp.float32),
            pltpu.VMEM(twiddle.shape, jnp.float32),
            pltpu.VMEM(w.shape, jnp.bfloat16),
            pltpu.VMEM((2, 2, UNIT, row_dev), jnp.float32),
            pltpu.VMEM((2, 8, row_dev // 4), jnp.float32),
            pltpu.VMEM((8, row_dev // 4), jnp.float32),
            pltpu.VMEM((cols, 8, row_dev // 4), jnp.float32),
            pltpu.VMEM((2, 8, row_dev // 4), jnp.float32),
            dma((5,)),
            dma((blocks,)),
            dma((2, cols, units)),
            dma((2, cols, units)),
            dma((max(rows - 1, 1), places)),
            dma((max(rows - 1, 1), places)),
            dma((lots,)),
            dma((lots,)),
            dma((lots,)),
            dma((lots,)),
            dma((2,)),
            dma((2,)),
            dma((cols,)),
            dma((cols,)),
        ],
        compiler_params=pltpu.CompilerParams(
            collective_id=0, has_side_effects=True, vmem_limit_bytes=56 << 20
        ),
    )(
        lwe_matrix[:, 0, :],
        database,
        secret_ct[:, :, 0].reshape(2, 2, units, UNIT, row_dev),
        jnp.asarray(turn),
        jnp.asarray(twiddle),
        jnp.asarray(w),
    )


def solution(mesh):
    placed = (P(("grp", "row"), "col"), P("col", "limb", None), P(None, None, "limb", "col", "row"))
    return jax.shard_map(
        body, mesh=mesh, in_specs=placed, out_specs=P("grp", None, "row"), check_vma=False
    )
```

```python
import functools
import math

import jax
import jax.numpy as jnp
import numpy as np
from jax import lax
from jax.experimental import pallas as pl
from jax.experimental.pallas import tpu as pltpu
from jax.sharding import PartitionSpec as P

MESH = pl.DeviceIdType.MESH
UNIT = 8
LANES = 128
BLOCK = 256
EARLY = 2
LAG = 3
HOLD = 3


def fft(values):
    count = len(values)
    if count == 1:
        return values
    even, odd = fft(values[0::2]), fft(values[1::2])
    low, high = [], []
    for k in range(count // 2):
        (er, ei), (r, i) = even[k], odd[k]
        if k == 0:
            tr, ti = r, i
        elif 4 * k == count:
            tr, ti = i, -r
        elif 8 * k == count:
            half = math.sqrt(0.5)
            tr, ti = (r + i) * half, (i - r) * half
        elif 8 * k == 3 * count:
            half = math.sqrt(0.5)
            tr, ti = (i - r) * half, -(r + i) * half
        else:
            c, s = math.cos(2 * math.pi * k / count), math.sin(2 * math.pi * k / count)
            tr, ti = r * c + i * s, i * c - r * s
        low.append((er + tr, ei + ti))
        high.append((er - tr, ei - ti))
    return low + high


def swap_bits(blocks):
    blocks = list(blocks)
    lane = lax.broadcasted_iota(jnp.int32, blocks[0].shape, 1)
    step = 1
    while step < len(blocks):
        clear = (lane & step) == 0
        for b in range(len(blocks)):
            if not b & step:
                x, y = blocks[b], blocks[b + step]
                blocks[b] = jnp.where(clear, x, pltpu.roll(y, step, 1))
                blocks[b + step] = jnp.where(clear, pltpu.roll(x, LANES - step, 1), y)
        step *= 2
    return blocks


def kernel(cols, rows, grps, shared, l_hbm, d_hbm, s_hbm, turn_hbm, twiddle_hbm, w_hbm, out_ref,
           l_buf, lt, d_buf, part, from_left, from_right, land, cipher, turn, twiddle, w, acc,
           half_sum, half_in, z_in, whole_sum,
           load_sem, d_sem, send_sem, recv_sem, row_send, row_recv, s_send, s_recv, y_send, y_recv,
           limb_send, limb_recv, z_send, z_recv):
    me, row = lax.axis_index("col"), lax.axis_index("row")
    grp, limb = lax.axis_index("grp"), lax.axis_index("limb")
    units, row_dev = part.shape[1], part.shape[3]
    slow = row_dev // LANES
    blocks = d_buf.shape[0]
    first, last = me == 0, me == cols - 1
    end = first | last
    beside = jnp.where(first, 1, cols - 2)
    giver = ((me == 1) | (me == cols - 2)) if shared else None
    late = units - shared if shared else 0
    right_hold = HOLD * jnp.maximum(me - 1, 0)
    left_hold = HOLD * jnp.maximum(cols - 2 - me, 0)
    own_hold = jnp.where(end, 0, jnp.maximum(right_hold, left_hold))
    steps = max(shared + units, units + late + HOLD * max(cols - 3, 0))

    loads = [
        pltpu.make_async_copy(l_hbm, l_buf, load_sem.at[0]),
        pltpu.make_async_copy(turn_hbm.at[row], turn, load_sem.at[1]),
        pltpu.make_async_copy(twiddle_hbm, twiddle, load_sem.at[2]),
        pltpu.make_async_copy(w_hbm, w, load_sem.at[3]),
        pltpu.make_async_copy(s_hbm, cipher.at[:, :, pl.ds(0, units)], load_sem.at[4]),
    ]

    def d_load(b):
        return pltpu.make_async_copy(d_hbm.at[pl.ds(b * BLOCK, BLOCK)], d_buf.at[b], d_sem.at[b])

    loads[0].start()
    for b in range(blocks):
        d_load(b).start()
    for load in loads[1:]:
        load.start()

    barrier = pltpu.get_barrier_semaphore()
    greeted = 0
    peers = [{"col": lax.rem(me + step, cols)} for step in range(1, cols)]
    peers += [{"row": lax.rem(row + step, rows)} for step in range(1, rows)]
    peers += [{"limb": 1 - limb}]
    if shared:
        peers += [{"grp": 1 - grp}]
    for peer in peers:
        pl.semaphore_signal(barrier, inc=1, device_id=peer, device_id_type=MESH)
        greeted += 1

    acc[...] = jnp.zeros_like(acc)
    loads[0].wait()
    for c in range(0, l_buf.shape[0], BLOCK):
        lt[:, c : c + BLOCK] = l_buf[c : c + BLOCK, :].T
    pl.semaphore_wait(barrier, greeted)

    def remote(src, dst, send, recv, where):
        return pltpu.make_async_remote_copy(
            src_ref=src, dst_ref=dst, send_sem=send, recv_sem=recv, device_id=where, device_id_type=MESH
        )

    def hop(d, t, side, lanes=None):
        landing, lane = (from_left, 0) if side > 0 else (from_right, 1)
        src, dst = part.at[d, t], landing.at[d, t]
        if lanes is not None:
            src, dst = part.at[d, t, :, lanes], landing.at[d, t, :, lanes]
        return remote(src, dst, send_sem.at[lane, d, t], recv_sem.at[lane, d, t], {"col": me + side})

    def across(u, step):
        return remote(
            land.at[row, u], land.at[row, u], row_send.at[step - 1, u], row_recv.at[step - 1, u],
            {"row": lax.rem(row + step, rows)},
        )

    def give(u):
        there = jnp.where(me == 1, 0, cols - 1)
        return remote(
            s_hbm.at[grp, :, u], cipher.at[grp, :, units + u], s_send.at[u], s_recv.at[u], {"col": there}
        )

    def swap(u):
        here = cipher.at[grp, :, units + u]
        return remote(here, here, y_send.at[u], y_recv.at[u], {"grp": 1 - grp})

    if shared:
        @pl.when(giver)
        def _():
            @pl.loop(0, shared)
            def _(u):
                give(u).start()

    far = lambda side: range(cols - 1, 0, -1) if side > 0 else range(cols - 1)
    near = lambda side: (1 if side > 0 else cols - 2) if shared else None

    @pl.loop(0, blocks)
    def _(b):
        d_load(b).wait()
        lanes = pl.ds(pl.multiple_of(b * BLOCK, BLOCK), BLOCK)
        part[:, :, :, lanes] = lax.dot_general(
            lt[...], d_buf[b], (((1,), (1,)), ((), ())), preferred_element_type=jnp.float32
        ).reshape(cols, units, UNIT, BLOCK)
        for there, side in ((first, 1), (last, -1)):
            @pl.when(there)
            def _():
                for t in range(min(EARLY, units)):
                    for d in far(side):
                        if d != near(side):
                            hop(d, t, side, lanes).start()

    for there, side in ((first, 1), (last, -1)):
        @pl.when(there)
        def _():
            @pl.loop(min(EARLY, units), units)
            def _(t):
                for d in far(side):
                    if d != near(side):
                        hop(d, t, side).start()

            if shared:
                @pl.loop(shared, units)
                def _(t):
                    hop(near(side), t, side).start()

    for load in loads[1:]:
        load.wait()

    def consume(u):
        real, imag = [], []
        for s in range(slow):
            lanes = slice(s * LANES, (s + 1) * LANES)
            x = [land[m, u, :, lanes] for m in range(rows)]
            real.append(sum(x[m] * turn[m, 0, s : s + 1] for m in range(rows)))
            imag.append(sum(x[m] * turn[m, 1, s : s + 1] for m in range(rows)))
        both = jnp.concatenate([jnp.concatenate(real, 0), jnp.concatenate(imag, 0)], 1)
        high = both.astype(jnp.bfloat16)
        low = (both - high.astype(jnp.float32)).astype(jnp.bfloat16)
        mixed = jnp.dot(
            jnp.concatenate([high, low, high], 1), w[...], preferred_element_type=jnp.float32
        )
        spread = []
        for s in range(slow):
            r = mixed[s * UNIT : (s + 1) * UNIT, :LANES]
            i = mixed[s * UNIT : (s + 1) * UNIT, LANES:]
            c, n = twiddle[0, s : s + 1], twiddle[1, s : s + 1]
            spread.append((r * c - i * n, r * n + i * c) if s else (r, i))
        for v, (r, i) in enumerate(fft(spread)):
            lanes = slice(v * LANES, (v + 1) * LANES)
            for k in range(2):
                a, b = cipher[k, 0, u, :, lanes], cipher[k, 1, u, :, lanes]
                acc[k, 0, :, lanes] += r * a - i * b
                acc[k, 1, :, lanes] += r * b + i * a

    def place(i):
        at_end = jnp.where(i < shared, units + i, i - shared)
        inside = jnp.where(i < units - late, i, i - late)
        busy = jnp.where(
            end, (i >= 0) & (i < shared + units),
            (i >= 0) & ((i < units - late) | ((i >= units) & (i < units + late))),
        )
        return busy, jnp.where(end, at_end, inside)

    @pl.loop(0, steps + LAG)
    def _(i):
        t_right, t_left = i - right_hold, i - left_hold

        @pl.when(jnp.logical_not(end) & (t_right >= 0) & (t_right < units))
        def _():
            for d in range(cols - 1, 1, -1):
                @pl.when(d > me)
                def _():
                    hop(d, t_right, 1).wait_recv()
                    part[d, t_right] += from_left[d, t_right]
                    hop(d, t_right, 1).start()

        @pl.when(jnp.logical_not(end) & (t_left >= 0) & (t_left < units))
        def _():
            for d in range(cols - 2):
                @pl.when(d < me)
                def _():
                    hop(d, t_left, -1).wait_recv()
                    part[d, t_left] += from_right[d, t_left]
                    hop(d, t_left, -1).start()

        busy, u = place(i - own_hold)

        @pl.when(busy)
        def _():
            lent = u >= units
            d = jnp.where(lent, beside, me)
            t = jnp.where(lent, u - units, u)
            kept = t < shared

            @pl.when((me > 0) & jnp.logical_not(lent | ((me == 1) & kept)))
            def _():
                hop(me, t, 1).wait_recv()
                part[me, t] += from_left[me, t]

            @pl.when((me < cols - 1) & jnp.logical_not(lent | ((me == cols - 2) & kept)))
            def _():
                hop(me, t, -1).wait_recv()
                part[me, t] += from_right[me, t]

            moved = swap_bits(
                [part[d, t, :, b * LANES : (b + 1) * LANES] for b in range(slow)]
            )
            for s in range(slow):
                land[row, u, :, s * LANES : (s + 1) * LANES] = moved[s]
            for step in range(1, rows):
                across(u, step).start()
            if shared:
                @pl.when(lent)
                def _():
                    give(t).wait_recv()
                    swap(t).start()

        ready, v = place(i - own_hold - LAG)

        @pl.when(ready)
        def _():
            for step in range(1, rows):
                across(v, step).wait_recv()
            if shared:
                @pl.when(v >= units)
                def _():
                    swap(v - units).wait_recv()
            consume(v)

    width = half_sum.shape[2]
    for k in range(2):
        for p in range(2):
            total = jnp.sum(acc[k, p], axis=0, keepdims=True)
            for q in range(4):
                r = (2 * k + p) * 2 + q % 2
                half_sum[q // 2, r : r + 1, :] = total[:, q * width : (q + 1) * width]
    other = {"limb": 1 - limb}
    trade = remote(half_sum.at[1 - limb], half_in, limb_send.at[0], limb_recv.at[0], other)
    trade.start()
    trade.wait_recv()
    z_in[me] = half_sum[limb] + half_in[...]

    def spread_to(step, peer):
        return remote(
            z_in.at[me], z_in.at[me], z_send.at[step], z_recv.at[step], {"col": peer}
        )

    for step in range(1, cols):
        spread_to(step, lax.rem(me + step, cols)).start()
    for step in range(1, cols):
        spread_to(step, lax.rem(me + step, cols)).wait_recv()
    total = z_in[0]
    for c in range(1, cols):
        total = total + z_in[c]
    whole_sum[limb] = total
    gather = remote(whole_sum.at[limb], whole_sum.at[limb], limb_send.at[1], limb_recv.at[1], other)
    gather.start()
    gather.wait_recv()
    for k in range(2):
        for p in range(2):
            for q in range(4):
                r = (2 * k + p) * 2 + q % 2
                out_ref[k, p : p + 1, q * width : (q + 1) * width] = whole_sum[q // 2, r : r + 1, :]

    for there, side in ((first, 1), (last, -1)):
        @pl.when(there)
        def _():
            @pl.loop(0, units)
            def _(t):
                for d in far(side):
                    if d != near(side):
                        hop(d, t, side).wait_send()

            if shared:
                @pl.loop(shared, units)
                def _(t):
                    hop(near(side), t, side).wait_send()

    @pl.when(jnp.logical_not(end))
    def _():
        @pl.loop(0, units)
        def _(t):
            for d in range(cols - 1, 1, -1):
                @pl.when(d > me)
                def _():
                    hop(d, t, 1).wait_send()
            for d in range(cols - 2):
                @pl.when(d < me)
                def _():
                    hop(d, t, -1).wait_send()

    if shared:
        @pl.when(giver)
        def _():
            @pl.loop(0, shared)
            def _(u):
                give(u).wait_send()

        @pl.when(end)
        def _():
            @pl.loop(0, shared)
            def _(u):
                swap(u).wait_send()
                for step in range(1, rows):
                    across(units + u, step).wait_send()

    @pl.loop(0, units)
    def _(u):
        for step in range(1, rows):
            across(u, step).wait_send()

    trade.wait_send()
    gather.wait_send()
    for step in range(1, cols):
        spread_to(step, lax.rem(me + step, cols)).wait_send()


def tables(rows, row_dev, half):
    slow = row_dev // LANES
    degree = rows * row_dev
    scale = 1.0 / (math.sqrt(degree) * math.sqrt(2 * half))
    lane = np.arange(LANES)
    at = LANES // slow * (lane % slow) + lane // slow
    n = np.arange(slow)[:, None] + slow * at[None, :]
    a, m = np.arange(rows)[:, None, None, None], np.arange(rows)[None, :, None, None]
    turn = -np.pi * ((n + m * row_dev) * (2 * a + 1) % (2 * degree)) / degree
    turn = np.exp(1j * turn) * scale
    turn = np.stack([turn.real, turn.imag], 2).astype(np.float32)
    twiddle = np.exp(-2j * np.pi * np.arange(slow)[:, None] * lane[None, :] / row_dev)
    twiddle = np.stack([twiddle.real, twiddle.imag], 0).astype(np.float32)
    w = np.exp(-2j * np.pi * (at[:, None] * lane[None, :] % LANES) / LANES)
    w = np.block([[w.real, w.imag], [-w.imag, w.real]]).astype(np.float32)
    high = w.astype(jnp.bfloat16)
    low = (w - high.astype(np.float32)).astype(jnp.bfloat16)
    return turn, twiddle, np.concatenate([high, high, low], 0)


def body(database, lwe_matrix, secret_ct):
    rows, cols = lax.axis_size("row"), lax.axis_size("col")
    grps = lax.axis_size("grp")
    row_dev, depth = database.shape
    half = lwe_matrix.shape[2]
    own = half // cols
    units = own // UNIT
    slow = row_dev // LANES
    shared = units * 5 // 8 if cols > 3 and grps == 2 else 0
    places = units + shared
    blocks = row_dev // BLOCK
    turn, twiddle, w = tables(rows, row_dev, half)
    dma = pltpu.SemaphoreType.DMA
    flow = pltpu.VMEM((cols, units, UNIT, row_dev), jnp.float32)
    lots = max(shared, 1)
    hbm = pl.BlockSpec(memory_space=pl.ANY)
    return pl.pallas_call(
        functools.partial(kernel, cols, rows, grps, shared),
        out_shape=jax.ShapeDtypeStruct((2, 2, row_dev), jnp.float32),
        in_specs=[hbm] * 6,
        out_specs=pl.BlockSpec(memory_space=pltpu.VMEM),
        scratch_shapes=[
            pltpu.VMEM((depth, half), lwe_matrix.dtype),
            pltpu.VMEM((half, depth), lwe_matrix.dtype),
            pltpu.VMEM((blocks, BLOCK, depth), database.dtype),
            flow,
            flow,
            flow,
            pltpu.VMEM((rows, places, UNIT, row_dev), jnp.float32),
            pltpu.VMEM((2, 2, places, UNIT, row_dev), jnp.float32),
            pltpu.VMEM(turn.shape[1:], jnp.float32),
            pltpu.VMEM(twiddle.shape, jnp.float32),
            pltpu.VMEM(w.shape, jnp.bfloat16),
            pltpu.VMEM((2, 2, UNIT, row_dev), jnp.float32),
            pltpu.VMEM((2, 8, row_dev // 4), jnp.float32),
            pltpu.VMEM((8, row_dev // 4), jnp.float32),
            pltpu.VMEM((cols, 8, row_dev // 4), jnp.float32),
            pltpu.VMEM((2, 8, row_dev // 4), jnp.float32),
            dma((5,)),
            dma((blocks,)),
            dma((2, cols, units)),
            dma((2, cols, units)),
            dma((max(rows - 1, 1), places)),
            dma((max(rows - 1, 1), places)),
            dma((lots,)),
            dma((lots,)),
            dma((lots,)),
            dma((lots,)),
            dma((2,)),
            dma((2,)),
            dma((cols,)),
            dma((cols,)),
        ],
        compiler_params=pltpu.CompilerParams(
            collective_id=0, has_side_effects=True, vmem_limit_bytes=56 << 20
        ),
    )(
        lwe_matrix[:, 0, :],
        database,
        secret_ct[:, :, 0].reshape(2, 2, units, UNIT, row_dev),
        jnp.asarray(turn),
        jnp.asarray(twiddle),
        jnp.asarray(w),
    )


def solution(mesh):
    placed = (P(("grp", "row"), "col"), P("col", "limb", None), P(None, None, "limb", "col", "row"))
    return jax.shard_map(
        body, mesh=mesh, in_specs=placed, out_specs=P("grp", None, "row"), check_vma=False
    )
```

```python
import functools
import math

import jax
import jax.numpy as jnp
import numpy as np
from jax import lax
from jax.experimental import pallas as pl
from jax.experimental.pallas import tpu as pltpu
from jax.sharding import PartitionSpec as P

MESH = pl.DeviceIdType.MESH
UNIT = 8
LANES = 128
BLOCK = 256
LEAD = 4
EARLY = 4
PIECES = 4
LAG = 3
HOLD = 3


def fft(values):
    count = len(values)
    if count == 1:
        return values
    even, odd = fft(values[0::2]), fft(values[1::2])
    low, high = [], []
    for k in range(count // 2):
        (er, ei), (r, i) = even[k], odd[k]
        if k == 0:
            tr, ti = r, i
        elif 4 * k == count:
            tr, ti = i, -r
        elif 8 * k == count:
            half = math.sqrt(0.5)
            tr, ti = (r + i) * half, (i - r) * half
        elif 8 * k == 3 * count:
            half = math.sqrt(0.5)
            tr, ti = (i - r) * half, -(r + i) * half
        else:
            c, s = math.cos(2 * math.pi * k / count), math.sin(2 * math.pi * k / count)
            tr, ti = r * c + i * s, i * c - r * s
        low.append((er + tr, ei + ti))
        high.append((er - tr, ei - ti))
    return low + high


def swap_bits(blocks):
    blocks = list(blocks)
    lane = lax.broadcasted_iota(jnp.int32, blocks[0].shape, 1)
    step = 1
    while step < len(blocks):
        clear = (lane & step) == 0
        for b in range(len(blocks)):
            if not b & step:
                x, y = blocks[b], blocks[b + step]
                blocks[b] = jnp.where(clear, x, pltpu.roll(y, step, 1))
                blocks[b + step] = jnp.where(clear, pltpu.roll(x, LANES - step, 1), y)
        step *= 2
    return blocks


def kernel(cols, rows, grps, shared, l_hbm, d_hbm, s_hbm, table_hbm, w_hbm, out_ref,
           l_buf, lt, d_buf, part, from_left, from_right, land, cipher, table, w, acc,
           half_sum, half_in, z_in, whole_sum,
           load_sem, d_sem, send_sem, recv_sem, row_send, row_recv, s_send, s_recv, y_send, y_recv,
           limb_send, limb_recv, z_send, z_recv, near_send, near_recv, bit_send, bit_recv):
    me, row = lax.axis_index("col"), lax.axis_index("row")
    grp, limb = lax.axis_index("grp"), lax.axis_index("limb")
    units, row_dev = part.shape[1], part.shape[3]
    slow = row_dev // LANES
    blocks = d_buf.shape[0]
    first, last = me == 0, me == cols - 1
    end = first | last
    beside = jnp.where(first, 1, cols - 2)
    giver = ((me == 1) | (me == cols - 2)) if shared else None
    late = units - shared if shared else 0
    right_hold = HOLD * jnp.maximum(me - 1, 0)
    left_hold = HOLD * jnp.maximum(cols - 2 - me, 0)
    lag = lambda d, side: LEAD * (cols - 1 - d) if side > 0 else LEAD * d
    by_left, by_right = right_hold + lag(me, 1), left_hold + lag(me, -1)
    if shared:
        by_left, by_right = jnp.where(me == 1, 0, by_left), jnp.where(me == cols - 2, 0, by_right)
    own_hold = jnp.where(end, 0, jnp.maximum(by_left, by_right))
    steps = max(shared + units, units + late + (HOLD + LEAD) * max(cols - 2, 0))

    loads = [
        pltpu.make_async_copy(l_hbm, l_buf, load_sem.at[0]),
        pltpu.make_async_copy(table_hbm.at[row], table, load_sem.at[1]),
        pltpu.make_async_copy(w_hbm, w, load_sem.at[2]),
        pltpu.make_async_copy(s_hbm, cipher.at[:, :, pl.ds(0, units)], load_sem.at[3]),
    ]

    def d_load(b):
        return pltpu.make_async_copy(d_hbm.at[pl.ds(b * BLOCK, BLOCK)], d_buf.at[b], d_sem.at[b])

    loads[0].start()
    for b in range(blocks):
        d_load(b).start()
    for load in loads[1:]:
        load.start()

    barrier = pltpu.get_barrier_semaphore()
    greeted = 0
    peers = [{"col": lax.rem(me + step, cols)} for step in range(1, cols)]
    peers += [{"row": lax.rem(row + step, rows)} for step in range(1, rows)]
    peers += [{"limb": 1 - limb}]
    if shared:
        peers += [{"grp": 1 - grp}]
    for peer in peers:
        pl.semaphore_signal(barrier, inc=1, device_id=peer, device_id_type=MESH)
        greeted += 1

    acc[...] = jnp.zeros_like(acc)
    loads[0].wait()
    for c in range(0, l_buf.shape[0], BLOCK):
        lt[:, c : c + BLOCK] = l_buf[c : c + BLOCK, :].T
    pl.semaphore_wait(barrier, greeted)

    def remote(src, dst, send, recv, where):
        return pltpu.make_async_remote_copy(
            src_ref=src, dst_ref=dst, send_sem=send, recv_sem=recv, device_id=where, device_id_type=MESH
        )

    def hop(d, t, side, lanes=None):
        landing, lane = (from_left, 0) if side > 0 else (from_right, 1)
        src, dst = part.at[d, t], landing.at[d, t]
        if lanes is not None:
            src, dst = part.at[d, t, :, lanes], landing.at[d, t, :, lanes]
        return remote(src, dst, send_sem.at[lane, d, t], recv_sem.at[lane, d, t], {"col": me + side})

    def across(u, step):
        return remote(
            land.at[row, u], land.at[row, u], row_send.at[step - 1, u], row_recv.at[step - 1, u],
            {"row": lax.rem(row + step, rows)},
        )

    span = row_dev // PIECES
    piece = lambda p: slice(p * span, (p + 1) * span)

    def near_hop(t, p, side):
        landing, d = (from_left, 1) if side > 0 else (from_right, cols - 2)
        return remote(
            part.at[d, t, :, piece(p)], landing.at[d, t, :, piece(p)],
            near_send.at[t - shared, p], near_recv.at[t - shared, p], {"col": me + side},
        )

    def bit_across(u, step, p):
        here = land.at[row, u, :, piece(p)]
        return remote(
            here, here, bit_send.at[step - 1, u - shared, p], bit_recv.at[step - 1, u - shared, p],
            {"row": lax.rem(row + step, rows)},
        )

    def give(u):
        there = jnp.where(me == 1, 0, cols - 1)
        return remote(
            s_hbm.at[grp, :, u], cipher.at[grp, :, units + u], s_send.at[u], s_recv.at[u], {"col": there}
        )

    def swap(u):
        here = cipher.at[grp, :, units + u]
        return remote(here, here, y_send.at[u], y_recv.at[u], {"grp": 1 - grp})

    if shared:
        @pl.when(giver)
        def _():
            @pl.loop(0, shared)
            def _(u):
                give(u).start()

    far = lambda side: range(cols - 1, 0, -1) if side > 0 else range(cols - 1)
    near = lambda side: (1 if side > 0 else cols - 2) if shared else None

    @pl.loop(0, blocks)
    def _(b):
        d_load(b).wait()
        lanes = pl.ds(pl.multiple_of(b * BLOCK, BLOCK), BLOCK)
        part[:, :, :, lanes] = lax.dot_general(
            lt[...], d_buf[b], (((1,), (1,)), ((), ())), preferred_element_type=jnp.float32
        ).reshape(cols, units, UNIT, BLOCK)
        for there, side in ((first, 1), (last, -1)):
            @pl.when(there)
            def _():
                for d in far(side):
                    if d != near(side):
                        for t in range(min(EARLY - lag(d, side), units)):
                            hop(d, t, side, lanes).start()

    for there, side in ((first, 1), (last, -1)):
        @pl.when(there)
        def _():
            @pl.loop(EARLY, units + LEAD * (cols - 1))
            def _(i):
                for d in far(side):
                    if d != near(side):
                        @pl.when((i >= lag(d, side)) & (i < units + lag(d, side)))
                        def _():
                            hop(d, i - lag(d, side), side).start()

            if shared:
                @pl.loop(shared, units)
                def _(t):
                    for p in range(PIECES):
                        near_hop(t, p, side).start()

    for load in loads[1:]:
        load.wait()

    def consume(u):
        real, imag = [], []
        for s in range(slow):
            lanes = slice(s * LANES, (s + 1) * LANES)
            x = [land[m, u, :, lanes] for m in range(rows)]
            real.append(sum(x[m] * table[2 * m + 2, s : s + 1] for m in range(rows)))
            imag.append(sum(x[m] * table[2 * m + 3, s : s + 1] for m in range(rows)))
        real, imag = swap_bits(real), swap_bits(imag)
        both = jnp.concatenate([jnp.concatenate(real, 0), jnp.concatenate(imag, 0)], 1)
        high = both.astype(jnp.bfloat16)
        low = (both - high.astype(jnp.float32)).astype(jnp.bfloat16)
        mixed = jnp.dot(
            jnp.concatenate([high, low, high], 1), w[...], preferred_element_type=jnp.float32
        )
        spread = []
        for s in range(slow):
            r = mixed[s * UNIT : (s + 1) * UNIT, :LANES]
            i = mixed[s * UNIT : (s + 1) * UNIT, LANES:]
            c, n = table[0, s : s + 1], table[1, s : s + 1]
            spread.append((r * c - i * n, r * n + i * c) if s else (r, i))
        for v, (r, i) in enumerate(fft(spread)):
            lanes = slice(v * LANES, (v + 1) * LANES)
            for k in range(2):
                a, b = cipher[k, 0, u, :, lanes], cipher[k, 1, u, :, lanes]
                acc[k, 0, :, lanes] += r * a - i * b
                acc[k, 1, :, lanes] += r * b + i * a

    def place(i):
        at_end = jnp.where(i < shared, units + i, i - shared)
        inside = jnp.where(i < units - late, i, i - late)
        busy = jnp.where(
            end, (i >= 0) & (i < shared + units),
            (i >= 0) & ((i < units - late) | ((i >= units) & (i < units + late))),
        )
        return busy, jnp.where(end, at_end, inside)

    def in_pieces(u):
        return jnp.logical_not(end) & (u >= shared) & (u < units) if shared else False

    @pl.loop(0, steps + LAG)
    def _(i):
        for d in range(cols - 1, 1, -1):
            t = i - right_hold - lag(d, 1)

            @pl.when(jnp.logical_not(end) & (d > me) & (t >= 0) & (t < units))
            def _():
                hop(d, t, 1).wait_recv()
                part[d, t] += from_left[d, t]
                hop(d, t, 1).start()

        for d in range(cols - 2):
            t = i - left_hold - lag(d, -1)

            @pl.when(jnp.logical_not(end) & (d < me) & (t >= 0) & (t < units))
            def _():
                hop(d, t, -1).wait_recv()
                part[d, t] += from_right[d, t]
                hop(d, t, -1).start()

        busy, u = place(i - own_hold)

        @pl.when(busy)
        def _():
            lent = u >= units
            d = jnp.where(lent, beside, me)
            t = jnp.where(lent, u - units, u)
            whole_left, whole_right = me > 0, me < cols - 1
            if shared:
                whole_left, whole_right = whole_left & (me != 1), whole_right & (me != cols - 2)

            @pl.when(whole_left & jnp.logical_not(lent))
            def _():
                hop(me, t, 1).wait_recv()
                part[me, t] += from_left[me, t]

            @pl.when(whole_right & jnp.logical_not(lent))
            def _():
                hop(me, t, -1).wait_recv()
                part[me, t] += from_right[me, t]

            @pl.when(jnp.logical_not(in_pieces(u)))
            def _():
                land[row, u] = part[d, t]
                for step in range(1, rows):
                    across(u, step).start()

            if shared:
                @pl.when(in_pieces(u))
                def _():
                    for p in range(PIECES):
                        for there, side, landing in ((me == 1, 1, from_left), (me == cols - 2, -1, from_right)):
                            @pl.when(there)
                            def _():
                                near_hop(u, p, side).wait_recv()
                                part[me, u, :, piece(p)] += landing[me, u, :, piece(p)]
                        land[row, u, :, piece(p)] = part[me, u, :, piece(p)]
                        for step in range(1, rows):
                            bit_across(u, step, p).start()

            if shared:
                @pl.when(lent)
                def _():
                    give(t).wait_recv()
                    swap(t).start()

        ready, v = place(i - own_hold - LAG)

        @pl.when(ready)
        def _():
            @pl.when(jnp.logical_not(in_pieces(v)))
            def _():
                for step in range(1, rows):
                    across(v, step).wait_recv()

            if shared:
                @pl.when(in_pieces(v))
                def _():
                    for step in range(1, rows):
                        for p in range(PIECES):
                            bit_across(v, step, p).wait_recv()

                @pl.when(v >= units)
                def _():
                    swap(v - units).wait_recv()
            consume(v)

    width = half_sum.shape[2]
    for k in range(2):
        for p in range(2):
            total = jnp.sum(acc[k, p], axis=0, keepdims=True)
            for q in range(4):
                r = (2 * k + p) * 2 + q % 2
                half_sum[q // 2, r : r + 1, :] = total[:, q * width : (q + 1) * width]
    other = {"limb": 1 - limb}
    trade = remote(half_sum.at[1 - limb], half_in, limb_send.at[0], limb_recv.at[0], other)
    trade.start()
    trade.wait_recv()
    z_in[me] = half_sum[limb] + half_in[...]

    def tell(src, dst):
        return remote(z_in.at[src], z_in.at[src], z_send.at[dst], z_recv.at[src], {"col": dst})

    tellers = range(1, cols - 1) if cols > 3 else range(cols)
    ahead = [(me + side * step) for step in range(cols - 1, 0, -1) for side in (1, -1)]
    if cols > 3:
        @pl.when(end)
        def _():
            tell(me, beside).start()

        for there, src in ((me == 1, 0), (me == cols - 2, cols - 1)):
            @pl.when(there)
            def _():
                tell(src, me).wait_recv()
                z_in[me] += z_in[src]

    for dst in ahead:
        @pl.when((jnp.logical_not(end) | (cols <= 3)) & (dst >= 0) & (dst < cols))
        def _():
            tell(me, dst).start()
    for src in tellers:
        @pl.when(me != src)
        def _():
            tell(src, me).wait_recv()
    total = z_in[tellers[0]]
    for c in tellers[1:]:
        total = total + z_in[c]
    whole_sum[limb] = total
    gather = remote(whole_sum.at[limb], whole_sum.at[limb], limb_send.at[1], limb_recv.at[1], other)
    gather.start()
    gather.wait_recv()
    for k in range(2):
        for p in range(2):
            for q in range(4):
                r = (2 * k + p) * 2 + q % 2
                out_ref[k, p : p + 1, q * width : (q + 1) * width] = whole_sum[q // 2, r : r + 1, :]

    for there, side in ((first, 1), (last, -1)):
        @pl.when(there)
        def _():
            @pl.loop(0, units)
            def _(t):
                for d in far(side):
                    if d != near(side):
                        hop(d, t, side).wait_send()

            if shared:
                @pl.loop(shared, units)
                def _(t):
                    for p in range(PIECES):
                        near_hop(t, p, side).wait_send()

    @pl.when(jnp.logical_not(end))
    def _():
        @pl.loop(0, units)
        def _(t):
            for d in range(cols - 1, 1, -1):
                @pl.when(d > me)
                def _():
                    hop(d, t, 1).wait_send()
            for d in range(cols - 2):
                @pl.when(d < me)
                def _():
                    hop(d, t, -1).wait_send()

    if shared:
        @pl.when(giver)
        def _():
            @pl.loop(0, shared)
            def _(u):
                give(u).wait_send()

        @pl.when(end)
        def _():
            @pl.loop(0, shared)
            def _(u):
                swap(u).wait_send()
                for step in range(1, rows):
                    across(units + u, step).wait_send()

    @pl.loop(0, units)
    def _(u):
        @pl.when(jnp.logical_not(in_pieces(u)))
        def _():
            for step in range(1, rows):
                across(u, step).wait_send()

        if shared:
            @pl.when(in_pieces(u))
            def _():
                for step in range(1, rows):
                    for p in range(PIECES):
                        bit_across(u, step, p).wait_send()

    trade.wait_send()
    gather.wait_send()
    if cols > 3:
        @pl.when(end)
        def _():
            tell(me, beside).wait_send()
    for dst in ahead:
        @pl.when((jnp.logical_not(end) | (cols <= 3)) & (dst >= 0) & (dst < cols))
        def _():
            tell(me, dst).wait_send()


def tables(rows, row_dev, half):
    slow = row_dev // LANES
    degree = rows * row_dev
    scale = 1.0 / (math.sqrt(degree) * math.sqrt(2 * half))
    lane = np.arange(LANES)
    at = LANES // slow * (lane % slow) + lane // slow
    n = LANES * np.arange(slow)[:, None] + lane[None, :]
    a, m = np.arange(rows)[:, None, None, None], np.arange(rows)[None, :, None, None]
    turn = -np.pi * ((n + m * row_dev) * (2 * a + 1) % (2 * degree)) / degree
    turn = np.exp(1j * turn) * scale
    turn = np.stack([turn.real, turn.imag], 2).reshape(rows, 2 * rows, slow, LANES)
    twiddle = np.exp(-2j * np.pi * np.arange(slow)[:, None] * lane[None, :] / row_dev)
    twiddle = np.stack([twiddle.real, twiddle.imag], 0)
    twiddle = np.broadcast_to(twiddle, (rows,) + twiddle.shape)
    table = np.concatenate([twiddle, turn], 1).astype(np.float32)
    w = np.exp(-2j * np.pi * (at[:, None] * lane[None, :] % LANES) / LANES)
    w = np.block([[w.real, w.imag], [-w.imag, w.real]]).astype(np.float32)
    high = w.astype(jnp.bfloat16)
    low = (w - high.astype(np.float32)).astype(jnp.bfloat16)
    return table, np.concatenate([high, high, low], 0)


def body(database, lwe_matrix, secret_ct):
    rows, cols = lax.axis_size("row"), lax.axis_size("col")
    grps = lax.axis_size("grp")
    row_dev, depth = database.shape
    half = lwe_matrix.shape[2]
    own = half // cols
    units = own // UNIT
    slow = row_dev // LANES
    shared = units * 5 // 8 if cols > 3 and grps == 2 else 0
    places = units + shared
    blocks = row_dev // BLOCK
    table, w = tables(rows, row_dev, half)
    dma = pltpu.SemaphoreType.DMA
    flow = pltpu.VMEM((cols, units, UNIT, row_dev), jnp.float32)
    lots = max(shared, 1)
    hbm = pl.BlockSpec(memory_space=pl.ANY)
    return pl.pallas_call(
        functools.partial(kernel, cols, rows, grps, shared),
        out_shape=jax.ShapeDtypeStruct((2, 2, row_dev), jnp.float32),
        in_specs=[hbm] * 5,
        out_specs=pl.BlockSpec(memory_space=pltpu.VMEM),
        scratch_shapes=[
            pltpu.VMEM((depth, half), lwe_matrix.dtype),
            pltpu.VMEM((half, depth), lwe_matrix.dtype),
            pltpu.VMEM((blocks, BLOCK, depth), database.dtype),
            flow,
            flow,
            flow,
            pltpu.VMEM((rows, places, UNIT, row_dev), jnp.float32),
            pltpu.VMEM((2, 2, places, UNIT, row_dev), jnp.float32),
            pltpu.VMEM(table.shape[1:], jnp.float32),
            pltpu.VMEM(w.shape, jnp.bfloat16),
            pltpu.VMEM((2, 2, UNIT, row_dev), jnp.float32),
            pltpu.VMEM((2, 8, row_dev // 4), jnp.float32),
            pltpu.VMEM((8, row_dev // 4), jnp.float32),
            pltpu.VMEM((cols, 8, row_dev // 4), jnp.float32),
            pltpu.VMEM((2, 8, row_dev // 4), jnp.float32),
            dma((4,)),
            dma((blocks,)),
            dma((2, cols, units)),
            dma((2, cols, units)),
            dma((max(rows - 1, 1), places)),
            dma((max(rows - 1, 1), places)),
            dma((lots,)),
            dma((lots,)),
            dma((lots,)),
            dma((lots,)),
            dma((2,)),
            dma((2,)),
            dma((cols,)),
            dma((cols,)),
            dma((units - shared, PIECES)),
            dma((units - shared, PIECES)),
            dma((max(rows - 1, 1), units - shared, PIECES)),
            dma((max(rows - 1, 1), units - shared, PIECES)),
        ],
        compiler_params=pltpu.CompilerParams(
            collective_id=0, has_side_effects=True, vmem_limit_bytes=55168 << 10
        ),
    )(
        lwe_matrix[:, 0, :],
        database,
        secret_ct[:, :, 0].reshape(2, 2, units, UNIT, row_dev),
        jnp.asarray(table),
        jnp.asarray(w),
    )


def solution(mesh):
    placed = (P(("grp", "row"), "col"), P("col", "limb", None), P(None, None, "limb", "col", "row"))
    return jax.shard_map(
        body, mesh=mesh, in_specs=placed, out_specs=P("grp", None, "row"), check_vma=False
    )
```

```python
import functools
import math

import jax
import jax.numpy as jnp
import numpy as np
from jax import lax
from jax.experimental import pallas as pl
from jax.experimental.pallas import tpu as pltpu
from jax.sharding import PartitionSpec as P

MESH = pl.DeviceIdType.MESH
UNIT = 8
LANES = 128
BLOCK = 256
LEAD = 4
AHEAD = 2
EARLY = 4
PIECES = 2
LAG = 3
HOLD = 3


def fft(values):
    count = len(values)
    if count == 1:
        return values
    even, odd = fft(values[0::2]), fft(values[1::2])
    low, high = [], []
    for k in range(count // 2):
        (er, ei), (r, i) = even[k], odd[k]
        if k == 0:
            tr, ti = r, i
        elif 4 * k == count:
            tr, ti = i, -r
        elif 8 * k == count:
            half = math.sqrt(0.5)
            tr, ti = (r + i) * half, (i - r) * half
        elif 8 * k == 3 * count:
            half = math.sqrt(0.5)
            tr, ti = (i - r) * half, -(r + i) * half
        else:
            c, s = math.cos(2 * math.pi * k / count), math.sin(2 * math.pi * k / count)
            tr, ti = r * c + i * s, i * c - r * s
        low.append((er + tr, ei + ti))
        high.append((er - tr, ei - ti))
    return low + high


def swap_bits(blocks):
    blocks = list(blocks)
    lane = lax.broadcasted_iota(jnp.int32, blocks[0].shape, 1)
    step = 1
    while step < len(blocks):
        clear = (lane & step) == 0
        for b in range(len(blocks)):
            if not b & step:
                x, y = blocks[b], blocks[b + step]
                blocks[b] = jnp.where(clear, x, pltpu.roll(y, step, 1))
                blocks[b + step] = jnp.where(clear, pltpu.roll(x, LANES - step, 1), y)
        step *= 2
    return blocks


def kernel(cols, rows, grps, shared, l_hbm, d_hbm, s_hbm, table_hbm, w_hbm, out_ref,
           l_buf, lt, d_buf, part, from_left, from_right, land, cipher, table, w, acc,
           half_sum, half_in, z_in, whole_sum,
           load_sem, l_sem, d_sem, send_sem, recv_sem, row_send, row_recv, s_send, s_recv, y_send, y_recv,
           limb_send, limb_recv, z_send, z_recv, near_send, near_recv, bit_send, bit_recv, pair_send, pair_recv):
    me, row = lax.axis_index("col"), lax.axis_index("row")
    grp, limb = lax.axis_index("grp"), lax.axis_index("limb")
    units, row_dev = part.shape[1], part.shape[3]
    slow = row_dev // LANES
    blocks = d_buf.shape[0]
    first, last = me == 0, me == cols - 1
    end = first | last
    beside = jnp.where(first, 1, cols - 2)
    giver = ((me == 1) | (me == cols - 2)) if shared else None
    late = units - shared if shared else 0
    right_hold = HOLD * jnp.maximum(me - 1, 0)
    left_hold = HOLD * jnp.maximum(cols - 2 - me, 0)
    lag = lambda d, side: LEAD * (cols - 1 - d) if side > 0 else LEAD * d
    by_left, by_right = right_hold + lag(me, 1), left_hold + lag(me, -1)
    if shared:
        by_left, by_right = jnp.where(me == 1, 0, by_left), jnp.where(me == cols - 2, 0, by_right)
    own_hold = jnp.where(end, 0, jnp.maximum(by_left, by_right))
    steps = max(shared + units, units + late + 1 + (HOLD + LEAD) * max(cols - 2, 0))
    final = units + shared

    loads = [
        pltpu.make_async_copy(table_hbm.at[row], table, load_sem.at[0]),
        pltpu.make_async_copy(w_hbm, w, load_sem.at[1]),
        pltpu.make_async_copy(s_hbm, cipher.at[:, :, pl.ds(0, units)], load_sem.at[2]),
    ]
    chunk = l_buf.shape[0] // l_sem.shape[0]
    l_loads = [
        pltpu.make_async_copy(
            l_hbm.at[pl.ds(c * chunk, chunk)], l_buf.at[pl.ds(c * chunk, chunk)], l_sem.at[c]
        )
        for c in range(l_sem.shape[0])
    ]

    def d_load(b):
        return pltpu.make_async_copy(d_hbm.at[pl.ds(b * BLOCK, BLOCK)], d_buf.at[b], d_sem.at[b])

    for load in l_loads:
        load.start()
    for b in range(min(AHEAD, blocks)):
        d_load(b).start()

    barrier = pltpu.get_barrier_semaphore()
    greeted = 0
    peers = [{"row": lax.rem(row + step, rows)} for step in range(1, rows)]
    peers += [{"limb": 1 - limb}]
    if shared:
        peers += [{"grp": 1 - grp}]
    for peer in peers:
        pl.semaphore_signal(barrier, inc=1, device_id=peer, device_id_type=MESH)
        greeted += 1
    for there, side in ((me > 0, -1), (me < cols - 1, 1)):
        @pl.when(there)
        def _():
            pl.semaphore_signal(barrier, inc=1, device_id={"col": me + side}, device_id_type=MESH)

    acc[...] = jnp.zeros_like(acc)
    for c, load in enumerate(l_loads):
        load.wait()
        lt[:, c * chunk : (c + 1) * chunk] = l_buf[c * chunk : (c + 1) * chunk, :].T

    @pl.when(end)
    def _():
        pl.semaphore_wait(barrier, greeted + min(cols - 1, 1))

    @pl.when(jnp.logical_not(end))
    def _():
        pl.semaphore_wait(barrier, greeted + 2)

    def remote(src, dst, send, recv, where):
        return pltpu.make_async_remote_copy(
            src_ref=src, dst_ref=dst, send_sem=send, recv_sem=recv, device_id=where, device_id_type=MESH
        )

    def hop(d, t, side, lanes=None):
        landing, lane = (from_left, 0) if side > 0 else (from_right, 1)
        src, dst = part.at[d, t], landing.at[d, t]
        if lanes is not None:
            src, dst = part.at[d, t, :, lanes], landing.at[d, t, :, lanes]
        return remote(src, dst, send_sem.at[lane, d, t], recv_sem.at[lane, d, t], {"col": me + side})

    def across(u, step):
        return remote(
            land.at[row, u], land.at[row, u], row_send.at[step - 1, u], row_recv.at[step - 1, u],
            {"row": lax.rem(row + step, rows)},
        )

    span = row_dev // PIECES
    piece = lambda p: slice(p * span, (p + 1) * span)

    def near_hop(t, p, side):
        landing, d = (from_left, 1) if side > 0 else (from_right, cols - 2)
        return remote(
            part.at[d, t, :, piece(p)], landing.at[d, t, :, piece(p)],
            near_send.at[t - shared, p], near_recv.at[t - shared, p], {"col": me + side},
        )

    def bit_across(u, step, p):
        here = land.at[row, u, :, piece(p)]
        return remote(
            here, here, bit_send.at[step - 1, u - shared, p], bit_recv.at[step - 1, u - shared, p],
            {"row": lax.rem(row + step, rows)},
        )

    def give(u):
        there = jnp.where(me == 1, 0, cols - 1)
        return remote(
            s_hbm.at[grp, :, u], cipher.at[grp, :, units + u], s_send.at[u], s_recv.at[u], {"col": there}
        )

    def swap(u):
        here = cipher.at[grp, :, units + u]
        return remote(here, here, y_send.at[u], y_recv.at[u], {"grp": 1 - grp})

    if shared:
        @pl.when(giver)
        def _():
            @pl.loop(0, shared)
            def _(u):
                give(u).start()

    far = lambda side: range(cols - 1, 0, -1) if side > 0 else range(cols - 1)
    near = lambda side: (1 if side > 0 else cols - 2) if shared else None

    @pl.loop(0, blocks)
    def _(b):
        d_load(b).wait()

        @pl.when(b + AHEAD < blocks)
        def _():
            d_load(b + AHEAD).start()

        lanes = pl.ds(pl.multiple_of(b * BLOCK, BLOCK), BLOCK)
        part[:, :, :, lanes] = lax.dot_general(
            lt[...], d_buf[b], (((1,), (1,)), ((), ())), preferred_element_type=jnp.float32
        ).reshape(cols, units, UNIT, BLOCK)
        for there, side in ((first, 1), (last, -1)):
            @pl.when(there)
            def _():
                for d in far(side):
                    if d != near(side):
                        for t in range(min(EARLY - lag(d, side), units)):
                            hop(d, t, side, lanes).start()

    for there, side in ((first, 1), (last, -1)):
        @pl.when(there)
        def _():
            @pl.loop(EARLY, units + LEAD * (cols - 1))
            def _(i):
                for d in far(side):
                    if d != near(side):
                        @pl.when((i >= lag(d, side)) & (i < units + lag(d, side)))
                        def _():
                            hop(d, i - lag(d, side), side).start()

            if shared:
                @pl.loop(shared, units - 1)
                def _(t):
                    for p in range(PIECES):
                        near_hop(t, p, side).start()

    for load in loads:
        load.start()
    for load in loads:
        load.wait()

    def pair(m):
        here = land.at[m, final]
        return remote(here, here, pair_send.at[m], pair_recv.at[m], {"col": beside})

    def consume(u, secret):
        real, imag = [], []
        for s in range(slow):
            lanes = slice(s * LANES, (s + 1) * LANES)
            x = [land[m, u, :, lanes] for m in range(rows)]
            real.append(sum(x[m] * table[2 * m + 2, s : s + 1] for m in range(rows)))
            imag.append(sum(x[m] * table[2 * m + 3, s : s + 1] for m in range(rows)))
        real, imag = swap_bits(real), swap_bits(imag)
        both = jnp.concatenate([jnp.concatenate(real, 0), jnp.concatenate(imag, 0)], 1)
        high = both.astype(jnp.bfloat16)
        low = (both - high.astype(jnp.float32)).astype(jnp.bfloat16)
        mixed = jnp.dot(
            jnp.concatenate([high, low, high], 1), w[...], preferred_element_type=jnp.float32
        )
        spread = []
        for s in range(slow):
            r = mixed[s * UNIT : (s + 1) * UNIT, :LANES]
            i = mixed[s * UNIT : (s + 1) * UNIT, LANES:]
            c, n = table[0, s : s + 1], table[1, s : s + 1]
            spread.append((r * c - i * n, r * n + i * c) if s else (r, i))
        for v, (r, i) in enumerate(fft(spread)):
            lanes = slice(v * LANES, (v + 1) * LANES)
            for k in range(2):
                a, b = cipher[k, 0, secret, :, lanes], cipher[k, 1, secret, :, lanes]
                acc[k, 0, :, lanes] += r * a - i * b
                acc[k, 1, :, lanes] += r * b + i * a

    extra = jnp.where(giver, 1, 0) if shared else 0

    def place(i):
        at_end = jnp.where(i < shared, units + i, i - shared)
        inside = jnp.where(i < units - late, i, jnp.where(i < units + late, i - late, final))
        busy = jnp.where(
            end, (i >= 0) & (i < shared + units),
            (i >= 0) & ((i < units - late) | ((i >= units) & (i < units + late + extra))),
        )
        return busy, jnp.where(end, at_end, inside)

    def in_pieces(u):
        return jnp.logical_not(end) & (u >= shared) & (u < units - 1) if shared else False

    @pl.loop(0, steps + LAG)
    def _(i):
        for d in range(cols - 1, 1, -1):
            t = i - right_hold - lag(d, 1)

            @pl.when(jnp.logical_not(end) & (d > me) & (t >= 0) & (t < units))
            def _():
                hop(d, t, 1).wait_recv()
                part[d, t] += from_left[d, t]
                hop(d, t, 1).start()

        for d in range(cols - 2):
            t = i - left_hold - lag(d, -1)

            @pl.when(jnp.logical_not(end) & (d < me) & (t >= 0) & (t < units))
            def _():
                hop(d, t, -1).wait_recv()
                part[d, t] += from_right[d, t]
                hop(d, t, -1).start()

        busy, u = place(i - own_hold)

        if shared:
            @pl.when(end & (i == 0))
            def _():
                land[row, final] = part[beside, units - 1]
                for step in range(1, rows):
                    across(final, step).start()

            @pl.when(end & (i == LAG))
            def _():
                for step in range(1, rows):
                    across(final, step).wait_recv()
                for m in range(rows):
                    pair(m).start()

        @pl.when(busy & (u != final))
        def _():
            lent = u >= units
            d = jnp.where(lent, beside, me)
            t = jnp.where(lent, u - units, u)
            whole_left, whole_right = me > 0, me < cols - 1
            if shared:
                whole_left, whole_right = whole_left & (me != 1), whole_right & (me != cols - 2)

            @pl.when(whole_left & jnp.logical_not(lent))
            def _():
                hop(me, t, 1).wait_recv()
                part[me, t] += from_left[me, t]

            @pl.when(whole_right & jnp.logical_not(lent))
            def _():
                hop(me, t, -1).wait_recv()
                part[me, t] += from_right[me, t]

            @pl.when(jnp.logical_not(in_pieces(u)))
            def _():
                land[row, u] = part[d, t]
                for step in range(1, rows):
                    across(u, step).start()

            if shared:
                @pl.when(in_pieces(u))
                def _():
                    for p in range(PIECES):
                        for there, side, landing in ((me == 1, 1, from_left), (me == cols - 2, -1, from_right)):
                            @pl.when(there)
                            def _():
                                near_hop(u, p, side).wait_recv()
                                part[me, u, :, piece(p)] += landing[me, u, :, piece(p)]
                        land[row, u, :, piece(p)] = part[me, u, :, piece(p)]
                        for step in range(1, rows):
                            bit_across(u, step, p).start()

            if shared:
                @pl.when(lent)
                def _():
                    give(t).wait_recv()
                    swap(t).start()

        ready, v = place(i - own_hold - LAG)

        @pl.when(ready)
        def _():
            @pl.when(jnp.logical_not(in_pieces(v)) & (v != final))
            def _():
                for step in range(1, rows):
                    across(v, step).wait_recv()

            if shared:
                @pl.when(in_pieces(v))
                def _():
                    for step in range(1, rows):
                        for p in range(PIECES):
                            bit_across(v, step, p).wait_recv()

                @pl.when((v >= units) & (v != final))
                def _():
                    swap(v - units).wait_recv()

                @pl.when(v == final)
                def _():
                    for m in range(rows):
                        pair(m).wait_recv()
            consume(v, jnp.where(v == final, units - 1, v) if shared else v)

    width = half_sum.shape[2]
    for k in range(2):
        for p in range(2):
            total = jnp.sum(acc[k, p], axis=0, keepdims=True)
            for q in range(4):
                r = (2 * k + p) * 2 + q % 2
                half_sum[q // 2, r : r + 1, :] = total[:, q * width : (q + 1) * width]
    other = {"limb": 1 - limb}
    trade = remote(half_sum.at[1 - limb], half_in, limb_send.at[0], limb_recv.at[0], other)
    trade.start()
    trade.wait_recv()
    z_in[me] = half_sum[limb] + half_in[...]

    def tell(src, dst):
        return remote(z_in.at[src], z_in.at[src], z_send.at[dst], z_recv.at[src], {"col": dst})

    tellers = range(1, cols - 1) if cols > 3 else range(cols)
    ahead = [(me + side * step) for step in range(cols - 1, 0, -1) for side in (1, -1)]
    if cols > 3:
        @pl.when(end)
        def _():
            tell(me, beside).start()

        for there, src in ((me == 1, 0), (me == cols - 2, cols - 1)):
            @pl.when(there)
            def _():
                tell(src, me).wait_recv()
                z_in[me] += z_in[src]

    for dst in ahead:
        @pl.when((jnp.logical_not(end) | (cols <= 3)) & (dst >= 0) & (dst < cols))
        def _():
            tell(me, dst).start()
    for src in tellers:
        @pl.when(me != src)
        def _():
            tell(src, me).wait_recv()
    total = z_in[tellers[0]]
    for c in tellers[1:]:
        total = total + z_in[c]
    whole_sum[limb] = total
    gather = remote(whole_sum.at[limb], whole_sum.at[limb], limb_send.at[1], limb_recv.at[1], other)
    gather.start()
    gather.wait_recv()
    for k in range(2):
        for p in range(2):
            for q in range(4):
                r = (2 * k + p) * 2 + q % 2
                out_ref[k, p : p + 1, q * width : (q + 1) * width] = whole_sum[q // 2, r : r + 1, :]

    for there, side in ((first, 1), (last, -1)):
        @pl.when(there)
        def _():
            @pl.loop(0, units)
            def _(t):
                for d in far(side):
                    if d != near(side):
                        hop(d, t, side).wait_send()

            if shared:
                @pl.loop(shared, units - 1)
                def _(t):
                    for p in range(PIECES):
                        near_hop(t, p, side).wait_send()
                for step in range(1, rows):
                    across(final, step).wait_send()
                for m in range(rows):
                    pair(m).wait_send()

    @pl.when(jnp.logical_not(end))
    def _():
        @pl.loop(0, units)
        def _(t):
            for d in range(cols - 1, 1, -1):
                @pl.when(d > me)
                def _():
                    hop(d, t, 1).wait_send()
            for d in range(cols - 2):
                @pl.when(d < me)
                def _():
                    hop(d, t, -1).wait_send()

    if shared:
        @pl.when(giver)
        def _():
            @pl.loop(0, shared)
            def _(u):
                give(u).wait_send()

        @pl.when(end)
        def _():
            @pl.loop(0, shared)
            def _(u):
                swap(u).wait_send()
                for step in range(1, rows):
                    across(units + u, step).wait_send()

    @pl.loop(0, units)
    def _(u):
        @pl.when(jnp.logical_not(in_pieces(u)))
        def _():
            for step in range(1, rows):
                across(u, step).wait_send()

        if shared:
            @pl.when(in_pieces(u))
            def _():
                for step in range(1, rows):
                    for p in range(PIECES):
                        bit_across(u, step, p).wait_send()

    trade.wait_send()
    gather.wait_send()
    if cols > 3:
        @pl.when(end)
        def _():
            tell(me, beside).wait_send()
    for dst in ahead:
        @pl.when((jnp.logical_not(end) | (cols <= 3)) & (dst >= 0) & (dst < cols))
        def _():
            tell(me, dst).wait_send()


def tables(rows, row_dev, half):
    slow = row_dev // LANES
    degree = rows * row_dev
    scale = 1.0 / (math.sqrt(degree) * math.sqrt(2 * half))
    lane = np.arange(LANES)
    at = LANES // slow * (lane % slow) + lane // slow
    n = LANES * np.arange(slow)[:, None] + lane[None, :]
    a, m = np.arange(rows)[:, None, None, None], np.arange(rows)[None, :, None, None]
    turn = -np.pi * ((n + m * row_dev) * (2 * a + 1) % (2 * degree)) / degree
    turn = np.exp(1j * turn) * scale
    turn = np.stack([turn.real, turn.imag], 2).reshape(rows, 2 * rows, slow, LANES)
    twiddle = np.exp(-2j * np.pi * np.arange(slow)[:, None] * lane[None, :] / row_dev)
    twiddle = np.stack([twiddle.real, twiddle.imag], 0)
    twiddle = np.broadcast_to(twiddle, (rows,) + twiddle.shape)
    table = np.concatenate([twiddle, turn], 1).astype(np.float32)
    w = np.exp(-2j * np.pi * (at[:, None] * lane[None, :] % LANES) / LANES)
    w = np.block([[w.real, w.imag], [-w.imag, w.real]]).astype(np.float32)
    high = w.astype(jnp.bfloat16)
    low = (w - high.astype(np.float32)).astype(jnp.bfloat16)
    return table, np.concatenate([high, high, low], 0)


def body(database, lwe_matrix, secret_ct):
    rows, cols = lax.axis_size("row"), lax.axis_size("col")
    grps = lax.axis_size("grp")
    row_dev, depth = database.shape
    half = lwe_matrix.shape[2]
    own = half // cols
    units = own // UNIT
    slow = row_dev // LANES
    shared = units * 5 // 8 if cols > 3 and grps == 2 else 0
    places = units + shared + 1
    blocks = row_dev // BLOCK
    table, w = tables(rows, row_dev, half)
    dma = pltpu.SemaphoreType.DMA
    flow = pltpu.VMEM((cols, units, UNIT, row_dev), jnp.float32)
    lots = max(shared, 1)
    hbm = pl.BlockSpec(memory_space=pl.ANY)
    return pl.pallas_call(
        functools.partial(kernel, cols, rows, grps, shared),
        out_shape=jax.ShapeDtypeStruct((2, 2, row_dev), jnp.float32),
        in_specs=[hbm] * 5,
        out_specs=pl.BlockSpec(memory_space=pltpu.VMEM),
        scratch_shapes=[
            pltpu.VMEM((depth, half), lwe_matrix.dtype),
            pltpu.VMEM((half, depth), lwe_matrix.dtype),
            pltpu.VMEM((blocks, BLOCK, depth), database.dtype),
            flow,
            flow,
            flow,
            pltpu.VMEM((rows, places, UNIT, row_dev), jnp.float32),
            pltpu.VMEM((2, 2, units + shared, UNIT, row_dev), jnp.float32),
            pltpu.VMEM(table.shape[1:], jnp.float32),
            pltpu.VMEM(w.shape, jnp.bfloat16),
            pltpu.VMEM((2, 2, UNIT, row_dev), jnp.float32),
            pltpu.VMEM((2, 8, row_dev // 4), jnp.float32),
            pltpu.VMEM((8, row_dev // 4), jnp.float32),
            pltpu.VMEM((cols, 8, row_dev // 4), jnp.float32),
            pltpu.VMEM((2, 8, row_dev // 4), jnp.float32),
            dma((3,)),
            dma((4,)),
            dma((blocks,)),
            dma((2, cols, units)),
            dma((2, cols, units)),
            dma((max(rows - 1, 1), places)),
            dma((max(rows - 1, 1), places)),
            dma((lots,)),
            dma((lots,)),
            dma((lots,)),
            dma((lots,)),
            dma((2,)),
            dma((2,)),
            dma((cols,)),
            dma((cols,)),
            dma((units - shared, PIECES)),
            dma((units - shared, PIECES)),
            dma((max(rows - 1, 1), units - shared, PIECES)),
            dma((max(rows - 1, 1), units - shared, PIECES)),
            dma((rows,)),
            dma((rows,)),
        ],
        compiler_params=pltpu.CompilerParams(
            collective_id=0, has_side_effects=True, vmem_limit_bytes=55168 << 10
        ),
    )(
        lwe_matrix[:, 0, :],
        database,
        secret_ct[:, :, 0].reshape(2, 2, units, UNIT, row_dev),
        jnp.asarray(table),
        jnp.asarray(w),
    )


def solution(mesh):
    placed = (P(("grp", "row"), "col"), P("col", "limb", None), P(None, None, "limb", "col", "row"))
    return jax.shard_map(
        body, mesh=mesh, in_specs=placed, out_specs=P("grp", None, "row"), check_vma=False
    )
```

```python
import functools
import math

import jax
import jax.numpy as jnp
import numpy as np
from jax import lax
from jax.experimental import pallas as pl
from jax.experimental.pallas import tpu as pltpu
from jax.sharding import PartitionSpec as P

MESH = pl.DeviceIdType.MESH
UNIT = 8
LANES = 128
BLOCK = 256
LEAD = 4
AHEAD = 2
EARLY = 4
PIECES = 2
LAG = 3
END_LAG = 5
HOLD = 3


def fft(values):
    count = len(values)
    if count == 1:
        return values
    even, odd = fft(values[0::2]), fft(values[1::2])
    low, high = [], []
    for k in range(count // 2):
        (er, ei), (r, i) = even[k], odd[k]
        if k == 0:
            tr, ti = r, i
        elif 4 * k == count:
            tr, ti = i, -r
        elif 8 * k == count:
            half = math.sqrt(0.5)
            tr, ti = (r + i) * half, (i - r) * half
        elif 8 * k == 3 * count:
            half = math.sqrt(0.5)
            tr, ti = (i - r) * half, -(r + i) * half
        else:
            c, s = math.cos(2 * math.pi * k / count), math.sin(2 * math.pi * k / count)
            tr, ti = r * c + i * s, i * c - r * s
        low.append((er + tr, ei + ti))
        high.append((er - tr, ei - ti))
    return low + high


def swap_bits(blocks):
    blocks = list(blocks)
    lane = lax.broadcasted_iota(jnp.int32, blocks[0].shape, 1)
    step = 1
    while step < len(blocks):
        clear = (lane & step) == 0
        for b in range(len(blocks)):
            if not b & step:
                x, y = blocks[b], blocks[b + step]
                blocks[b] = jnp.where(clear, x, pltpu.roll(y, step, 1))
                blocks[b + step] = jnp.where(clear, pltpu.roll(x, LANES - step, 1), y)
        step *= 2
    return blocks


def kernel(cols, rows, grps, shared, l_hbm, d_hbm, s_hbm, table_hbm, w_hbm, out_ref,
           l_buf, lt, d_buf, part, from_left, from_right, land, cipher, table, w, acc,
           half_sum, half_in, z_in, whole_sum,
           load_sem, l_sem, d_sem, send_sem, recv_sem, row_send, row_recv, s_send, s_recv, y_send, y_recv,
           limb_send, limb_recv, z_send, z_recv, near_send, near_recv, bit_recv, pair_send, pair_recv):
    me, row = lax.axis_index("col"), lax.axis_index("row")
    grp, limb = lax.axis_index("grp"), lax.axis_index("limb")
    units, row_dev = part.shape[1], part.shape[3]
    slow = row_dev // LANES
    blocks = d_buf.shape[0]
    first, last = me == 0, me == cols - 1
    end = first | last
    beside = jnp.where(first, 1, cols - 2)
    giver = ((me == 1) | (me == cols - 2)) if shared else None
    late = units - shared if shared else 0
    right_hold = HOLD * jnp.maximum(me - 1, 0)
    left_hold = HOLD * jnp.maximum(cols - 2 - me, 0)
    lag = lambda d, side: LEAD * (cols - 1 - d) if side > 0 else LEAD * d
    by_left, by_right = right_hold + lag(me, 1), left_hold + lag(me, -1)
    if shared:
        by_left, by_right = jnp.where(me == 1, 0, by_left), jnp.where(me == cols - 2, 0, by_right)
    own_hold = jnp.where(end, 0, jnp.maximum(by_left, by_right))
    final = units + shared

    loads = [
        pltpu.make_async_copy(table_hbm.at[row], table, load_sem.at[0]),
        pltpu.make_async_copy(w_hbm, w, load_sem.at[1]),
        pltpu.make_async_copy(s_hbm, cipher.at[:, :, pl.ds(0, units)], load_sem.at[2]),
    ]
    chunk = l_buf.shape[0] // l_sem.shape[0]
    l_loads = [
        pltpu.make_async_copy(
            l_hbm.at[pl.ds(c * chunk, chunk)], l_buf.at[pl.ds(c * chunk, chunk)], l_sem.at[c]
        )
        for c in range(l_sem.shape[0])
    ]

    def d_load(b):
        return pltpu.make_async_copy(d_hbm.at[pl.ds(b * BLOCK, BLOCK)], d_buf.at[b], d_sem.at[b])

    for load in l_loads:
        load.start()
    for b in range(min(AHEAD, blocks)):
        d_load(b).start()
    for load in loads[:-1]:
        load.start()

    barrier = pltpu.get_barrier_semaphore()
    greeted = 0
    peers = [{"row": lax.rem(row + step, rows)} for step in range(1, rows)]
    peers += [{"limb": 1 - limb}]
    if shared:
        peers += [{"grp": 1 - grp}]
    for peer in peers:
        pl.semaphore_signal(barrier, inc=1, device_id=peer, device_id_type=MESH)
        greeted += 1
    for there, side in ((me > 0, -1), (me < cols - 1, 1)):
        @pl.when(there)
        def _():
            pl.semaphore_signal(barrier, inc=1, device_id={"col": me + side}, device_id_type=MESH)

    acc[...] = jnp.zeros_like(acc)
    for c, load in enumerate(l_loads):
        load.wait()
        lt[:, c * chunk : (c + 1) * chunk] = l_buf[c * chunk : (c + 1) * chunk, :].T

    @pl.when(end)
    def _():
        pl.semaphore_wait(barrier, greeted + min(cols - 1, 1))

    @pl.when(jnp.logical_not(end))
    def _():
        pl.semaphore_wait(barrier, greeted + 2)

    def remote(src, dst, send, recv, where):
        return pltpu.make_async_remote_copy(
            src_ref=src, dst_ref=dst, send_sem=send, recv_sem=recv, device_id=where, device_id_type=MESH
        )

    def hop(d, t, side, lanes=None, to=None):
        landing, lane = (from_left, 0) if side > 0 else (from_right, 1)
        src, dst = part.at[d, t], landing.at[d, t]
        if lanes is not None:
            src, dst = part.at[d, t, :, lanes], landing.at[d, t, :, lanes]
        to = me + side if to is None else to
        slot = d if side > 0 else jnp.where(d == to, cols, d)
        return remote(src, dst, send_sem.at[lane, d], recv_sem.at[slot, t], {"col": me + side})

    def arrived(d, t, side):
        hop(d, t, side, to=me).wait_recv()

    def sent(src, sem):
        remote(src, src, sem, sem, {"col": me}).wait_send()

    def across(u, step):
        return remote(
            land.at[row, u], land.at[row, u], row_send.at[step - 1], row_recv.at[step - 1, u],
            {"row": lax.rem(row + step, rows)},
        )

    span = row_dev // PIECES
    piece = lambda p: slice(p * span, (p + 1) * span)

    def near_hop(t, p, side):
        landing, d = (from_left, 1) if side > 0 else (from_right, cols - 2)
        return remote(
            part.at[d, t, :, piece(p)], landing.at[d, t, :, piece(p)],
            near_send.at[0], near_recv.at[t - shared, p], {"col": me + side},
        )

    def bit_across(u, step, p):
        here = land.at[row, u, :, piece(p)]
        return remote(
            here, here, row_send.at[step - 1], bit_recv.at[step - 1, u - shared, p],
            {"row": lax.rem(row + step, rows)},
        )

    def give(u):
        there = jnp.where(me == 1, 0, cols - 1)
        return remote(
            s_hbm.at[grp, :, u], cipher.at[grp, :, units + u], s_send.at[0], s_recv.at[u], {"col": there}
        )

    def swap(u):
        here = cipher.at[grp, :, units + u]
        return remote(here, here, y_send.at[0], y_recv.at[u], {"grp": 1 - grp})

    if shared:
        @pl.when(giver)
        def _():
            @pl.loop(0, shared)
            def _(u):
                give(u).start()

    far = lambda side: range(cols - 1, 0, -1) if side > 0 else range(cols - 1)
    near = lambda side: (1 if side > 0 else cols - 2) if shared else None

    @pl.loop(0, blocks)
    def _(b):
        d_load(b).wait()

        @pl.when(b + AHEAD < blocks)
        def _():
            d_load(b + AHEAD).start()

        @pl.when(b == 1)
        def _():
            loads[-1].start()

        lanes = pl.ds(pl.multiple_of(b * BLOCK, BLOCK), BLOCK)
        part[:, :, :, lanes] = lax.dot_general(
            lt[...], d_buf[b], (((1,), (1,)), ((), ())), preferred_element_type=jnp.float32
        ).reshape(cols, units, UNIT, BLOCK)
        for there, side in ((first, 1), (last, -1)):
            @pl.when(there)
            def _():
                for d in far(side):
                    if d != near(side):
                        for t in range(min(EARLY - lag(d, side), units)):
                            hop(d, t, side, lanes).start()

    for there, side in ((first, 1), (last, -1)):
        @pl.when(there)
        def _():
            @pl.loop(EARLY, units + LEAD * (cols - 1))
            def _(i):
                for d in far(side):
                    if d != near(side):
                        @pl.when((i >= lag(d, side)) & (i < units + lag(d, side)))
                        def _():
                            hop(d, i - lag(d, side), side).start()

            if shared:
                @pl.loop(shared, units - 1)
                def _(t):
                    for p in range(PIECES):
                        near_hop(t, p, side).start()

    for load in loads:
        load.wait()

    def pair(m):
        here = land.at[m, final]
        return remote(here, here, pair_send.at[0], pair_recv.at[m], {"col": beside})

    def consume(u, secret):
        real, imag = [], []
        for s in range(slow):
            lanes = slice(s * LANES, (s + 1) * LANES)
            x = [land[m, u, :, lanes] for m in range(rows)]
            real.append(sum(x[m] * table[2 * m + 2, s : s + 1] for m in range(rows)))
            imag.append(sum(x[m] * table[2 * m + 3, s : s + 1] for m in range(rows)))
        real, imag = swap_bits(real), swap_bits(imag)
        both = jnp.concatenate([jnp.concatenate(real, 0), jnp.concatenate(imag, 0)], 1)
        high = both.astype(jnp.bfloat16)
        low = (both - high.astype(jnp.float32)).astype(jnp.bfloat16)
        mixed = jnp.dot(
            jnp.concatenate([high, low, high], 1), w[...], preferred_element_type=jnp.float32
        )
        spread = []
        for s in range(slow):
            r = mixed[s * UNIT : (s + 1) * UNIT, :LANES]
            i = mixed[s * UNIT : (s + 1) * UNIT, LANES:]
            c, n = table[0, s : s + 1], table[1, s : s + 1]
            spread.append((r * c - i * n, r * n + i * c) if s else (r, i))
        for v, (r, i) in enumerate(fft(spread)):
            lanes = slice(v * LANES, (v + 1) * LANES)
            for k in range(2):
                a, b = cipher[k, 0, secret, :, lanes], cipher[k, 1, secret, :, lanes]
                acc[k, 0, :, lanes] += r * a - i * b
                acc[k, 1, :, lanes] += r * b + i * a

    extra = jnp.where(giver, 1, 0) if shared else 0

    def place(i):
        at_end = jnp.where(i < shared, units + i, i - shared)
        after = jnp.where(i == units, units - 1, jnp.where(i < units + late, i - late - 1, final))
        inside = jnp.where(i < units - late, i, after)
        busy = jnp.where(
            end, (i >= 0) & (i < shared + units),
            (i >= 0) & ((i < units - late) | ((i >= units) & (i < units + late + extra))),
        )
        return busy, jnp.where(end, at_end, inside)

    def in_pieces(u):
        return jnp.logical_not(end) & (u >= shared) & (u < units - 1) if shared else False

    wait = jnp.where(end, END_LAG, LAG)
    rest = jnp.maximum(
        right_hold + LEAD * jnp.maximum(cols - 2 - me, 0), left_hold + LEAD * jnp.maximum(me - 1, 0)
    )
    rest = jnp.maximum(rest, own_hold + late + extra + LAG)
    steps = units + jnp.where(end, shared + END_LAG, rest)

    def forward(d, side, i):
        beyond, hold, landing = (
            (d > me, right_hold, from_left) if side > 0 else (d < me, left_hold, from_right)
        )
        t = i - hold - lag(d, side)

        @pl.when(jnp.logical_not(end) & beyond & (t >= 0) & (t < units))
        def _():
            arrived(d, t, side)
            part[d, t] += landing[d, t]
            hop(d, t, side).start()

    def step_of(i, carry):
        for d in range(cols - 1, 1, -1):
            forward(d, 1, i)
        for d in range(cols - 2):
            forward(d, -1, i)
        busy, u = place(i - own_hold)

        if shared:
            @pl.when(end & (i == 0))
            def _():
                land[row, final] = part[beside, units - 1]
                for step in range(1, rows):
                    across(final, step).start()

            @pl.when(end & (i == LAG))
            def _():
                for step in range(1, rows):
                    across(final, step).wait_recv()
                for m in range(rows):
                    pair(m).start()

        @pl.when(busy & (u != final))
        def _():
            lent = u >= units
            d = jnp.where(lent, beside, me)
            t = jnp.where(lent, u - units, u)
            whole_left, whole_right = me > 0, me < cols - 1
            if shared:
                whole_left, whole_right = whole_left & (me != 1), whole_right & (me != cols - 2)

            @pl.when(whole_left & jnp.logical_not(lent))
            def _():
                arrived(me, t, 1)
                part[me, t] += from_left[me, t]

            @pl.when(whole_right & jnp.logical_not(lent))
            def _():
                arrived(me, t, -1)
                part[me, t] += from_right[me, t]

            @pl.when(jnp.logical_not(in_pieces(u)))
            def _():
                land[row, u] = part[d, t]
                for step in range(1, rows):
                    across(u, step).start()

            if shared:
                @pl.when(in_pieces(u))
                def _():
                    for p in range(PIECES):
                        for there, side, landing in ((me == 1, 1, from_left), (me == cols - 2, -1, from_right)):
                            @pl.when(there)
                            def _():
                                near_hop(u, p, side).wait_recv()
                                part[me, u, :, piece(p)] += landing[me, u, :, piece(p)]
                        land[row, u, :, piece(p)] = part[me, u, :, piece(p)]
                        for step in range(1, rows):
                            bit_across(u, step, p).start()

            if shared:
                @pl.when(lent)
                def _():
                    give(t).wait_recv()
                    swap(t).start()

        ready, v = place(i - own_hold - wait)

        @pl.when(ready)
        def _():
            @pl.when(jnp.logical_not(in_pieces(v)) & (v != final))
            def _():
                for step in range(1, rows):
                    across(v, step).wait_recv()

            if shared:
                @pl.when(in_pieces(v))
                def _():
                    for step in range(1, rows):
                        for p in range(PIECES):
                            bit_across(v, step, p).wait_recv()

                @pl.when((v >= units) & (v != final))
                def _():
                    swap(v - units).wait_recv()

                @pl.when(v == final)
                def _():
                    for m in range(rows):
                        pair(m).wait_recv()
            consume(v, jnp.where(v == final, units - 1, v) if shared else v)

        return carry

    lax.fori_loop(0, steps, step_of, 0)

    width = half_sum.shape[2]
    for k in range(2):
        for p in range(2):
            total = jnp.sum(acc[k, p], axis=0, keepdims=True)
            for q in range(4):
                r = (2 * k + p) * 2 + q % 2
                half_sum[q // 2, r : r + 1, :] = total[:, q * width : (q + 1) * width]
    other = {"limb": 1 - limb}
    trade = remote(half_sum.at[1 - limb], half_in, limb_send.at[0], limb_recv.at[0], other)
    trade.start()
    trade.wait_recv()
    z_in[me] = half_sum[limb] + half_in[...]

    def tell(src, dst):
        return remote(z_in.at[src], z_in.at[src], z_send.at[0], z_recv.at[src], {"col": dst})

    tellers = range(1, cols - 1) if cols > 3 else range(cols)
    ahead = [(me + side * step) for step in range(cols - 1, 0, -1) for side in (1, -1)]
    if cols > 3:
        @pl.when(end)
        def _():
            tell(me, beside).start()

        for there, src in ((me == 1, 0), (me == cols - 2, cols - 1)):
            @pl.when(there)
            def _():
                tell(src, me).wait_recv()
                z_in[me] += z_in[src]

    for dst in ahead:
        @pl.when((jnp.logical_not(end) | (cols <= 3)) & (dst >= 0) & (dst < cols))
        def _():
            tell(me, dst).start()
    for there, side in ((first, 1), (last, -1)):
        @pl.when(there)
        def _():
            lane = 0 if side > 0 else 1
            for d in far(side):
                if d != near(side):
                    sent(part.at[d], send_sem.at[lane, d])
            for step in range(1, rows):
                sent(land.at[row, pl.ds(0, final + 1 if shared else units)], row_send.at[step - 1])
            if shared:
                if units - 1 > shared:
                    sent(part.at[near(side), pl.ds(shared, units - 1 - shared)], near_send.at[0])
                sent(land.at[:, final], pair_send.at[0])
                sent(cipher.at[grp, :, pl.ds(units, shared)], y_send.at[0])

    @pl.when(jnp.logical_not(end))
    def _():
        for d in range(cols - 1, 1, -1):
            @pl.when(d > me)
            def _():
                sent(part.at[d], send_sem.at[0, d])
        for d in range(cols - 2):
            @pl.when(d < me)
            def _():
                sent(part.at[d], send_sem.at[1, d])
        for step in range(1, rows):
            sent(land.at[row, pl.ds(0, units)], row_send.at[step - 1])

    if shared:
        @pl.when(giver)
        def _():
            sent(cipher.at[grp, :, pl.ds(units, shared)], s_send.at[0])

    for src in tellers:
        @pl.when(me != src)
        def _():
            tell(src, me).wait_recv()
    total = z_in[tellers[0]]
    for c in tellers[1:]:
        total = total + z_in[c]
    whole_sum[limb] = total
    gather = remote(whole_sum.at[limb], whole_sum.at[limb], limb_send.at[1], limb_recv.at[1], other)
    gather.start()
    gather.wait_recv()
    for k in range(2):
        for p in range(2):
            for q in range(4):
                r = (2 * k + p) * 2 + q % 2
                out_ref[k, p : p + 1, q * width : (q + 1) * width] = whole_sum[q // 2, r : r + 1, :]

    trade.wait_send()
    gather.wait_send()
    if cols > 3:
        @pl.when(end)
        def _():
            sent(z_in.at[0], z_send.at[0])

        @pl.when(jnp.logical_not(end))
        def _():
            sent(z_in.at[pl.ds(0, cols - 1)], z_send.at[0])
    elif cols > 1:
        sent(z_in.at[pl.ds(0, cols - 1)], z_send.at[0])


def tables(rows, row_dev, half):
    slow = row_dev // LANES
    degree = rows * row_dev
    scale = 1.0 / (math.sqrt(degree) * math.sqrt(2 * half))
    lane = np.arange(LANES)
    at = LANES // slow * (lane % slow) + lane // slow
    n = LANES * np.arange(slow)[:, None] + lane[None, :]
    a, m = np.arange(rows)[:, None, None, None], np.arange(rows)[None, :, None, None]
    turn = -np.pi * ((n + m * row_dev) * (2 * a + 1) % (2 * degree)) / degree
    turn = np.exp(1j * turn) * scale
    turn = np.stack([turn.real, turn.imag], 2).reshape(rows, 2 * rows, slow, LANES)
    twiddle = np.exp(-2j * np.pi * np.arange(slow)[:, None] * lane[None, :] / row_dev)
    twiddle = np.stack([twiddle.real, twiddle.imag], 0)
    twiddle = np.broadcast_to(twiddle, (rows,) + twiddle.shape)
    table = np.concatenate([twiddle, turn], 1).astype(np.float32)
    w = np.exp(-2j * np.pi * (at[:, None] * lane[None, :] % LANES) / LANES)
    w = np.block([[w.real, w.imag], [-w.imag, w.real]]).astype(np.float32)
    high = w.astype(jnp.bfloat16)
    low = (w - high.astype(np.float32)).astype(jnp.bfloat16)
    return table, np.concatenate([high, high, low], 0)


def body(database, lwe_matrix, secret_ct):
    rows, cols = lax.axis_size("row"), lax.axis_size("col")
    grps = lax.axis_size("grp")
    row_dev, depth = database.shape
    half = lwe_matrix.shape[2]
    own = half // cols
    units = own // UNIT
    slow = row_dev // LANES
    shared = units * 11 // 16 if cols > 3 and grps == 2 else 0
    places = units + shared + 1
    blocks = row_dev // BLOCK
    table, w = tables(rows, row_dev, half)
    dma = pltpu.SemaphoreType.DMA
    flow = pltpu.VMEM((cols, units, UNIT, row_dev), jnp.float32)
    lots = max(shared, 1)
    hbm = pl.BlockSpec(memory_space=pl.ANY)
    return pl.pallas_call(
        functools.partial(kernel, cols, rows, grps, shared),
        out_shape=jax.ShapeDtypeStruct((2, 2, row_dev), jnp.float32),
        in_specs=[hbm] * 5,
        out_specs=pl.BlockSpec(memory_space=pltpu.VMEM),
        scratch_shapes=[
            pltpu.VMEM((depth, half), lwe_matrix.dtype),
            pltpu.VMEM((half, depth), lwe_matrix.dtype),
            pltpu.VMEM((blocks, BLOCK, depth), database.dtype),
            flow,
            flow,
            flow,
            pltpu.VMEM((rows, places, UNIT, row_dev), jnp.float32),
            pltpu.VMEM((2, 2, units + shared, UNIT, row_dev), jnp.float32),
            pltpu.VMEM(table.shape[1:], jnp.float32),
            pltpu.VMEM(w.shape, jnp.bfloat16),
            pltpu.VMEM((2, 2, UNIT, row_dev), jnp.float32),
            pltpu.VMEM((2, 8, row_dev // 4), jnp.float32),
            pltpu.VMEM((8, row_dev // 4), jnp.float32),
            pltpu.VMEM((cols, 8, row_dev // 4), jnp.float32),
            pltpu.VMEM((2, 8, row_dev // 4), jnp.float32),
            dma((3,)),
            dma((4,)),
            dma((blocks,)),
            dma((2, cols)),
            dma((cols + 1, units)),
            dma((max(rows - 1, 1),)),
            dma((max(rows - 1, 1), places)),
            dma((1,)),
            dma((lots,)),
            dma((1,)),
            dma((lots,)),
            dma((2,)),
            dma((2,)),
            dma((1,)),
            dma((cols,)),
            dma((1,)),
            dma((max(units - 1 - shared, 1), PIECES)),
            dma((max(rows - 1, 1), max(units - 1 - shared, 1), PIECES)),
            dma((1,)),
            dma((rows,)),
        ],
        compiler_params=pltpu.CompilerParams(
            collective_id=0, has_side_effects=True, vmem_limit_bytes=55168 << 10
        ),
    )(
        lwe_matrix[:, 0, :],
        database,
        secret_ct[:, :, 0].reshape(2, 2, units, UNIT, row_dev),
        jnp.asarray(table),
        jnp.asarray(w),
    )


def solution(mesh):
    placed = (P(("grp", "row"), "col"), P("col", "limb", None), P(None, None, "limb", "col", "row"))
    return jax.shard_map(
        body, mesh=mesh, in_specs=placed, out_specs=P("grp", None, "row"), check_vma=False
    )
```

```python
import functools
import math

import jax
import jax.numpy as jnp
import numpy as np
from jax import lax
from jax.experimental import pallas as pl
from jax.experimental.pallas import tpu as pltpu
from jax.sharding import PartitionSpec as P

MESH = pl.DeviceIdType.MESH
UNIT = 8
LANES = 128
BLOCK = 256
LEAD = 4
AHEAD = 2
EARLY = 4
DELAY = 3
PIECES = 2
LAG = 3
END_LAG = 5
HOLD = 3


def fft(values):
    count = len(values)
    if count == 1:
        return values
    even, odd = fft(values[0::2]), fft(values[1::2])
    low, high = [], []
    for k in range(count // 2):
        (er, ei), (r, i) = even[k], odd[k]
        if k == 0:
            tr, ti = r, i
        elif 4 * k == count:
            tr, ti = i, -r
        elif 8 * k == count:
            half = math.sqrt(0.5)
            tr, ti = (r + i) * half, (i - r) * half
        elif 8 * k == 3 * count:
            half = math.sqrt(0.5)
            tr, ti = (i - r) * half, -(r + i) * half
        else:
            c, s = math.cos(2 * math.pi * k / count), math.sin(2 * math.pi * k / count)
            tr, ti = r * c + i * s, i * c - r * s
        low.append((er + tr, ei + ti))
        high.append((er - tr, ei - ti))
    return low + high


def swap_bits(blocks):
    blocks = list(blocks)
    lane = lax.broadcasted_iota(jnp.int32, blocks[0].shape, 1)
    step = 1
    while step < len(blocks):
        clear = (lane & step) == 0
        for b in range(len(blocks)):
            if not b & step:
                x, y = blocks[b], blocks[b + step]
                blocks[b] = jnp.where(clear, x, pltpu.roll(y, step, 1))
                blocks[b + step] = jnp.where(clear, pltpu.roll(x, LANES - step, 1), y)
        step *= 2
    return blocks


def kernel(cols, rows, grps, shared, l_hbm, d_hbm, s_hbm, table_hbm, w_hbm, out_ref,
           l_buf, lt, d_buf, part, from_left, from_right, land, cipher, table, w, acc,
           half_sum, half_in, z_in, whole_sum,
           load_sem, l_sem, d_sem, send_sem, recv_sem, row_send, row_recv, s_send, s_recv, y_send, y_recv,
           limb_send, limb_recv, z_send, z_recv, near_send, near_recv, bit_recv, pair_send, pair_recv, early_recv):
    me, row = lax.axis_index("col"), lax.axis_index("row")
    grp, limb = lax.axis_index("grp"), lax.axis_index("limb")
    units, row_dev = part.shape[1], part.shape[3]
    slow = row_dev // LANES
    blocks = d_buf.shape[0]
    first, last = me == 0, me == cols - 1
    end = first | last
    beside = jnp.where(first, 1, cols - 2)
    giver = ((me == 1) | (me == cols - 2)) if shared else None
    late = units - shared if shared else 0
    right_hold = HOLD * jnp.maximum(me - 1, 0)
    left_hold = HOLD * jnp.maximum(cols - 2 - me, 0)
    lag = lambda d, side: LEAD * (cols - 1 - d) if side > 0 else LEAD * d
    by_left, by_right = right_hold + lag(me, 1), left_hold + lag(me, -1)
    if shared:
        by_left, by_right = jnp.where(me == 1, 0, by_left), jnp.where(me == cols - 2, 0, by_right)
    own_hold = jnp.where(end, 0, jnp.maximum(by_left, by_right))
    final = units + shared

    loads = [
        pltpu.make_async_copy(table_hbm.at[row], table, load_sem.at[0]),
        pltpu.make_async_copy(w_hbm, w, load_sem.at[1]),
        pltpu.make_async_copy(s_hbm, cipher.at[:, :, pl.ds(0, units)], load_sem.at[2]),
    ]
    chunk = l_buf.shape[0] // l_sem.shape[0]
    l_loads = [
        pltpu.make_async_copy(
            l_hbm.at[pl.ds(c * chunk, chunk)], l_buf.at[pl.ds(c * chunk, chunk)], l_sem.at[c]
        )
        for c in range(l_sem.shape[0])
    ]

    def d_load(b):
        return pltpu.make_async_copy(d_hbm.at[pl.ds(b * BLOCK, BLOCK)], d_buf.at[b], d_sem.at[b])

    for load in l_loads:
        load.start()
    for b in range(min(AHEAD, blocks)):
        d_load(b).start()
    for load in loads[:-1]:
        load.start()

    barrier = pltpu.get_barrier_semaphore()
    greeted = 0
    peers = [{"row": lax.rem(row + step, rows)} for step in range(1, rows)]
    peers += [{"limb": 1 - limb}]
    if shared:
        peers += [{"grp": 1 - grp}]
    for peer in peers:
        pl.semaphore_signal(barrier, inc=1, device_id=peer, device_id_type=MESH)
        greeted += 1
    for there, side in ((me > 0, -1), (me < cols - 1, 1)):
        @pl.when(there)
        def _():
            pl.semaphore_signal(barrier, inc=1, device_id={"col": me + side}, device_id_type=MESH)

    acc[...] = jnp.zeros_like(acc)
    for c, load in enumerate(l_loads):
        load.wait()
        lt[:, c * chunk : (c + 1) * chunk] = l_buf[c * chunk : (c + 1) * chunk, :].T

    @pl.when(end)
    def _():
        pl.semaphore_wait(barrier, greeted + min(cols - 1, 1))

    @pl.when(jnp.logical_not(end))
    def _():
        pl.semaphore_wait(barrier, greeted + 2)

    def remote(src, dst, send, recv, where):
        return pltpu.make_async_remote_copy(
            src_ref=src, dst_ref=dst, send_sem=send, recv_sem=recv, device_id=where, device_id_type=MESH
        )

    early = min(EARLY, units)
    farthest = lambda side: cols - 1 if side > 0 else 0

    def early_hop(b, side):
        landing, lane = (from_left, 0) if side > 0 else (from_right, 1)
        lanes = pl.ds(pl.multiple_of(b * BLOCK, BLOCK), BLOCK)
        d = farthest(side)
        return remote(
            part.at[d, pl.ds(0, early), :, lanes], landing.at[d, pl.ds(0, early), :, lanes],
            send_sem.at[lane, d], early_recv.at[lane, b], {"col": me + side},
        )

    def hop(d, t, side, to=None):
        landing, lane = (from_left, 0) if side > 0 else (from_right, 1)
        src, dst = part.at[d, t], landing.at[d, t]
        to = me + side if to is None else to
        slot = d if side > 0 else jnp.where(d == to, cols, d)
        return remote(src, dst, send_sem.at[lane, d], recv_sem.at[slot, t], {"col": me + side})

    def arrived(d, t, side):
        hop(d, t, side, to=me).wait_recv()

    def sent(src, sem):
        remote(src, src, sem, sem, {"col": me}).wait_send()

    def across(u, step):
        return remote(
            land.at[row, u], land.at[row, u], row_send.at[step - 1], row_recv.at[step - 1, u],
            {"row": lax.rem(row + step, rows)},
        )

    span = row_dev // PIECES
    piece = lambda p: slice(p * span, (p + 1) * span)

    def near_hop(t, p, side):
        landing, d = (from_left, 1) if side > 0 else (from_right, cols - 2)
        return remote(
            part.at[d, t, :, piece(p)], landing.at[d, t, :, piece(p)],
            near_send.at[0], near_recv.at[t - shared, p], {"col": me + side},
        )

    def bit_across(u, step, p):
        here = land.at[row, u, :, piece(p)]
        return remote(
            here, here, row_send.at[step - 1], bit_recv.at[step - 1, u - shared, p],
            {"row": lax.rem(row + step, rows)},
        )

    def give(u):
        there = jnp.where(me == 1, 0, cols - 1)
        return remote(
            s_hbm.at[grp, :, u], cipher.at[grp, :, units + u], s_send.at[0], s_recv.at[u], {"col": there}
        )

    def swap(u):
        here = cipher.at[grp, :, units + u]
        return remote(here, here, y_send.at[0], y_recv.at[u], {"grp": 1 - grp})

    if shared:
        @pl.when(giver)
        def _():
            @pl.loop(0, shared)
            def _(u):
                give(u).start()

    far = lambda side: range(cols - 1, 0, -1) if side > 0 else range(cols - 1)
    near = lambda side: (1 if side > 0 else cols - 2) if shared else None

    def block(b, carry):
        @pl.when(b < blocks)
        def _():
            d_load(b).wait()

            @pl.when(b + AHEAD < blocks)
            def _():
                d_load(b + AHEAD).start()

            @pl.when(b == 1)
            def _():
                loads[-1].start()

            lanes = pl.ds(pl.multiple_of(b * BLOCK, BLOCK), BLOCK)
            part[:, :, :, lanes] = lax.dot_general(
                lt[...], d_buf[b], (((1,), (1,)), ((), ())), preferred_element_type=jnp.float32
            ).reshape(cols, units, UNIT, BLOCK)
            if cols > 1:
                for there, side in ((first, 1), (last, -1)):
                    @pl.when(there)
                    def _():
                        early_hop(b, side).start()

        for side, hops, landing in ((1, me, from_left), (-1, cols - 1 - me, from_right)):
            c = b - DELAY * hops

            @pl.when(jnp.logical_not(end) & (c >= 0) & (c < blocks))
            def _():
                early_hop(c, side).wait_recv()
                d, lanes = farthest(side), pl.ds(pl.multiple_of(c * BLOCK, BLOCK), BLOCK)
                part[d, 0:early, :, lanes] += landing[d, 0:early, :, lanes]
                early_hop(c, side).start()

        return carry

    follow = jnp.where(end, 0, DELAY * jnp.maximum(me, cols - 1 - me))
    lax.fori_loop(0, blocks + follow, block, 0)

    for there, side in ((first, 1), (last, -1)):
        @pl.when(there)
        def _():
            @pl.loop(early, units + LEAD * (cols - 1))
            def _(i):
                for d in far(side):
                    if d != near(side):
                        @pl.when((i >= lag(d, side)) & (i < units + lag(d, side)))
                        def _():
                            hop(d, i - lag(d, side), side).start()

            if shared:
                @pl.loop(shared, units - 1)
                def _(t):
                    for p in range(PIECES):
                        near_hop(t, p, side).start()

    for load in loads:
        load.wait()

    def pair(m):
        here = land.at[m, final]
        return remote(here, here, pair_send.at[0], pair_recv.at[m], {"col": beside})

    def consume(u, secret):
        real, imag = [], []
        for s in range(slow):
            lanes = slice(s * LANES, (s + 1) * LANES)
            x = [land[m, u, :, lanes] for m in range(rows)]
            real.append(sum(x[m] * table[2 * m + 2, s : s + 1] for m in range(rows)))
            imag.append(sum(x[m] * table[2 * m + 3, s : s + 1] for m in range(rows)))
        real, imag = swap_bits(real), swap_bits(imag)
        both = jnp.concatenate([jnp.concatenate(real, 0), jnp.concatenate(imag, 0)], 1)
        high = both.astype(jnp.bfloat16)
        low = (both - high.astype(jnp.float32)).astype(jnp.bfloat16)
        mixed = jnp.dot(
            jnp.concatenate([high, low, high], 1), w[...], preferred_element_type=jnp.float32
        )
        spread = []
        for s in range(slow):
            r = mixed[s * UNIT : (s + 1) * UNIT, :LANES]
            i = mixed[s * UNIT : (s + 1) * UNIT, LANES:]
            c, n = table[0, s : s + 1], table[1, s : s + 1]
            spread.append((r * c - i * n, r * n + i * c) if s else (r, i))
        for v, (r, i) in enumerate(fft(spread)):
            lanes = slice(v * LANES, (v + 1) * LANES)
            for k in range(2):
                a, b = cipher[k, 0, secret, :, lanes], cipher[k, 1, secret, :, lanes]
                acc[k, 0, :, lanes] += r * a - i * b
                acc[k, 1, :, lanes] += r * b + i * a

    extra = jnp.where(giver, 1, 0) if shared else 0
    late_from = jnp.maximum(units + LEAD, shared + own_hold)

    def place(i):
        at_end = jnp.where(i < shared, units + i, i - shared)
        m = i - late_from
        inside = jnp.where(m < 0, i - own_hold, shared + m)
        if late > 1:
            inside = jnp.where(m == late - 2, units - 1, jnp.where(m == late - 1, units - 2, inside))
        if late:
            inside = jnp.where(m == late, final, inside)
        early_ones = (i >= own_hold) & (i < own_hold + units - late)
        busy = jnp.where(
            end, (i >= 0) & (i < shared + units), early_ones | ((m >= 0) & (m < late + extra))
        )
        return busy, jnp.where(end, at_end, inside)

    def in_pieces(u):
        return jnp.logical_not(end) & (u >= shared) & (u < units - 1) if shared else False

    wait = jnp.where(end, END_LAG, LAG)
    rest = jnp.maximum(
        right_hold + LEAD * jnp.maximum(cols - 2 - me, 0), left_hold + LEAD * jnp.maximum(me - 1, 0)
    )
    rest = jnp.maximum(units + rest, own_hold + units - late + LAG)
    if late:
        rest = jnp.maximum(rest, late_from + late + extra + LAG)
    steps = jnp.where(end, shared + units + END_LAG, rest)

    def forward(d, side, i):
        beyond, hold, landing = (
            (d > me, right_hold, from_left) if side > 0 else (d < me, left_hold, from_right)
        )
        t = i - hold - lag(d, side)

        @pl.when(jnp.logical_not(end) & beyond & (t >= (early if d == farthest(side) else 0)) & (t < units))
        def _():
            arrived(d, t, side)
            part[d, t] += landing[d, t]
            hop(d, t, side).start()

    def step_of(i, carry):
        for d in range(cols - 1, 1, -1):
            forward(d, 1, i)
        for d in range(cols - 2):
            forward(d, -1, i)
        busy, u = place(i)

        if shared:
            @pl.when(end & (i == 0))
            def _():
                land[row, final] = part[beside, units - 1]
                for step in range(1, rows):
                    across(final, step).start()

            @pl.when(end & (i == LAG))
            def _():
                for step in range(1, rows):
                    across(final, step).wait_recv()
                for m in range(rows):
                    pair(m).start()

        @pl.when(busy & (u != final))
        def _():
            lent = u >= units
            d = jnp.where(lent, beside, me)
            t = jnp.where(lent, u - units, u)
            whole_left, whole_right = me > 0, me < cols - 1
            if shared:
                whole_left, whole_right = whole_left & (me != 1), whole_right & (me != cols - 2)

            @pl.when(end & (u == 0) & (cols > 1))
            def _():
                for there, side in ((last, 1), (first, -1)):
                    @pl.when(there)
                    def _():
                        @pl.loop(0, blocks)
                        def _(b):
                            early_hop(b, side).wait_recv()

            by_blocks = end & (t < early)

            @pl.when(whole_left & jnp.logical_not(lent))
            def _():
                @pl.when(jnp.logical_not(by_blocks))
                def _():
                    arrived(me, t, 1)

                part[me, t] += from_left[me, t]

            @pl.when(whole_right & jnp.logical_not(lent))
            def _():
                @pl.when(jnp.logical_not(by_blocks))
                def _():
                    arrived(me, t, -1)

                part[me, t] += from_right[me, t]

            @pl.when(jnp.logical_not(in_pieces(u)))
            def _():
                land[row, u] = part[d, t]
                for step in range(1, rows):
                    across(u, step).start()

            if shared:
                @pl.when(in_pieces(u))
                def _():
                    for p in range(PIECES):
                        for there, side, landing in ((me == 1, 1, from_left), (me == cols - 2, -1, from_right)):
                            @pl.when(there)
                            def _():
                                near_hop(u, p, side).wait_recv()
                                part[me, u, :, piece(p)] += landing[me, u, :, piece(p)]
                        land[row, u, :, piece(p)] = part[me, u, :, piece(p)]
                        for step in range(1, rows):
                            bit_across(u, step, p).start()

            if shared:
                @pl.when(lent)
                def _():
                    give(t).wait_recv()
                    swap(t).start()

        ready, v = place(i - wait)

        @pl.when(ready)
        def _():
            @pl.when(jnp.logical_not(in_pieces(v)) & (v != final))
            def _():
                for step in range(1, rows):
                    across(v, step).wait_recv()

            if shared:
                @pl.when(in_pieces(v))
                def _():
                    for step in range(1, rows):
                        for p in range(PIECES):
                            bit_across(v, step, p).wait_recv()

                @pl.when((v >= units) & (v != final))
                def _():
                    swap(v - units).wait_recv()

                @pl.when(v == final)
                def _():
                    for m in range(rows):
                        pair(m).wait_recv()
            consume(v, jnp.where(v == final, units - 1, v) if shared else v)

        return carry

    lax.fori_loop(0, steps, step_of, 0)

    width = half_sum.shape[2]
    for k in range(2):
        for p in range(2):
            total = jnp.sum(acc[k, p], axis=0, keepdims=True)
            for q in range(4):
                r = (2 * k + p) * 2 + q % 2
                half_sum[q // 2, r : r + 1, :] = total[:, q * width : (q + 1) * width]
    other = {"limb": 1 - limb}
    trade = remote(half_sum.at[1 - limb], half_in, limb_send.at[0], limb_recv.at[0], other)
    trade.start()
    trade.wait_recv()
    z_in[me] = half_sum[limb] + half_in[...]

    def tell(src, dst):
        return remote(z_in.at[src], z_in.at[src], z_send.at[0], z_recv.at[src], {"col": dst})

    tellers = range(1, cols - 1) if cols > 3 else range(cols)
    ahead = [(me + side * step) for step in range(cols - 1, 0, -1) for side in (1, -1)]
    if cols > 3:
        @pl.when(end)
        def _():
            tell(me, beside).start()

        for there, src in ((me == 1, 0), (me == cols - 2, cols - 1)):
            @pl.when(there)
            def _():
                tell(src, me).wait_recv()
                z_in[me] += z_in[src]

    for dst in ahead:
        @pl.when((jnp.logical_not(end) | (cols <= 3)) & (dst >= 0) & (dst < cols))
        def _():
            tell(me, dst).start()
    for there, side in ((first, 1), (last, -1)):
        @pl.when(there)
        def _():
            lane = 0 if side > 0 else 1
            for d in far(side):
                if d != near(side):
                    sent(part.at[d], send_sem.at[lane, d])
            for step in range(1, rows):
                sent(land.at[row, pl.ds(0, final + 1 if shared else units)], row_send.at[step - 1])
            if shared:
                if units - 1 > shared:
                    sent(part.at[near(side), pl.ds(shared, units - 1 - shared)], near_send.at[0])
                sent(land.at[:, final], pair_send.at[0])
                sent(cipher.at[grp, :, pl.ds(units, shared)], y_send.at[0])

    @pl.when(jnp.logical_not(end))
    def _():
        for d in range(cols - 1, 1, -1):
            @pl.when(d > me)
            def _():
                sent(part.at[d], send_sem.at[0, d])
        for d in range(cols - 2):
            @pl.when(d < me)
            def _():
                sent(part.at[d], send_sem.at[1, d])
        for step in range(1, rows):
            sent(land.at[row, pl.ds(0, units)], row_send.at[step - 1])

    if shared:
        @pl.when(giver)
        def _():
            sent(cipher.at[grp, :, pl.ds(units, shared)], s_send.at[0])

    for src in tellers:
        @pl.when(me != src)
        def _():
            tell(src, me).wait_recv()
    total = z_in[tellers[0]]
    for c in tellers[1:]:
        total = total + z_in[c]
    whole_sum[limb] = total
    gather = remote(whole_sum.at[limb], whole_sum.at[limb], limb_send.at[1], limb_recv.at[1], other)
    gather.start()
    gather.wait_recv()
    for k in range(2):
        for p in range(2):
            for q in range(4):
                r = (2 * k + p) * 2 + q % 2
                out_ref[k, p : p + 1, q * width : (q + 1) * width] = whole_sum[q // 2, r : r + 1, :]

    trade.wait_send()
    gather.wait_send()
    if cols > 3:
        @pl.when(end)
        def _():
            sent(z_in.at[0], z_send.at[0])

        @pl.when(jnp.logical_not(end))
        def _():
            sent(z_in.at[pl.ds(0, cols - 1)], z_send.at[0])
    elif cols > 1:
        sent(z_in.at[pl.ds(0, cols - 1)], z_send.at[0])


def tables(rows, row_dev, half):
    slow = row_dev // LANES
    degree = rows * row_dev
    scale = 1.0 / (math.sqrt(degree) * math.sqrt(2 * half))
    lane = np.arange(LANES)
    at = LANES // slow * (lane % slow) + lane // slow
    n = LANES * np.arange(slow)[:, None] + lane[None, :]
    a, m = np.arange(rows)[:, None, None, None], np.arange(rows)[None, :, None, None]
    turn = -np.pi * ((n + m * row_dev) * (2 * a + 1) % (2 * degree)) / degree
    turn = np.exp(1j * turn) * scale
    turn = np.stack([turn.real, turn.imag], 2).reshape(rows, 2 * rows, slow, LANES)
    twiddle = np.exp(-2j * np.pi * np.arange(slow)[:, None] * lane[None, :] / row_dev)
    twiddle = np.stack([twiddle.real, twiddle.imag], 0)
    twiddle = np.broadcast_to(twiddle, (rows,) + twiddle.shape)
    table = np.concatenate([twiddle, turn], 1).astype(np.float32)
    w = np.exp(-2j * np.pi * (at[:, None] * lane[None, :] % LANES) / LANES)
    w = np.block([[w.real, w.imag], [-w.imag, w.real]]).astype(np.float32)
    high = w.astype(jnp.bfloat16)
    low = (w - high.astype(np.float32)).astype(jnp.bfloat16)
    return table, np.concatenate([high, high, low], 0)


def body(database, lwe_matrix, secret_ct):
    rows, cols = lax.axis_size("row"), lax.axis_size("col")
    grps = lax.axis_size("grp")
    row_dev, depth = database.shape
    half = lwe_matrix.shape[2]
    own = half // cols
    units = own // UNIT
    slow = row_dev // LANES
    shared = units * 10 // 16 if cols > 3 and grps == 2 else 0
    places = units + shared + 1
    blocks = row_dev // BLOCK
    table, w = tables(rows, row_dev, half)
    dma = pltpu.SemaphoreType.DMA
    flow = pltpu.VMEM((cols, units, UNIT, row_dev), jnp.float32)
    lots = max(shared, 1)
    hbm = pl.BlockSpec(memory_space=pl.ANY)
    return pl.pallas_call(
        functools.partial(kernel, cols, rows, grps, shared),
        out_shape=jax.ShapeDtypeStruct((2, 2, row_dev), jnp.float32),
        in_specs=[hbm] * 5,
        out_specs=pl.BlockSpec(memory_space=pltpu.VMEM),
        scratch_shapes=[
            pltpu.VMEM((depth, half), lwe_matrix.dtype),
            pltpu.VMEM((half, depth), lwe_matrix.dtype),
            pltpu.VMEM((blocks, BLOCK, depth), database.dtype),
            flow,
            flow,
            flow,
            pltpu.VMEM((rows, places, UNIT, row_dev), jnp.float32),
            pltpu.VMEM((2, 2, units + shared, UNIT, row_dev), jnp.float32),
            pltpu.VMEM(table.shape[1:], jnp.float32),
            pltpu.VMEM(w.shape, jnp.bfloat16),
            pltpu.VMEM((2, 2, UNIT, row_dev), jnp.float32),
            pltpu.VMEM((2, 8, row_dev // 4), jnp.float32),
            pltpu.VMEM((8, row_dev // 4), jnp.float32),
            pltpu.VMEM((cols, 8, row_dev // 4), jnp.float32),
            pltpu.VMEM((2, 8, row_dev // 4), jnp.float32),
            dma((3,)),
            dma((4,)),
            dma((blocks,)),
            dma((2, cols)),
            dma((cols + 1, units)),
            dma((max(rows - 1, 1),)),
            dma((max(rows - 1, 1), places)),
            dma((1,)),
            dma((lots,)),
            dma((1,)),
            dma((lots,)),
            dma((2,)),
            dma((2,)),
            dma((1,)),
            dma((cols,)),
            dma((1,)),
            dma((max(units - 1 - shared, 1), PIECES)),
            dma((max(rows - 1, 1), max(units - 1 - shared, 1), PIECES)),
            dma((1,)),
            dma((rows,)),
            dma((2, blocks)),
        ],
        compiler_params=pltpu.CompilerParams(
            collective_id=0, has_side_effects=True, vmem_limit_bytes=55168 << 10
        ),
    )(
        lwe_matrix[:, 0, :],
        database,
        secret_ct[:, :, 0].reshape(2, 2, units, UNIT, row_dev),
        jnp.asarray(table),
        jnp.asarray(w),
    )


def solution(mesh):
    placed = (P(("grp", "row"), "col"), P("col", "limb", None), P(None, None, "limb", "col", "row"))
    return jax.shard_map(
        body, mesh=mesh, in_specs=placed, out_specs=P("grp", None, "row"), check_vma=False
    )
```

```python
import functools
import math

import jax
import jax.numpy as jnp
import numpy as np
from jax import lax
from jax.experimental import pallas as pl
from jax.experimental.pallas import tpu as pltpu
from jax.sharding import PartitionSpec as P

MESH = pl.DeviceIdType.MESH
UNIT = 8
LANES = 128
BLOCK = 256
LEAD = 4
AHEAD = 4
EARLY = 4
NEXT = 2
DELAY = 4
PIECES = 1
LAG = 3
END_LAG = 5
HOLD = 3


def fft(values):
    count = len(values)
    if count == 1:
        return values
    even, odd = fft(values[0::2]), fft(values[1::2])
    low, high = [], []
    for k in range(count // 2):
        (er, ei), (r, i) = even[k], odd[k]
        if k == 0:
            tr, ti = r, i
        elif 4 * k == count:
            tr, ti = i, -r
        elif 8 * k == count:
            half = math.sqrt(0.5)
            tr, ti = (r + i) * half, (i - r) * half
        elif 8 * k == 3 * count:
            half = math.sqrt(0.5)
            tr, ti = (i - r) * half, -(r + i) * half
        else:
            c, s = math.cos(2 * math.pi * k / count), math.sin(2 * math.pi * k / count)
            tr, ti = r * c + i * s, i * c - r * s
        low.append((er + tr, ei + ti))
        high.append((er - tr, ei - ti))
    return low + high


def swap_bits(blocks):
    blocks = list(blocks)
    lane = lax.broadcasted_iota(jnp.int32, blocks[0].shape, 1)
    step = 1
    while step < len(blocks):
        clear = (lane & step) == 0
        for b in range(len(blocks)):
            if not b & step:
                x, y = blocks[b], blocks[b + step]
                blocks[b] = jnp.where(clear, x, pltpu.roll(y, step, 1))
                blocks[b + step] = jnp.where(clear, pltpu.roll(x, LANES - step, 1), y)
        step *= 2
    return blocks


def kernel(cols, rows, grps, shared, l_hbm, d_hbm, s_hbm, table_hbm, w_hbm, out_ref,
           l_buf, lt_outer, lt_inner, d_buf, part, from_left, from_right, land, cipher, table, w, acc,
           half_sum, half_in, z_in, whole_sum,
           load_sem, l_sem, d_sem, send_sem, recv_sem, row_send, row_recv, s_send, s_recv, y_send, y_recv,
           limb_send, limb_recv, z_send, z_recv, near_send, near_recv, bit_recv, pair_send, pair_recv, early_recv):
    me, row = lax.axis_index("col"), lax.axis_index("row")
    grp, limb = lax.axis_index("grp"), lax.axis_index("limb")
    units, row_dev = part.shape[1], part.shape[3]
    slow = row_dev // LANES
    blocks = d_buf.shape[0]
    first, last = me == 0, me == cols - 1
    end = first | last
    beside = jnp.where(first, 1, cols - 2)
    giver = ((me == 1) | (me == cols - 2)) if shared else None
    late = units - shared if shared else 0
    right_hold = HOLD * jnp.maximum(me - 1, 0)
    left_hold = HOLD * jnp.maximum(cols - 2 - me, 0)
    lag = lambda d, side: LEAD * (cols - 1 - d) if side > 0 else LEAD * d
    by_left, by_right = right_hold + lag(me, 1), left_hold + lag(me, -1)
    if shared:
        by_left, by_right = jnp.where(me == 1, 0, by_left), jnp.where(me == cols - 2, 0, by_right)
    own_hold = jnp.where(end, 0, jnp.maximum(by_left, by_right))
    final = units + shared

    loads = [
        pltpu.make_async_copy(table_hbm.at[row], table, load_sem.at[0]),
        pltpu.make_async_copy(w_hbm, w, load_sem.at[1]),
        pltpu.make_async_copy(s_hbm, cipher.at[:, :, pl.ds(0, units)], load_sem.at[2]),
    ]
    chunks = l_sem.shape[0]
    chunk = l_buf.shape[1] // chunks
    outer = [0, chunks - 1] if chunks > 1 else [0]
    inner = list(range(1, chunks - 1))
    held = chunk * cols // l_buf.shape[1]

    def l_load(c):
        there = pl.ds(c * chunk, chunk)
        return pltpu.make_async_copy(l_hbm.at[:, there], l_buf.at[:, there], l_sem.at[c])

    def turn_over(c, lt, at):
        l_load(c).wait()
        lt[at * chunk : (at + 1) * chunk, :] = l_buf[:, c * chunk : (c + 1) * chunk].T

    def d_load(b):
        return pltpu.make_async_copy(
            d_hbm.at[pl.ds(b * BLOCK, BLOCK)], d_buf.at[b], d_sem.at[lax.rem(b, AHEAD)]
        )

    for c in outer:
        l_load(c).start()
    for b in range(min(AHEAD, blocks)):
        d_load(b).start()
    for c in inner:
        l_load(c).start()
    for load in loads[:-1]:
        load.start()

    barrier = pltpu.get_barrier_semaphore()
    greeted = 0
    peers = [{"row": lax.rem(row + step, rows)} for step in range(1, rows)]
    peers += [{"limb": 1 - limb}]
    if shared:
        peers += [{"grp": 1 - grp}]
    for peer in peers:
        pl.semaphore_signal(barrier, inc=1, device_id=peer, device_id_type=MESH)
        greeted += 1
    for there, side in ((me > 0, -1), (me < cols - 1, 1)):
        @pl.when(there)
        def _():
            pl.semaphore_signal(barrier, inc=1, device_id={"col": me + side}, device_id_type=MESH)

    acc[...] = jnp.zeros_like(acc)
    for at, c in enumerate(outer):
        turn_over(c, lt_outer, at)

    @pl.when(end)
    def _():
        pl.semaphore_wait(barrier, greeted + min(cols - 1, 1))

    @pl.when(jnp.logical_not(end))
    def _():
        pl.semaphore_wait(barrier, greeted + 2)

    def remote(src, dst, send, recv, where):
        return pltpu.make_async_remote_copy(
            src_ref=src, dst_ref=dst, send_sem=send, recv_sem=recv, device_id=where, device_id_type=MESH
        )

    early, ahead_of_rest = min(EARLY, units), min(EARLY + NEXT, units)
    farthest = lambda side: cols - 1 if side > 0 else 0

    def early_hop(b, side):
        landing, lane = (from_left, 0) if side > 0 else (from_right, 1)
        lanes = pl.ds(pl.multiple_of(b * BLOCK, BLOCK), BLOCK)
        d = farthest(side)
        return remote(
            part.at[d, pl.ds(0, early), :, lanes], landing.at[d, pl.ds(0, early), :, lanes],
            send_sem.at[lane, d], early_recv.at[lane, b], {"col": me + side},
        )

    def hop(d, t, side, to=None):
        landing, lane = (from_left, 0) if side > 0 else (from_right, 1)
        src, dst = part.at[d, t], landing.at[d, t]
        to = me + side if to is None else to
        slot = d if side > 0 or recv_sem.shape[0] == cols else jnp.where(d == to, cols, d)
        return remote(src, dst, send_sem.at[lane, d], recv_sem.at[slot, t], {"col": me + side})

    def arrived(d, t, side):
        hop(d, t, side, to=me).wait_recv()

    def sent(src, sem):
        remote(src, src, sem, sem, {"col": me}).wait_send()

    def across(u, step):
        return remote(
            land.at[row, u], land.at[row, u], row_send.at[step - 1], row_recv.at[step - 1, u],
            {"row": lax.rem(row + step, rows)},
        )

    span = row_dev // PIECES
    piece = lambda p: slice(p * span, (p + 1) * span)

    def near_hop(t, p, side):
        landing, d = (from_left, 1) if side > 0 else (from_right, cols - 2)
        return remote(
            part.at[d, t, :, piece(p)], landing.at[d, t, :, piece(p)],
            near_send.at[0], near_recv.at[t - shared, p], {"col": me + side},
        )

    def bit_across(u, step, p):
        here = land.at[row, u, :, piece(p)]
        return remote(
            here, here, row_send.at[step - 1], bit_recv.at[step - 1, u - shared, p],
            {"row": lax.rem(row + step, rows)},
        )

    def give(u):
        there = jnp.where(me == 1, 0, cols - 1)
        return remote(
            s_hbm.at[grp, :, u], cipher.at[grp, :, units + u], s_send.at[0], s_recv.at[u], {"col": there}
        )

    def swap(u):
        here = cipher.at[grp, :, units + u]
        return remote(here, here, y_send.at[0], y_recv.at[u], {"grp": 1 - grp})

    if shared:
        @pl.when(giver)
        def _():
            @pl.loop(0, shared)
            def _(u):
                give(u).start()

    far = lambda side: range(cols - 1, 0, -1) if side > 0 else range(cols - 1)
    near = lambda side: (1 if side > 0 else cols - 2) if shared else None

    def product(lt, b):
        found = lax.dot_general(
            lt[...], d_buf[b], (((1,), (1,)), ((), ())), preferred_element_type=jnp.float32
        )
        return found.reshape(-1, units, UNIT, BLOCK)

    def block(b, carry):
        @pl.when(b < blocks)
        def _():
            d_load(b).wait()

            @pl.when(b + AHEAD < blocks)
            def _():
                d_load(b + AHEAD).start()

            lanes = pl.ds(pl.multiple_of(b * BLOCK, BLOCK), BLOCK)
            found = product(lt_outer, b)
            for at, c in enumerate(outer):
                part[c * held : (c + 1) * held, :, :, lanes] = found[at * held : (at + 1) * held]
            if cols > 1:
                for there, side in ((first, 1), (last, -1)):
                    @pl.when(there)
                    def _():
                        early_hop(b, side).start()

        @pl.when(b == blocks)
        def _():
            if cols > 1:
                for there, side in ((first, 1), (last, -1)):
                    @pl.when(there)
                    def _():
                        for t in range(early, ahead_of_rest):
                            hop(farthest(side), t, side).start()

            loads[-1].start()
            for at, c in enumerate(inner):
                turn_over(c, lt_inner, at)

        if inner:
            @pl.when((b >= blocks) & (b < 2 * blocks))
            def _():
                lanes = pl.ds(pl.multiple_of((b - blocks) * BLOCK, BLOCK), BLOCK)
                part[held : cols - held, :, :, lanes] = product(lt_inner, b - blocks)

        for side, hops, landing in ((1, me, from_left), (-1, cols - 1 - me, from_right)):
            c = b - DELAY * hops

            @pl.when(jnp.logical_not(end) & (c >= 0) & (c < blocks))
            def _():
                early_hop(c, side).wait_recv()
                d, lanes = farthest(side), pl.ds(pl.multiple_of(c * BLOCK, BLOCK), BLOCK)
                part[d, 0:early, :, lanes] += landing[d, 0:early, :, lanes]
                early_hop(c, side).start()

        return carry

    follow = jnp.where(end, 0, DELAY * jnp.maximum(me, cols - 1 - me))
    lax.fori_loop(0, blocks + jnp.maximum(follow, blocks), block, 0)

    for there, side in ((first, 1), (last, -1)):
        @pl.when(there)
        def _():
            @pl.loop(min(early, LEAD), units + LEAD * (cols - 1))
            def _(i):
                for d in far(side):
                    if d != near(side):
                        t = i - lag(d, side)

                        @pl.when((t >= (ahead_of_rest if d == farthest(side) else 0)) & (t < units))
                        def _():
                            hop(d, t, side).start()

            if shared:
                @pl.loop(shared, units - 1)
                def _(t):
                    for p in range(PIECES):
                        near_hop(t, p, side).start()

    for load in loads:
        load.wait()

    def pair(m):
        here = land.at[m, final]
        return remote(here, here, pair_send.at[0], pair_recv.at[m], {"col": beside})

    def consume(u, secret):
        real, imag = [], []
        for s in range(slow):
            lanes = slice(s * LANES, (s + 1) * LANES)
            x = [land[m, u, :, lanes] for m in range(rows)]
            real.append(sum(x[m] * table[2 * m + 2, s : s + 1] for m in range(rows)))
            imag.append(sum(x[m] * table[2 * m + 3, s : s + 1] for m in range(rows)))
        real, imag = swap_bits(real), swap_bits(imag)
        both = jnp.concatenate([jnp.concatenate(real, 0), jnp.concatenate(imag, 0)], 1)
        high = both.astype(jnp.bfloat16)
        low = (both - high.astype(jnp.float32)).astype(jnp.bfloat16)
        mixed = jnp.dot(
            jnp.concatenate([high, low, high], 1), w[...], preferred_element_type=jnp.float32
        )
        spread = []
        for s in range(slow):
            r = mixed[s * UNIT : (s + 1) * UNIT, :LANES]
            i = mixed[s * UNIT : (s + 1) * UNIT, LANES:]
            c, n = table[0, s : s + 1], table[1, s : s + 1]
            spread.append((r * c - i * n, r * n + i * c) if s else (r, i))
        for v, (r, i) in enumerate(fft(spread)):
            lanes = slice(v * LANES, (v + 1) * LANES)
            for k in range(2):
                a, b = cipher[k, 0, secret, :, lanes], cipher[k, 1, secret, :, lanes]
                acc[k, 0, :, lanes] += r * a - i * b
                acc[k, 1, :, lanes] += r * b + i * a

    extra = jnp.where(giver, 1, 0) if shared else 0
    late_from = jnp.maximum(units + LEAD, shared + own_hold)

    def place(i):
        at_end = jnp.where(i < shared, units + i, i - shared)
        m = i - late_from
        inside = jnp.where(m < 0, i - own_hold, shared + m)
        if late > 1:
            inside = jnp.where(m == late - 2, units - 1, jnp.where(m == late - 1, units - 2, inside))
        if late:
            inside = jnp.where(m == late, final, inside)
        early_ones = (i >= own_hold) & (i < own_hold + units - late)
        busy = jnp.where(
            end, (i >= 0) & (i < shared + units), early_ones | ((m >= 0) & (m < late + extra))
        )
        return busy, jnp.where(end, at_end, inside)

    def in_pieces(u):
        return jnp.logical_not(end) & (u >= shared) & (u < units - 1) if shared else False

    wait = jnp.where(end, END_LAG, LAG)
    rest = jnp.maximum(
        right_hold + LEAD * jnp.maximum(cols - 2 - me, 0), left_hold + LEAD * jnp.maximum(me - 1, 0)
    )
    rest = jnp.maximum(units + rest, own_hold + units - late + LAG)
    if late:
        rest = jnp.maximum(rest, late_from + late + extra + LAG)
    steps = jnp.where(end, shared + units + END_LAG, rest)

    def forward(d, side, i):
        beyond, hold, landing = (
            (d > me, right_hold, from_left) if side > 0 else (d < me, left_hold, from_right)
        )
        t = i - hold - lag(d, side)

        @pl.when(jnp.logical_not(end) & beyond & (t >= (early if d == farthest(side) else 0)) & (t < units))
        def _():
            arrived(d, t, side)
            part[d, t] += landing[d, t]
            hop(d, t, side).start()

    def step_of(i, carry):
        for d in range(cols - 1, 1, -1):
            forward(d, 1, i)
        for d in range(cols - 2):
            forward(d, -1, i)
        busy, u = place(i)

        if shared:
            @pl.when(end & (i == 0))
            def _():
                land[row, final] = part[beside, units - 1]
                for step in range(1, rows):
                    across(final, step).start()

            @pl.when(end & (i == LAG))
            def _():
                for step in range(1, rows):
                    across(final, step).wait_recv()
                for m in range(rows):
                    pair(m).start()

        @pl.when(busy & (u != final))
        def _():
            lent = u >= units
            d = jnp.where(lent, beside, me)
            t = jnp.where(lent, u - units, u)
            whole_left, whole_right = me > 0, me < cols - 1
            if shared:
                whole_left, whole_right = whole_left & (me != 1), whole_right & (me != cols - 2)

            @pl.when(end & (u == 0) & (cols > 1))
            def _():
                for there, side in ((last, 1), (first, -1)):
                    @pl.when(there)
                    def _():
                        @pl.loop(0, blocks)
                        def _(b):
                            early_hop(b, side).wait_recv()

            by_blocks = end & (t < early)

            @pl.when(whole_left & jnp.logical_not(lent))
            def _():
                @pl.when(jnp.logical_not(by_blocks))
                def _():
                    arrived(me, t, 1)

                part[me, t] += from_left[me, t]

            @pl.when(whole_right & jnp.logical_not(lent))
            def _():
                @pl.when(jnp.logical_not(by_blocks))
                def _():
                    arrived(me, t, -1)

                part[me, t] += from_right[me, t]

            @pl.when(jnp.logical_not(in_pieces(u)))
            def _():
                land[row, u] = part[d, t]
                for step in range(1, rows):
                    across(u, step).start()

            if shared:
                @pl.when(in_pieces(u))
                def _():
                    for p in range(PIECES):
                        for there, side, landing in ((me == 1, 1, from_left), (me == cols - 2, -1, from_right)):
                            @pl.when(there)
                            def _():
                                near_hop(u, p, side).wait_recv()
                                part[me, u, :, piece(p)] += landing[me, u, :, piece(p)]
                        land[row, u, :, piece(p)] = part[me, u, :, piece(p)]
                        for step in range(1, rows):
                            bit_across(u, step, p).start()

            if shared:
                @pl.when(lent)
                def _():
                    give(t).wait_recv()
                    swap(t).start()

        ready, v = place(i - wait)

        @pl.when(ready)
        def _():
            @pl.when(jnp.logical_not(in_pieces(v)) & (v != final))
            def _():
                for step in range(1, rows):
                    across(v, step).wait_recv()

            if shared:
                @pl.when(in_pieces(v))
                def _():
                    for step in range(1, rows):
                        for p in range(PIECES):
                            bit_across(v, step, p).wait_recv()

                @pl.when((v >= units) & (v != final))
                def _():
                    swap(v - units).wait_recv()

                @pl.when(v == final)
                def _():
                    for m in range(rows):
                        pair(m).wait_recv()
            consume(v, jnp.where(v == final, units - 1, v) if shared else v)

        return carry

    lax.fori_loop(0, steps, step_of, 0)

    width = half_sum.shape[2]
    for k in range(2):
        for p in range(2):
            total = jnp.sum(acc[k, p], axis=0, keepdims=True)
            for q in range(4):
                r = (2 * k + p) * 2 + q % 2
                half_sum[q // 2, r : r + 1, :] = total[:, q * width : (q + 1) * width]
    other = {"limb": 1 - limb}
    trade = remote(half_sum.at[1 - limb], half_in, limb_send.at[0], limb_recv.at[0], other)
    trade.start()
    trade.wait_recv()
    z_in[me] = half_sum[limb] + half_in[...]

    def tell(src, dst):
        return remote(z_in.at[src], z_in.at[src], z_send.at[0], z_recv.at[src], {"col": dst})

    tellers = range(1, cols - 1) if cols > 3 else range(cols)
    ahead = [(me + side * step) for step in range(cols - 1, 0, -1) for side in (1, -1)]
    if cols > 3:
        @pl.when(end)
        def _():
            tell(me, beside).start()

        for there, src in ((me == 1, 0), (me == cols - 2, cols - 1)):
            @pl.when(there)
            def _():
                tell(src, me).wait_recv()
                z_in[me] += z_in[src]

    for dst in ahead:
        @pl.when((jnp.logical_not(end) | (cols <= 3)) & (dst >= 0) & (dst < cols))
        def _():
            tell(me, dst).start()
    for there, side in ((first, 1), (last, -1)):
        @pl.when(there)
        def _():
            lane = 0 if side > 0 else 1
            for d in far(side):
                if d != near(side):
                    sent(part.at[d], send_sem.at[lane, d])
            for step in range(1, rows):
                sent(land.at[row, pl.ds(0, final + 1 if shared else units)], row_send.at[step - 1])
            if shared:
                if units - 1 > shared:
                    sent(part.at[near(side), pl.ds(shared, units - 1 - shared)], near_send.at[0])
                sent(land.at[:, final], pair_send.at[0])
                sent(cipher.at[grp, :, pl.ds(units, shared)], y_send.at[0])

    @pl.when(jnp.logical_not(end))
    def _():
        for d in range(cols - 1, 1, -1):
            @pl.when(d > me)
            def _():
                sent(part.at[d], send_sem.at[0, d])
        for d in range(cols - 2):
            @pl.when(d < me)
            def _():
                sent(part.at[d], send_sem.at[1, d])
        for step in range(1, rows):
            sent(land.at[row, pl.ds(0, units)], row_send.at[step - 1])

    if shared:
        @pl.when(giver)
        def _():
            sent(cipher.at[grp, :, pl.ds(units, shared)], s_send.at[0])

    for src in tellers:
        @pl.when(me != src)
        def _():
            tell(src, me).wait_recv()
    total = z_in[tellers[0]]
    for c in tellers[1:]:
        total = total + z_in[c]
    whole_sum[limb] = total
    gather = remote(whole_sum.at[limb], whole_sum.at[limb], limb_send.at[1], limb_recv.at[1], other)
    gather.start()
    gather.wait_recv()
    for k in range(2):
        for p in range(2):
            for q in range(4):
                r = (2 * k + p) * 2 + q % 2
                out_ref[k, p : p + 1, q * width : (q + 1) * width] = whole_sum[q // 2, r : r + 1, :]

    trade.wait_send()
    gather.wait_send()
    if cols > 3:
        @pl.when(end)
        def _():
            sent(z_in.at[0], z_send.at[0])

        @pl.when(jnp.logical_not(end))
        def _():
            sent(z_in.at[pl.ds(0, cols - 1)], z_send.at[0])
    elif cols > 1:
        sent(z_in.at[pl.ds(0, cols - 1)], z_send.at[0])


def tables(rows, row_dev, half):
    slow = row_dev // LANES
    degree = rows * row_dev
    scale = 1.0 / (math.sqrt(degree) * math.sqrt(2 * half))
    lane = np.arange(LANES)
    at = LANES // slow * (lane % slow) + lane // slow
    n = LANES * np.arange(slow)[:, None] + lane[None, :]
    a, m = np.arange(rows)[:, None, None, None], np.arange(rows)[None, :, None, None]
    turn = -np.pi * ((n + m * row_dev) * (2 * a + 1) % (2 * degree)) / degree
    turn = np.exp(1j * turn) * scale
    turn = np.stack([turn.real, turn.imag], 2).reshape(rows, 2 * rows, slow, LANES)
    twiddle = np.exp(-2j * np.pi * np.arange(slow)[:, None] * lane[None, :] / row_dev)
    twiddle = np.stack([twiddle.real, twiddle.imag], 0)
    twiddle = np.broadcast_to(twiddle, (rows,) + twiddle.shape)
    table = np.concatenate([twiddle, turn], 1).astype(np.float32)
    w = np.exp(-2j * np.pi * (at[:, None] * lane[None, :] % LANES) / LANES)
    w = np.block([[w.real, w.imag], [-w.imag, w.real]]).astype(np.float32)
    high = w.astype(jnp.bfloat16)
    low = (w - high.astype(np.float32)).astype(jnp.bfloat16)
    return table, np.concatenate([high, high, low], 0)


def body(database, lwe_matrix, secret_ct):
    rows, cols = lax.axis_size("row"), lax.axis_size("col")
    grps = lax.axis_size("grp")
    row_dev, depth = database.shape
    half = lwe_matrix.shape[2]
    own = half // cols
    units = own // UNIT
    slow = row_dev // LANES
    shared = units * 10 // 16 if cols > 3 and grps == 2 else 0
    places = units + shared + 1
    blocks = row_dev // BLOCK
    chunks = half // max(own, LANES)
    table, w = tables(rows, row_dev, half)
    dma = pltpu.SemaphoreType.DMA
    flow = pltpu.VMEM((cols, units, UNIT, row_dev), jnp.float32)
    lots = max(shared, 1)
    hbm = pl.BlockSpec(memory_space=pl.ANY)
    return pl.pallas_call(
        functools.partial(kernel, cols, rows, grps, shared),
        out_shape=jax.ShapeDtypeStruct((2, 2, row_dev), jnp.float32),
        in_specs=[hbm] * 5,
        out_specs=pl.BlockSpec(memory_space=pltpu.VMEM),
        scratch_shapes=[
            pltpu.VMEM((depth, half), lwe_matrix.dtype),
            pltpu.VMEM((min(2, chunks) * half // chunks, depth), lwe_matrix.dtype),
            pltpu.VMEM((max(chunks - 2, 1) * half // chunks, depth), lwe_matrix.dtype),
            pltpu.VMEM((blocks, BLOCK, depth), database.dtype),
            flow,
            flow,
            flow,
            pltpu.VMEM((rows, places, UNIT, row_dev), jnp.float32),
            pltpu.VMEM((2, 2, units + shared, UNIT, row_dev), jnp.float32),
            pltpu.VMEM(table.shape[1:], jnp.float32),
            pltpu.VMEM(w.shape, jnp.bfloat16),
            pltpu.VMEM((2, 2, UNIT, row_dev), jnp.float32),
            pltpu.VMEM((2, 8, row_dev // 4), jnp.float32),
            pltpu.VMEM((8, row_dev // 4), jnp.float32),
            pltpu.VMEM((cols, 8, row_dev // 4), jnp.float32),
            pltpu.VMEM((2, 8, row_dev // 4), jnp.float32),
            dma((3,)),
            dma((chunks,)),
            dma((AHEAD,)),
            dma((2, cols)),
            dma((cols if shared and cols == 4 else cols + 1, units)),
            dma((max(rows - 1, 1),)),
            dma((max(rows - 1, 1), places)),
            dma((1,)),
            dma((lots,)),
            dma((1,)),
            dma((lots,)),
            dma((2,)),
            dma((2,)),
            dma((1,)),
            dma((cols,)),
            dma((1,)),
            dma((max(units - 1 - shared, 1), PIECES)),
            dma((max(rows - 1, 1), max(units - 1 - shared, 1), PIECES)),
            dma((1,)),
            dma((rows,)),
            dma((2, blocks)),
        ],
        compiler_params=pltpu.CompilerParams(
            collective_id=0, has_side_effects=True, vmem_limit_bytes=55168 << 10
        ),
    )(
        lwe_matrix[:, 0, :],
        database,
        secret_ct[:, :, 0].reshape(2, 2, units, UNIT, row_dev),
        jnp.asarray(table),
        jnp.asarray(w),
    )


def solution(mesh):
    placed = (P(("grp", "row"), "col"), P("col", "limb", None), P(None, None, "limb", "col", "row"))
    return jax.shard_map(
        body, mesh=mesh, in_specs=placed, out_specs=P("grp", None, "row"), check_vma=False
    )
```

```python
import functools
import math

import jax
import jax.numpy as jnp
import numpy as np
from jax import lax
from jax.experimental import pallas as pl
from jax.experimental.pallas import tpu as pltpu
from jax.sharding import PartitionSpec as P

MESH = pl.DeviceIdType.MESH
UNIT = 8
LANES = 128
BLOCK = 256
LEAD = 4
AHEAD = 4
HEAD = 5
PAIR = 2
EARLY = 4
NEXT = 2
DELAY = 4
PIECES = 1
LAG = 3
END_LAG = 5
HOLD = 3


def fft(values):
    count = len(values)
    if count == 1:
        return values
    even, odd = fft(values[0::2]), fft(values[1::2])
    low, high = [], []
    for k in range(count // 2):
        (er, ei), (r, i) = even[k], odd[k]
        if k == 0:
            tr, ti = r, i
        elif 4 * k == count:
            tr, ti = i, -r
        elif 8 * k == count:
            half = math.sqrt(0.5)
            tr, ti = (r + i) * half, (i - r) * half
        elif 8 * k == 3 * count:
            half = math.sqrt(0.5)
            tr, ti = (i - r) * half, -(r + i) * half
        else:
            c, s = math.cos(2 * math.pi * k / count), math.sin(2 * math.pi * k / count)
            tr, ti = r * c + i * s, i * c - r * s
        low.append((er + tr, ei + ti))
        high.append((er - tr, ei - ti))
    return low + high


def swap_bits(blocks):
    blocks = list(blocks)
    lane = lax.broadcasted_iota(jnp.int32, blocks[0].shape, 1)
    step = 1
    while step < len(blocks):
        clear = (lane & step) == 0
        for b in range(len(blocks)):
            if not b & step:
                x, y = blocks[b], blocks[b + step]
                blocks[b] = jnp.where(clear, x, pltpu.roll(y, step, 1))
                blocks[b + step] = jnp.where(clear, pltpu.roll(x, LANES - step, 1), y)
        step *= 2
    return blocks


def kernel(cols, rows, grps, shared, l_hbm, d_hbm, s_hbm, table_hbm, w_hbm, out_ref,
           l_buf, lt_outer, lt_inner, d_buf, part, from_left, from_right, land, cipher, table, w, acc,
           half_sum, half_in, z_in, whole_sum,
           load_sem, l_sem, d_sem, send_sem, recv_sem, row_send, row_recv, s_send, s_recv, y_send, y_recv,
           limb_send, limb_recv, z_send, z_recv, near_send, near_recv, bit_recv, pair_send, pair_recv, early_recv):
    me, row = lax.axis_index("col"), lax.axis_index("row")
    grp, limb = lax.axis_index("grp"), lax.axis_index("limb")
    units, row_dev = part.shape[1], part.shape[3]
    slow = row_dev // LANES
    blocks = d_buf.shape[0]
    first, last = me == 0, me == cols - 1
    end = first | last
    beside = jnp.where(first, 1, cols - 2)
    giver = ((me == 1) | (me == cols - 2)) if shared else None
    head = max(min(HEAD, shared), shared - units // 2)
    late = units - shared if shared else 0
    right_hold = HOLD * jnp.maximum(me - 1, 0)
    left_hold = HOLD * jnp.maximum(cols - 2 - me, 0)
    lag = lambda d, side: LEAD * (cols - 1 - d) if side > 0 else LEAD * d
    by_left, by_right = right_hold + lag(me, 1), left_hold + lag(me, -1)
    if shared:
        by_left, by_right = jnp.where(me == 1, 0, by_left), jnp.where(me == cols - 2, 0, by_right)
    own_hold = jnp.where(end, 0, jnp.maximum(by_left, by_right))
    final = units + shared

    loads = [
        pltpu.make_async_copy(table_hbm.at[row], table, load_sem.at[0]),
        pltpu.make_async_copy(w_hbm, w, load_sem.at[1]),
        pltpu.make_async_copy(s_hbm, cipher.at[:, :, pl.ds(0, units)], load_sem.at[2]),
    ]
    chunks = l_sem.shape[0]
    chunk = l_buf.shape[1] // chunks
    outer = [0, chunks - 1] if chunks > 1 else [0]
    inner = list(range(1, chunks - 1))
    held = chunk * cols // l_buf.shape[1]

    def l_load(c):
        there = pl.ds(c * chunk, chunk)
        return pltpu.make_async_copy(l_hbm.at[:, there], l_buf.at[:, there], l_sem.at[c])

    def turn_over(c, lt, at):
        l_load(c).wait()
        lt[at * chunk : (at + 1) * chunk, :] = l_buf[:, c * chunk : (c + 1) * chunk].T

    def d_load(b):
        return pltpu.make_async_copy(
            d_hbm.at[pl.ds(b * BLOCK, BLOCK)], d_buf.at[b], d_sem.at[lax.rem(b, AHEAD)]
        )

    for c in outer:
        l_load(c).start()
    for b in range(min(AHEAD, blocks)):
        d_load(b).start()
    for c in inner:
        l_load(c).start()
    for load in loads[:-1]:
        load.start()

    barrier = pltpu.get_barrier_semaphore()
    greeted = 0
    peers = [{"row": lax.rem(row + step, rows)} for step in range(1, rows)]
    peers += [{"limb": 1 - limb}]
    if shared:
        peers += [{"grp": 1 - grp}]
    for peer in peers:
        pl.semaphore_signal(barrier, inc=1, device_id=peer, device_id_type=MESH)
        greeted += 1
    for there, side in ((me > 0, -1), (me < cols - 1, 1)):
        @pl.when(there)
        def _():
            pl.semaphore_signal(barrier, inc=1, device_id={"col": me + side}, device_id_type=MESH)

    acc[...] = jnp.zeros_like(acc)
    for at, c in enumerate(outer):
        turn_over(c, lt_outer, at)

    @pl.when(end)
    def _():
        pl.semaphore_wait(barrier, greeted + min(cols - 1, 1))

    @pl.when(jnp.logical_not(end))
    def _():
        pl.semaphore_wait(barrier, greeted + 2)

    def remote(src, dst, send, recv, where):
        return pltpu.make_async_remote_copy(
            src_ref=src, dst_ref=dst, send_sem=send, recv_sem=recv, device_id=where, device_id_type=MESH
        )

    early, ahead_of_rest = min(EARLY, units), min(EARLY + NEXT, units)
    couple = units // recv_sem.shape[1]
    starts = lambda t: lax.rem(t, couple) == 0
    farthest = lambda side: cols - 1 if side > 0 else 0

    def early_hop(b, side):
        landing, lane = (from_left, 0) if side > 0 else (from_right, 1)
        lanes = pl.ds(pl.multiple_of(b * BLOCK, BLOCK), BLOCK)
        d = farthest(side)
        return remote(
            part.at[d, pl.ds(0, early), :, lanes], landing.at[d, pl.ds(0, early), :, lanes],
            send_sem.at[lane, d], early_recv.at[lane, b], {"col": me + side},
        )

    def hop(d, t, side, to=None):
        landing, lane = (from_left, 0) if side > 0 else (from_right, 1)
        src, dst = part.at[d, pl.ds(t, couple)], landing.at[d, pl.ds(t, couple)]
        to = me + side if to is None else to
        slot = d if side > 0 or recv_sem.shape[0] == cols else jnp.where(d == to, cols, d)
        return remote(src, dst, send_sem.at[lane, d], recv_sem.at[slot, t // couple], {"col": me + side})

    def arrived(d, t, side):
        hop(d, t, side, to=me).wait_recv()

    def sent(src, sem):
        remote(src, src, sem, sem, {"col": me}).wait_send()

    def across(u, step):
        return remote(
            land.at[row, u], land.at[row, u], row_send.at[step - 1], row_recv.at[step - 1, u],
            {"row": lax.rem(row + step, rows)},
        )

    span = row_dev // PIECES
    piece = lambda p: slice(p * span, (p + 1) * span)

    def near_hop(t, p, side):
        landing, d = (from_left, 1) if side > 0 else (from_right, cols - 2)
        return remote(
            part.at[d, t, :, piece(p)], landing.at[d, t, :, piece(p)],
            near_send.at[0], near_recv.at[t - shared, p], {"col": me + side},
        )

    def bit_across(u, step, p):
        here = land.at[row, u, :, piece(p)]
        return remote(
            here, here, row_send.at[step - 1], bit_recv.at[step - 1, u - shared, p],
            {"row": lax.rem(row + step, rows)},
        )

    def give(u):
        there = jnp.where(me == 1, 0, cols - 1)
        return remote(
            s_hbm.at[grp, :, u], cipher.at[grp, :, units + u], s_send.at[0], s_recv.at[u], {"col": there}
        )

    def swap(u):
        here = cipher.at[grp, :, units + u]
        return remote(here, here, y_send.at[0], y_recv.at[u], {"grp": 1 - grp})

    if shared:
        @pl.when(giver)
        def _():
            @pl.loop(0, head)
            def _(u):
                give(u).start()

    far = lambda side: range(cols - 1, 0, -1) if side > 0 else range(cols - 1)
    near = lambda side: (1 if side > 0 else cols - 2) if shared else None

    def product(lt, b):
        found = lax.dot_general(
            lt[...], d_buf[b], (((1,), (1,)), ((), ())), preferred_element_type=jnp.float32
        )
        return found.reshape(-1, units, UNIT, BLOCK)

    def block(b, carry):
        @pl.when(b < blocks)
        def _():
            d_load(b).wait()

            @pl.when(b + AHEAD < blocks)
            def _():
                d_load(b + AHEAD).start()

            lanes = pl.ds(pl.multiple_of(b * BLOCK, BLOCK), BLOCK)
            found = product(lt_outer, b)
            for at, c in enumerate(outer):
                part[c * held : (c + 1) * held, :, :, lanes] = found[at * held : (at + 1) * held]
            if cols > 1:
                for there, side in ((first, 1), (last, -1)):
                    @pl.when(there)
                    def _():
                        early_hop(b, side).start()

        @pl.when(b == blocks)
        def _():
            if cols > 1:
                for there, side in ((first, 1), (last, -1)):
                    @pl.when(there)
                    def _():
                        for t in range(early, ahead_of_rest, couple):
                            hop(farthest(side), t, side).start()

            loads[-1].start()
            for at, c in enumerate(inner):
                turn_over(c, lt_inner, at)

        if inner:
            @pl.when((b >= blocks) & (b < 2 * blocks))
            def _():
                lanes = pl.ds(pl.multiple_of((b - blocks) * BLOCK, BLOCK), BLOCK)
                part[held : cols - held, :, :, lanes] = product(lt_inner, b - blocks)

        for side, hops, landing in ((1, me, from_left), (-1, cols - 1 - me, from_right)):
            c = b - DELAY * hops

            @pl.when(jnp.logical_not(end) & (c >= 0) & (c < blocks))
            def _():
                early_hop(c, side).wait_recv()
                d, lanes = farthest(side), pl.ds(pl.multiple_of(c * BLOCK, BLOCK), BLOCK)
                part[d, 0:early, :, lanes] += landing[d, 0:early, :, lanes]
                early_hop(c, side).start()

        return carry

    follow = jnp.where(end, 0, DELAY * jnp.maximum(me, cols - 1 - me))
    lax.fori_loop(0, blocks + jnp.maximum(follow, blocks), block, 0)

    for there, side in ((first, 1), (last, -1)):
        @pl.when(there)
        def _():
            @pl.loop(min(early, LEAD), units + LEAD * (cols - 1))
            def _(i):
                for d in far(side):
                    if d != near(side):
                        t = i - lag(d, side)

                        @pl.when((t >= (ahead_of_rest if d == farthest(side) else 0)) & (t < units) & starts(t))
                        def _():
                            hop(d, t, side).start()

            if shared:
                @pl.loop(shared, units - 1)
                def _(t):
                    for p in range(PIECES):
                        near_hop(t, p, side).start()

    for load in loads:
        load.wait()

    def pair(m):
        here = land.at[m, final]
        return remote(here, here, pair_send.at[0], pair_recv.at[m], {"col": beside})

    def consume(u, secret):
        real, imag = [], []
        for s in range(slow):
            lanes = slice(s * LANES, (s + 1) * LANES)
            x = [land[m, u, :, lanes] for m in range(rows)]
            real.append(sum(x[m] * table[2 * m + 2, s : s + 1] for m in range(rows)))
            imag.append(sum(x[m] * table[2 * m + 3, s : s + 1] for m in range(rows)))
        real, imag = swap_bits(real), swap_bits(imag)
        both = jnp.concatenate([jnp.concatenate(real, 0), jnp.concatenate(imag, 0)], 1)
        high = both.astype(jnp.bfloat16)
        low = (both - high.astype(jnp.float32)).astype(jnp.bfloat16)
        mixed = jnp.dot(
            jnp.concatenate([high, low, high], 1), w[...], preferred_element_type=jnp.float32
        )
        spread = []
        for s in range(slow):
            r = mixed[s * UNIT : (s + 1) * UNIT, :LANES]
            i = mixed[s * UNIT : (s + 1) * UNIT, LANES:]
            c, n = table[0, s : s + 1], table[1, s : s + 1]
            spread.append((r * c - i * n, r * n + i * c) if s else (r, i))
        for v, (r, i) in enumerate(fft(spread)):
            lanes = slice(v * LANES, (v + 1) * LANES)
            for k in range(2):
                a, b = cipher[k, 0, secret, :, lanes], cipher[k, 1, secret, :, lanes]
                acc[k, 0, :, lanes] += r * a - i * b
                acc[k, 1, :, lanes] += r * b + i * a

    extra = jnp.where(giver, 1, 0) if shared else 0
    late_from = jnp.maximum(units + LEAD, shared + own_hold)

    def place(i):
        k = i - head
        group, r = k // 3, lax.rem(k, 3)
        mixed = jnp.where(r == 2, units + head + group, 2 * group + r)
        at_end = jnp.where(k < 0, units + i, jnp.where(group < shared - head, mixed, i - shared))
        m = i - late_from
        inside = jnp.where(m < 0, i - own_hold, shared + m)
        if late > 1:
            inside = jnp.where(m == late - 2, units - 1, jnp.where(m == late - 1, units - 2, inside))
        if late:
            inside = jnp.where(m == late, final, inside)
        early_ones = (i >= own_hold) & (i < own_hold + units - late)
        busy = jnp.where(
            end, (i >= 0) & (i < shared + units), early_ones | ((m >= 0) & (m < late + extra))
        )
        return busy, jnp.where(end, at_end, inside)

    def in_pieces(u):
        return jnp.logical_not(end) & (u >= shared) & (u < units - 1) if shared else False

    wait = jnp.where(end, END_LAG, LAG)
    rest = jnp.maximum(
        right_hold + LEAD * jnp.maximum(cols - 2 - me, 0), left_hold + LEAD * jnp.maximum(me - 1, 0)
    )
    rest = jnp.maximum(units + rest, own_hold + units - late + LAG)
    if late:
        rest = jnp.maximum(rest, late_from + late + extra + LAG)
    steps = jnp.where(end, shared + units + END_LAG, rest)

    def forward(d, side, i):
        beyond, hold, landing = (
            (d > me, right_hold, from_left) if side > 0 else (d < me, left_hold, from_right)
        )
        t = i - hold - lag(d, side)

        first_one = early if d == farthest(side) else 0

        @pl.when(jnp.logical_not(end) & beyond & (t >= first_one) & (t < units) & starts(t))
        def _():
            arrived(d, t, side)
            part[d, pl.ds(t, couple)] += landing[d, pl.ds(t, couple)]
            hop(d, t, side).start()

    def step_of(i, carry):
        for d in range(cols - 1, 1, -1):
            forward(d, 1, i)
        for d in range(cols - 2):
            forward(d, -1, i)
        if shared > head:
            g = i - HOLD * (cols - 3) - 1

            @pl.when(giver & (g >= 0) & (g < 2 * (shared - head)) & (lax.rem(g, 2) == 0))
            def _():
                give(head + g // 2).start()

        busy, u = place(i)

        if shared:
            @pl.when(end & (i == 0))
            def _():
                land[row, final] = part[beside, units - 1]
                for step in range(1, rows):
                    across(final, step).start()

            @pl.when(end & (i == LAG))
            def _():
                for step in range(1, rows):
                    across(final, step).wait_recv()
                for m in range(rows):
                    pair(m).start()

        @pl.when(busy & (u != final))
        def _():
            lent = u >= units
            d = jnp.where(lent, beside, me)
            t = jnp.where(lent, u - units, u)
            whole_left, whole_right = me > 0, me < cols - 1
            if shared:
                whole_left, whole_right = whole_left & (me != 1), whole_right & (me != cols - 2)

            @pl.when(end & (u == 0) & (cols > 1))
            def _():
                for there, side in ((last, 1), (first, -1)):
                    @pl.when(there)
                    def _():
                        @pl.loop(0, blocks)
                        def _(b):
                            early_hop(b, side).wait_recv()

            awaited, lead = starts(t), t
            if late > 1 and couple > 1:
                awaited = jnp.where(
                    jnp.logical_not(end) & (t >= units - 2), t == units - 1, awaited
                )
                lead = t - lax.rem(t, couple)
            awaited = awaited & jnp.logical_not(end & (t < early))

            @pl.when(whole_left & jnp.logical_not(lent))
            def _():
                @pl.when(awaited)
                def _():
                    arrived(me, lead, 1)

                part[me, t] += from_left[me, t]

            @pl.when(whole_right & jnp.logical_not(lent))
            def _():
                @pl.when(awaited)
                def _():
                    arrived(me, lead, -1)

                part[me, t] += from_right[me, t]

            @pl.when(jnp.logical_not(in_pieces(u)))
            def _():
                land[row, u] = part[d, t]
                for step in range(1, rows):
                    across(u, step).start()

            if shared:
                @pl.when(in_pieces(u))
                def _():
                    for p in range(PIECES):
                        for there, side, landing in ((me == 1, 1, from_left), (me == cols - 2, -1, from_right)):
                            @pl.when(there)
                            def _():
                                near_hop(u, p, side).wait_recv()
                                part[me, u, :, piece(p)] += landing[me, u, :, piece(p)]
                        land[row, u, :, piece(p)] = part[me, u, :, piece(p)]
                        for step in range(1, rows):
                            bit_across(u, step, p).start()

            if shared:
                @pl.when(lent)
                def _():
                    give(t).wait_recv()
                    swap(t).start()

        ready, v = place(i - wait)

        @pl.when(ready)
        def _():
            @pl.when(jnp.logical_not(in_pieces(v)) & (v != final))
            def _():
                for step in range(1, rows):
                    across(v, step).wait_recv()

            if shared:
                @pl.when(in_pieces(v))
                def _():
                    for step in range(1, rows):
                        for p in range(PIECES):
                            bit_across(v, step, p).wait_recv()

                @pl.when((v >= units) & (v != final))
                def _():
                    swap(v - units).wait_recv()

                @pl.when(v == final)
                def _():
                    for m in range(rows):
                        pair(m).wait_recv()
            consume(v, jnp.where(v == final, units - 1, v) if shared else v)

        return carry

    lax.fori_loop(0, steps, step_of, 0)

    width = half_sum.shape[2]
    for k in range(2):
        for p in range(2):
            total = jnp.sum(acc[k, p], axis=0, keepdims=True)
            for q in range(4):
                r = (2 * k + p) * 2 + q % 2
                half_sum[q // 2, r : r + 1, :] = total[:, q * width : (q + 1) * width]
    other = {"limb": 1 - limb}
    trade = remote(half_sum.at[1 - limb], half_in, limb_send.at[0], limb_recv.at[0], other)
    trade.start()
    trade.wait_recv()
    z_in[me] = half_sum[limb] + half_in[...]

    def tell(src, dst):
        return remote(z_in.at[src], z_in.at[src], z_send.at[0], z_recv.at[src], {"col": dst})

    tellers = range(1, cols - 1) if cols > 3 else range(cols)
    ahead = [(me + side * step) for step in range(cols - 1, 0, -1) for side in (1, -1)]
    if cols > 3:
        @pl.when(end)
        def _():
            tell(me, beside).start()

        for there, src in ((me == 1, 0), (me == cols - 2, cols - 1)):
            @pl.when(there)
            def _():
                tell(src, me).wait_recv()
                z_in[me] += z_in[src]

    for dst in ahead:
        @pl.when((jnp.logical_not(end) | (cols <= 3)) & (dst >= 0) & (dst < cols))
        def _():
            tell(me, dst).start()
    for there, side in ((first, 1), (last, -1)):
        @pl.when(there)
        def _():
            lane = 0 if side > 0 else 1
            for d in far(side):
                if d != near(side):
                    sent(part.at[d], send_sem.at[lane, d])
            for step in range(1, rows):
                sent(land.at[row, pl.ds(0, final + 1 if shared else units)], row_send.at[step - 1])
            if shared:
                if units - 1 > shared:
                    sent(part.at[near(side), pl.ds(shared, units - 1 - shared)], near_send.at[0])
                sent(land.at[:, final], pair_send.at[0])
                sent(cipher.at[grp, :, pl.ds(units, shared)], y_send.at[0])

    @pl.when(jnp.logical_not(end))
    def _():
        for d in range(cols - 1, 1, -1):
            @pl.when(d > me)
            def _():
                sent(part.at[d], send_sem.at[0, d])
        for d in range(cols - 2):
            @pl.when(d < me)
            def _():
                sent(part.at[d], send_sem.at[1, d])
        for step in range(1, rows):
            sent(land.at[row, pl.ds(0, units)], row_send.at[step - 1])

    if shared:
        @pl.when(giver)
        def _():
            sent(cipher.at[grp, :, pl.ds(units, shared)], s_send.at[0])

    for src in tellers:
        @pl.when(me != src)
        def _():
            tell(src, me).wait_recv()
    total = z_in[tellers[0]]
    for c in tellers[1:]:
        total = total + z_in[c]
    whole_sum[limb] = total
    gather = remote(whole_sum.at[limb], whole_sum.at[limb], limb_send.at[1], limb_recv.at[1], other)
    gather.start()
    gather.wait_recv()
    for k in range(2):
        for p in range(2):
            for q in range(4):
                r = (2 * k + p) * 2 + q % 2
                out_ref[k, p : p + 1, q * width : (q + 1) * width] = whole_sum[q // 2, r : r + 1, :]

    trade.wait_send()
    gather.wait_send()
    if cols > 3:
        @pl.when(end)
        def _():
            sent(z_in.at[0], z_send.at[0])

        @pl.when(jnp.logical_not(end))
        def _():
            sent(z_in.at[pl.ds(0, cols - 1)], z_send.at[0])
    elif cols > 1:
        sent(z_in.at[pl.ds(0, cols - 1)], z_send.at[0])


def tables(rows, row_dev, half):
    slow = row_dev // LANES
    degree = rows * row_dev
    scale = 1.0 / (math.sqrt(degree) * math.sqrt(2 * half))
    lane = np.arange(LANES)
    at = LANES // slow * (lane % slow) + lane // slow
    n = LANES * np.arange(slow)[:, None] + lane[None, :]
    a, m = np.arange(rows)[:, None, None, None], np.arange(rows)[None, :, None, None]
    turn = -np.pi * ((n + m * row_dev) * (2 * a + 1) % (2 * degree)) / degree
    turn = np.exp(1j * turn) * scale
    turn = np.stack([turn.real, turn.imag], 2).reshape(rows, 2 * rows, slow, LANES)
    twiddle = np.exp(-2j * np.pi * np.arange(slow)[:, None] * lane[None, :] / row_dev)
    twiddle = np.stack([twiddle.real, twiddle.imag], 0)
    twiddle = np.broadcast_to(twiddle, (rows,) + twiddle.shape)
    table = np.concatenate([twiddle, turn], 1).astype(np.float32)
    w = np.exp(-2j * np.pi * (at[:, None] * lane[None, :] % LANES) / LANES)
    w = np.block([[w.real, w.imag], [-w.imag, w.real]]).astype(np.float32)
    high = w.astype(jnp.bfloat16)
    low = (w - high.astype(np.float32)).astype(jnp.bfloat16)
    return table, np.concatenate([high, high, low], 0)


def body(database, lwe_matrix, secret_ct):
    rows, cols = lax.axis_size("row"), lax.axis_size("col")
    grps = lax.axis_size("grp")
    row_dev, depth = database.shape
    half = lwe_matrix.shape[2]
    own = half // cols
    units = own // UNIT
    slow = row_dev // LANES
    shared = units * 10 // 16 if cols > 3 and grps == 2 else 0
    places = units + shared + 1
    blocks = row_dev // BLOCK
    chunks = half // max(own, LANES)
    couple = PAIR if units % PAIR == 0 and EARLY % PAIR == 0 and NEXT % PAIR == 0 else 1
    table, w = tables(rows, row_dev, half)
    dma = pltpu.SemaphoreType.DMA
    flow = pltpu.VMEM((cols, units, UNIT, row_dev), jnp.float32)
    lots = max(shared, 1)
    hbm = pl.BlockSpec(memory_space=pl.ANY)
    return pl.pallas_call(
        functools.partial(kernel, cols, rows, grps, shared),
        out_shape=jax.ShapeDtypeStruct((2, 2, row_dev), jnp.float32),
        in_specs=[hbm] * 5,
        out_specs=pl.BlockSpec(memory_space=pltpu.VMEM),
        scratch_shapes=[
            pltpu.VMEM((depth, half), lwe_matrix.dtype),
            pltpu.VMEM((min(2, chunks) * half // chunks, depth), lwe_matrix.dtype),
            pltpu.VMEM((max(chunks - 2, 1) * half // chunks, depth), lwe_matrix.dtype),
            pltpu.VMEM((blocks, BLOCK, depth), database.dtype),
            flow,
            flow,
            flow,
            pltpu.VMEM((rows, places, UNIT, row_dev), jnp.float32),
            pltpu.VMEM((2, 2, units + shared, UNIT, row_dev), jnp.float32),
            pltpu.VMEM(table.shape[1:], jnp.float32),
            pltpu.VMEM(w.shape, jnp.bfloat16),
            pltpu.VMEM((2, 2, UNIT, row_dev), jnp.float32),
            pltpu.VMEM((2, 8, row_dev // 4), jnp.float32),
            pltpu.VMEM((8, row_dev // 4), jnp.float32),
            pltpu.VMEM((cols, 8, row_dev // 4), jnp.float32),
            pltpu.VMEM((2, 8, row_dev // 4), jnp.float32),
            dma((3,)),
            dma((chunks,)),
            dma((AHEAD,)),
            dma((2, cols)),
            dma((cols if shared and cols == 4 else cols + 1, units // couple)),
            dma((max(rows - 1, 1),)),
            dma((max(rows - 1, 1), places)),
            dma((1,)),
            dma((lots,)),
            dma((1,)),
            dma((lots,)),
            dma((2,)),
            dma((2,)),
            dma((1,)),
            dma((cols,)),
            dma((1,)),
            dma((max(units - 1 - shared, 1), PIECES)),
            dma((max(rows - 1, 1), max(units - 1 - shared, 1), PIECES)),
            dma((1,)),
            dma((rows,)),
            dma((2, blocks)),
        ],
        compiler_params=pltpu.CompilerParams(
            collective_id=0, has_side_effects=True, vmem_limit_bytes=55168 << 10
        ),
    )(
        lwe_matrix[:, 0, :],
        database,
        secret_ct[:, :, 0].reshape(2, 2, units, UNIT, row_dev),
        jnp.asarray(table),
        jnp.asarray(w),
    )


def solution(mesh):
    placed = (P(("grp", "row"), "col"), P("col", "limb", None), P(None, None, "limb", "col", "row"))
    return jax.shard_map(
        body, mesh=mesh, in_specs=placed, out_specs=P("grp", None, "row"), check_vma=False
    )
```

```python
import functools
import math

import jax
import jax.numpy as jnp
import numpy as np
from jax import lax
from jax.experimental import pallas as pl
from jax.experimental.pallas import tpu as pltpu
from jax.sharding import PartitionSpec as P

MESH = pl.DeviceIdType.MESH
UNIT = 8
LANES = 128
BLOCK = 256
LEAD = 4
AHEAD = 4
HEAD = 5
PAIR = 2
EARLY = 4
NEXT = 2
DELAY = 4
PIECES = 2
LAG = 3
END_LAG = 5
HOLD = 3


def fft(values):
    count = len(values)
    if count == 1:
        return values
    even, odd = fft(values[0::2]), fft(values[1::2])
    low, high = [], []
    for k in range(count // 2):
        (er, ei), (r, i) = even[k], odd[k]
        if k == 0:
            tr, ti = r, i
        elif 4 * k == count:
            tr, ti = i, -r
        elif 8 * k == count:
            half = math.sqrt(0.5)
            tr, ti = (r + i) * half, (i - r) * half
        elif 8 * k == 3 * count:
            half = math.sqrt(0.5)
            tr, ti = (i - r) * half, -(r + i) * half
        else:
            c, s = math.cos(2 * math.pi * k / count), math.sin(2 * math.pi * k / count)
            tr, ti = r * c + i * s, i * c - r * s
        low.append((er + tr, ei + ti))
        high.append((er - tr, ei - ti))
    return low + high


def swap_bits(blocks):
    blocks = list(blocks)
    lane = lax.broadcasted_iota(jnp.int32, blocks[0].shape, 1)
    step = 1
    while step < len(blocks):
        clear = (lane & step) == 0
        for b in range(len(blocks)):
            if not b & step:
                x, y = blocks[b], blocks[b + step]
                blocks[b] = jnp.where(clear, x, pltpu.roll(y, step, 1))
                blocks[b + step] = jnp.where(clear, pltpu.roll(x, LANES - step, 1), y)
        step *= 2
    return blocks


def kernel(cols, rows, grps, shared, l_hbm, d_hbm, s_hbm, table_hbm, w_hbm, out_ref,
           l_buf, lt_outer, lt_inner, d_buf, part, from_left, from_right, land, cipher, table, w, acc,
           half_sum, half_in, z_in, whole_sum,
           load_sem, l_sem, d_sem, send_sem, recv_sem, row_send, row_recv, s_send, s_recv, y_send, y_recv,
           limb_send, limb_recv, z_send, z_recv, near_send, near_recv, bit_recv, pair_send, pair_recv, early_recv):
    me, row = lax.axis_index("col"), lax.axis_index("row")
    grp, limb = lax.axis_index("grp"), lax.axis_index("limb")
    units, row_dev = part.shape[1], part.shape[3]
    slow = row_dev // LANES
    blocks = d_buf.shape[0]
    first, last = me == 0, me == cols - 1
    end = first | last
    beside = jnp.where(first, 1, cols - 2)
    giver = ((me == 1) | (me == cols - 2)) if shared else None
    head = max(min(HEAD, shared), shared - units // 2)
    late = units - shared if shared else 0
    right_hold = HOLD * jnp.maximum(me - 1, 0)
    left_hold = HOLD * jnp.maximum(cols - 2 - me, 0)
    lag = lambda d, side: LEAD * (cols - 1 - d) if side > 0 else LEAD * d
    by_left, by_right = right_hold + lag(me, 1), left_hold + lag(me, -1)
    if shared:
        by_left, by_right = jnp.where(me == 1, 0, by_left), jnp.where(me == cols - 2, 0, by_right)
    own_hold = jnp.where(end, 0, jnp.maximum(by_left, by_right))
    final = units + shared

    loads = [
        pltpu.make_async_copy(table_hbm.at[row], table, load_sem.at[0]),
        pltpu.make_async_copy(w_hbm, w, load_sem.at[1]),
        pltpu.make_async_copy(s_hbm, cipher.at[:, :, pl.ds(0, units)], load_sem.at[2]),
    ]
    chunks = l_sem.shape[0]
    chunk = l_buf.shape[1] // chunks
    outer = [0, chunks - 1] if chunks > 1 else [0]
    inner = list(range(1, chunks - 1))
    held = chunk * cols // l_buf.shape[1]

    def l_load(c):
        there = pl.ds(c * chunk, chunk)
        return pltpu.make_async_copy(l_hbm.at[:, there], l_buf.at[:, there], l_sem.at[c])

    def turn_over(c, lt, at):
        l_load(c).wait()
        lt[at * chunk : (at + 1) * chunk, :] = l_buf[:, c * chunk : (c + 1) * chunk].T

    def d_load(b):
        return pltpu.make_async_copy(
            d_hbm.at[pl.ds(b * BLOCK, BLOCK)], d_buf.at[b], d_sem.at[lax.rem(b, AHEAD)]
        )

    for c in outer:
        l_load(c).start()
    for b in range(min(AHEAD, blocks)):
        d_load(b).start()
    for c in inner:
        l_load(c).start()
    for load in loads[:-1]:
        load.start()

    barrier = pltpu.get_barrier_semaphore()
    greeted = 0
    peers = [{"row": lax.rem(row + step, rows)} for step in range(1, rows)]
    peers += [{"limb": 1 - limb}]
    if shared:
        peers += [{"grp": 1 - grp}]
    for peer in peers:
        pl.semaphore_signal(barrier, inc=1, device_id=peer, device_id_type=MESH)
        greeted += 1
    for there, side in ((me > 0, -1), (me < cols - 1, 1)):
        @pl.when(there)
        def _():
            pl.semaphore_signal(barrier, inc=1, device_id={"col": me + side}, device_id_type=MESH)

    acc[...] = jnp.zeros_like(acc)
    for at, c in enumerate(outer):
        turn_over(c, lt_outer, at)

    @pl.when(end)
    def _():
        pl.semaphore_wait(barrier, greeted + min(cols - 1, 1))

    @pl.when(jnp.logical_not(end))
    def _():
        pl.semaphore_wait(barrier, greeted + 2)

    def remote(src, dst, send, recv, where):
        return pltpu.make_async_remote_copy(
            src_ref=src, dst_ref=dst, send_sem=send, recv_sem=recv, device_id=where, device_id_type=MESH
        )

    early, ahead_of_rest = min(EARLY, units), min(EARLY + NEXT, units)
    couple = units // recv_sem.shape[1]
    starts = lambda t: lax.rem(t, couple) == 0
    farthest = lambda side: cols - 1 if side > 0 else 0

    def early_hop(b, side):
        landing, lane = (from_left, 0) if side > 0 else (from_right, 1)
        lanes = pl.ds(pl.multiple_of(b * BLOCK, BLOCK), BLOCK)
        d = farthest(side)
        return remote(
            part.at[d, pl.ds(0, early), :, lanes], landing.at[d, pl.ds(0, early), :, lanes],
            send_sem.at[lane, d], early_recv.at[lane, b], {"col": me + side},
        )

    def hop(d, t, side, to=None):
        landing, lane = (from_left, 0) if side > 0 else (from_right, 1)
        src, dst = part.at[d, pl.ds(t, couple)], landing.at[d, pl.ds(t, couple)]
        to = me + side if to is None else to
        slot = d if side > 0 or recv_sem.shape[0] == cols else jnp.where(d == to, cols, d)
        return remote(src, dst, send_sem.at[lane, d], recv_sem.at[slot, t // couple], {"col": me + side})

    def arrived(d, t, side):
        hop(d, t, side, to=me).wait_recv()

    def sent(src, sem):
        remote(src, src, sem, sem, {"col": me}).wait_send()

    def across(u, step):
        return remote(
            land.at[row, u], land.at[row, u], row_send.at[step - 1], row_recv.at[step - 1, u],
            {"row": lax.rem(row + step, rows)},
        )

    span = row_dev // PIECES
    piece = lambda p: slice(p * span, (p + 1) * span)

    def near_hop(t, p, side):
        landing, d = (from_left, 1) if side > 0 else (from_right, cols - 2)
        return remote(
            part.at[d, t, :, piece(p)], landing.at[d, t, :, piece(p)],
            near_send.at[0], near_recv.at[t - shared, p], {"col": me + side},
        )

    def bit_across(u, step, p):
        here = land.at[row, u, :, piece(p)]
        return remote(
            here, here, row_send.at[step - 1], bit_recv.at[step - 1, u - shared, p],
            {"row": lax.rem(row + step, rows)},
        )

    def give(u):
        there = jnp.where(me == 1, 0, cols - 1)
        return remote(
            s_hbm.at[grp, :, u], cipher.at[grp, :, units + u], s_send.at[0], s_recv.at[u], {"col": there}
        )

    def swap(u):
        here = cipher.at[grp, :, units + u]
        return remote(here, here, y_send.at[0], y_recv.at[u], {"grp": 1 - grp})

    if shared:
        @pl.when(giver)
        def _():
            @pl.loop(0, head)
            def _(u):
                give(u).start()

    far = lambda side: range(cols - 1, 0, -1) if side > 0 else range(cols - 1)
    near = lambda side: (1 if side > 0 else cols - 2) if shared else None

    def product(lt, b):
        found = lax.dot_general(
            lt[...], d_buf[b], (((1,), (1,)), ((), ())), preferred_element_type=jnp.float32
        )
        return found.reshape(-1, units, UNIT, BLOCK)

    def block(b, carry):
        @pl.when(b < blocks)
        def _():
            d_load(b).wait()

            @pl.when(b + AHEAD < blocks)
            def _():
                d_load(b + AHEAD).start()

            lanes = pl.ds(pl.multiple_of(b * BLOCK, BLOCK), BLOCK)
            found = product(lt_outer, b)
            for at, c in enumerate(outer):
                part[c * held : (c + 1) * held, :, :, lanes] = found[at * held : (at + 1) * held]
            if cols > 1:
                for there, side in ((first, 1), (last, -1)):
                    @pl.when(there)
                    def _():
                        early_hop(b, side).start()

        @pl.when(b == blocks)
        def _():
            if cols > 1:
                for there, side in ((first, 1), (last, -1)):
                    @pl.when(there)
                    def _():
                        for t in range(early, ahead_of_rest, couple):
                            hop(farthest(side), t, side).start()

            loads[-1].start()
            for at, c in enumerate(inner):
                turn_over(c, lt_inner, at)

        if inner:
            @pl.when((b >= blocks) & (b < 2 * blocks))
            def _():
                lanes = pl.ds(pl.multiple_of((b - blocks) * BLOCK, BLOCK), BLOCK)
                part[held : cols - held, :, :, lanes] = product(lt_inner, b - blocks)

        for side, hops, landing in ((1, me, from_left), (-1, cols - 1 - me, from_right)):
            c = b - DELAY * hops

            @pl.when(jnp.logical_not(end) & (c >= 0) & (c < blocks))
            def _():
                early_hop(c, side).wait_recv()
                d, lanes = farthest(side), pl.ds(pl.multiple_of(c * BLOCK, BLOCK), BLOCK)
                part[d, 0:early, :, lanes] += landing[d, 0:early, :, lanes]
                early_hop(c, side).start()

        return carry

    follow = jnp.where(end, 0, DELAY * jnp.maximum(me, cols - 1 - me))
    lax.fori_loop(0, blocks + jnp.maximum(follow, blocks), block, 0)

    for there, side in ((first, 1), (last, -1)):
        @pl.when(there)
        def _():
            @pl.loop(min(early, LEAD), units + LEAD * (cols - 1))
            def _(i):
                for d in far(side):
                    if d != near(side):
                        t = i - lag(d, side)

                        @pl.when((t >= (ahead_of_rest if d == farthest(side) else 0)) & (t < units) & starts(t))
                        def _():
                            hop(d, t, side).start()

            if shared:
                @pl.loop(shared, units - 1)
                def _(t):
                    for p in range(PIECES):
                        near_hop(t, p, side).start()

    for load in loads:
        load.wait()

    def pair(m):
        here = land.at[m, final]
        return remote(here, here, pair_send.at[0], pair_recv.at[m], {"col": beside})

    def consume(u, secret):
        real, imag = [], []
        for s in range(slow):
            lanes = slice(s * LANES, (s + 1) * LANES)
            x = [land[m, u, :, lanes] for m in range(rows)]
            real.append(sum(x[m] * table[2 * m + 2, s : s + 1] for m in range(rows)))
            imag.append(sum(x[m] * table[2 * m + 3, s : s + 1] for m in range(rows)))
        real, imag = swap_bits(real), swap_bits(imag)
        both = jnp.concatenate([jnp.concatenate(real, 0), jnp.concatenate(imag, 0)], 1)
        high = both.astype(jnp.bfloat16)
        low = (both - high.astype(jnp.float32)).astype(jnp.bfloat16)
        mixed = jnp.dot(
            jnp.concatenate([high, low, high], 1), w[...], preferred_element_type=jnp.float32
        )
        spread = []
        for s in range(slow):
            r = mixed[s * UNIT : (s + 1) * UNIT, :LANES]
            i = mixed[s * UNIT : (s + 1) * UNIT, LANES:]
            c, n = table[0, s : s + 1], table[1, s : s + 1]
            spread.append((r * c - i * n, r * n + i * c) if s else (r, i))
        for v, (r, i) in enumerate(fft(spread)):
            lanes = slice(v * LANES, (v + 1) * LANES)
            for k in range(2):
                a, b = cipher[k, 0, secret, :, lanes], cipher[k, 1, secret, :, lanes]
                acc[k, 0, :, lanes] += r * a - i * b
                acc[k, 1, :, lanes] += r * b + i * a

    extra = jnp.where(giver, 1, 0) if shared else 0
    late_from = jnp.maximum(units + LEAD - 2, shared + own_hold)

    def place(i):
        k = i - head
        group, r = k // 3, lax.rem(k, 3)
        mixed = jnp.where(r == 2, units + head + group, 2 * group + r)
        at_end = jnp.where(k < 0, units + i, jnp.where(group < shared - head, mixed, i - shared))
        m = i - late_from
        inside = jnp.where(m < 0, i - own_hold, shared + m)
        if late > 1:
            inside = jnp.where(m == late - 2, units - 1, jnp.where(m == late - 1, units - 2, inside))
        if late:
            inside = jnp.where(m == late, final, inside)
        early_ones = (i >= own_hold) & (i < own_hold + units - late)
        busy = jnp.where(
            end, (i >= 0) & (i < shared + units), early_ones | ((m >= 0) & (m < late + extra))
        )
        return busy, jnp.where(end, at_end, inside)

    def in_pieces(u):
        return jnp.logical_not(end) & (u >= shared) & (u < units - 1) if shared else False

    wait = jnp.where(end, END_LAG, LAG)
    rest = jnp.maximum(
        right_hold + LEAD * jnp.maximum(cols - 2 - me, 0), left_hold + LEAD * jnp.maximum(me - 1, 0)
    )
    rest = jnp.maximum(units + rest, own_hold + units - late + LAG)
    if late:
        rest = jnp.maximum(rest, late_from + late + extra + LAG)
    steps = jnp.where(end, shared + units + END_LAG, rest)

    def forward(d, side, i):
        beyond, hold, landing = (
            (d > me, right_hold, from_left) if side > 0 else (d < me, left_hold, from_right)
        )
        t = i - hold - lag(d, side)

        first_one = early if d == farthest(side) else 0

        @pl.when(jnp.logical_not(end) & beyond & (t >= first_one) & (t < units) & starts(t))
        def _():
            arrived(d, t, side)
            part[d, pl.ds(t, couple)] += landing[d, pl.ds(t, couple)]
            hop(d, t, side).start()

    def step_of(i, carry):
        for d in range(cols - 1, 1, -1):
            forward(d, 1, i)
        for d in range(cols - 2):
            forward(d, -1, i)
        if shared > head:
            g = i - HOLD * (cols - 3) - 1

            @pl.when(giver & (g >= 0) & (g < 2 * (shared - head)) & (lax.rem(g, 2) == 0))
            def _():
                give(head + g // 2).start()

        busy, u = place(i)

        if shared:
            @pl.when(end & (i == 0))
            def _():
                land[row, final] = part[beside, units - 1]
                for step in range(1, rows):
                    across(final, step).start()

            @pl.when(end & (i == LAG))
            def _():
                for step in range(1, rows):
                    across(final, step).wait_recv()
                for m in range(rows):
                    pair(m).start()

        @pl.when(busy & (u != final))
        def _():
            lent = u >= units
            d = jnp.where(lent, beside, me)
            t = jnp.where(lent, u - units, u)
            whole_left, whole_right = me > 0, me < cols - 1
            if shared:
                whole_left, whole_right = whole_left & (me != 1), whole_right & (me != cols - 2)

            @pl.when(end & (u == 0) & (cols > 1))
            def _():
                for there, side in ((last, 1), (first, -1)):
                    @pl.when(there)
                    def _():
                        @pl.loop(0, blocks)
                        def _(b):
                            early_hop(b, side).wait_recv()

            awaited, lead = starts(t), t
            if late > 1 and couple > 1:
                awaited = jnp.where(
                    jnp.logical_not(end) & (t >= units - 2), t == units - 1, awaited
                )
                lead = t - lax.rem(t, couple)
            awaited = awaited & jnp.logical_not(end & (t < early))

            @pl.when(whole_left & jnp.logical_not(lent))
            def _():
                @pl.when(awaited)
                def _():
                    arrived(me, lead, 1)

                part[me, t] += from_left[me, t]

            @pl.when(whole_right & jnp.logical_not(lent))
            def _():
                @pl.when(awaited)
                def _():
                    arrived(me, lead, -1)

                part[me, t] += from_right[me, t]

            @pl.when(jnp.logical_not(in_pieces(u)))
            def _():
                land[row, u] = part[d, t]
                for step in range(1, rows):
                    across(u, step).start()

            if shared:
                @pl.when(in_pieces(u))
                def _():
                    for p in range(PIECES):
                        for there, side, landing in ((me == 1, 1, from_left), (me == cols - 2, -1, from_right)):
                            @pl.when(there)
                            def _():
                                near_hop(u, p, side).wait_recv()
                                part[me, u, :, piece(p)] += landing[me, u, :, piece(p)]
                        land[row, u, :, piece(p)] = part[me, u, :, piece(p)]
                        for step in range(1, rows):
                            bit_across(u, step, p).start()

            if shared:
                @pl.when(lent)
                def _():
                    give(t).wait_recv()
                    swap(t).start()

        ready, v = place(i - wait)

        @pl.when(ready)
        def _():
            @pl.when(jnp.logical_not(in_pieces(v)) & (v != final))
            def _():
                for step in range(1, rows):
                    across(v, step).wait_recv()

            if shared:
                @pl.when(in_pieces(v))
                def _():
                    for step in range(1, rows):
                        for p in range(PIECES):
                            bit_across(v, step, p).wait_recv()

                @pl.when((v >= units) & (v != final))
                def _():
                    swap(v - units).wait_recv()

                @pl.when(v == final)
                def _():
                    for m in range(rows):
                        pair(m).wait_recv()
            consume(v, jnp.where(v == final, units - 1, v) if shared else v)

        return carry

    lax.fori_loop(0, steps, step_of, 0)

    width = half_sum.shape[2]
    for k in range(2):
        for p in range(2):
            total = jnp.sum(acc[k, p], axis=0, keepdims=True)
            for q in range(4):
                r = (2 * k + p) * 2 + q % 2
                half_sum[q // 2, r : r + 1, :] = total[:, q * width : (q + 1) * width]
    other = {"limb": 1 - limb}
    trade = remote(half_sum.at[1 - limb], half_in, limb_send.at[0], limb_recv.at[0], other)
    trade.start()
    trade.wait_recv()
    z_in[me] = half_sum[limb] + half_in[...]

    def tell(src, dst):
        return remote(z_in.at[src], z_in.at[src], z_send.at[0], z_recv.at[src], {"col": dst})

    tellers = range(1, cols - 1) if cols > 3 else range(cols)
    ahead = [(me + side * step) for step in range(cols - 1, 0, -1) for side in (1, -1)]
    if cols > 3:
        @pl.when(end)
        def _():
            tell(me, beside).start()

        for there, src in ((me == 1, 0), (me == cols - 2, cols - 1)):
            @pl.when(there)
            def _():
                tell(src, me).wait_recv()
                z_in[me] += z_in[src]

    for dst in ahead:
        @pl.when((jnp.logical_not(end) | (cols <= 3)) & (dst >= 0) & (dst < cols))
        def _():
            tell(me, dst).start()
    for there, side in ((first, 1), (last, -1)):
        @pl.when(there)
        def _():
            lane = 0 if side > 0 else 1
            for d in far(side):
                if d != near(side):
                    sent(part.at[d], send_sem.at[lane, d])
            for step in range(1, rows):
                sent(land.at[row, pl.ds(0, final + 1 if shared else units)], row_send.at[step - 1])
            if shared:
                if units - 1 > shared:
                    sent(part.at[near(side), pl.ds(shared, units - 1 - shared)], near_send.at[0])
                sent(land.at[:, final], pair_send.at[0])
                sent(cipher.at[grp, :, pl.ds(units, shared)], y_send.at[0])

    @pl.when(jnp.logical_not(end))
    def _():
        for d in range(cols - 1, 1, -1):
            @pl.when(d > me)
            def _():
                sent(part.at[d], send_sem.at[0, d])
        for d in range(cols - 2):
            @pl.when(d < me)
            def _():
                sent(part.at[d], send_sem.at[1, d])
        for step in range(1, rows):
            sent(land.at[row, pl.ds(0, units)], row_send.at[step - 1])

    if shared:
        @pl.when(giver)
        def _():
            sent(cipher.at[grp, :, pl.ds(units, shared)], s_send.at[0])

    for src in tellers:
        @pl.when(me != src)
        def _():
            tell(src, me).wait_recv()
    total = z_in[tellers[0]]
    for c in tellers[1:]:
        total = total + z_in[c]
    whole_sum[limb] = total
    gather = remote(whole_sum.at[limb], whole_sum.at[limb], limb_send.at[1], limb_recv.at[1], other)
    gather.start()
    gather.wait_recv()
    for k in range(2):
        for p in range(2):
            for q in range(4):
                r = (2 * k + p) * 2 + q % 2
                out_ref[k, p : p + 1, q * width : (q + 1) * width] = whole_sum[q // 2, r : r + 1, :]

    trade.wait_send()
    gather.wait_send()
    if cols > 3:
        @pl.when(end)
        def _():
            sent(z_in.at[0], z_send.at[0])

        @pl.when(jnp.logical_not(end))
        def _():
            sent(z_in.at[pl.ds(0, cols - 1)], z_send.at[0])
    elif cols > 1:
        sent(z_in.at[pl.ds(0, cols - 1)], z_send.at[0])


def tables(rows, row_dev, half):
    slow = row_dev // LANES
    degree = rows * row_dev
    scale = 1.0 / (math.sqrt(degree) * math.sqrt(2 * half))
    lane = np.arange(LANES)
    at = LANES // slow * (lane % slow) + lane // slow
    n = LANES * np.arange(slow)[:, None] + lane[None, :]
    a, m = np.arange(rows)[:, None, None, None], np.arange(rows)[None, :, None, None]
    turn = -np.pi * ((n + m * row_dev) * (2 * a + 1) % (2 * degree)) / degree
    turn = np.exp(1j * turn) * scale
    turn = np.stack([turn.real, turn.imag], 2).reshape(rows, 2 * rows, slow, LANES)
    twiddle = np.exp(-2j * np.pi * np.arange(slow)[:, None] * lane[None, :] / row_dev)
    twiddle = np.stack([twiddle.real, twiddle.imag], 0)
    twiddle = np.broadcast_to(twiddle, (rows,) + twiddle.shape)
    table = np.concatenate([twiddle, turn], 1).astype(np.float32)
    w = np.exp(-2j * np.pi * (at[:, None] * lane[None, :] % LANES) / LANES)
    w = np.block([[w.real, w.imag], [-w.imag, w.real]]).astype(np.float32)
    high = w.astype(jnp.bfloat16)
    low = (w - high.astype(np.float32)).astype(jnp.bfloat16)
    return table, np.concatenate([high, high, low], 0)


def body(database, lwe_matrix, secret_ct):
    rows, cols = lax.axis_size("row"), lax.axis_size("col")
    grps = lax.axis_size("grp")
    row_dev, depth = database.shape
    half = lwe_matrix.shape[2]
    own = half // cols
    units = own // UNIT
    slow = row_dev // LANES
    shared = units * 10 // 16 if cols > 3 and grps == 2 else 0
    places = units + shared + 1
    blocks = row_dev // BLOCK
    chunks = half // max(own, LANES)
    couple = PAIR if units % PAIR == 0 and EARLY % PAIR == 0 and NEXT % PAIR == 0 else 1
    table, w = tables(rows, row_dev, half)
    dma = pltpu.SemaphoreType.DMA
    flow = pltpu.VMEM((cols, units, UNIT, row_dev), jnp.float32)
    lots = max(shared, 1)
    hbm = pl.BlockSpec(memory_space=pl.ANY)
    return pl.pallas_call(
        functools.partial(kernel, cols, rows, grps, shared),
        out_shape=jax.ShapeDtypeStruct((2, 2, row_dev), jnp.float32),
        in_specs=[hbm] * 5,
        out_specs=pl.BlockSpec(memory_space=pltpu.VMEM),
        scratch_shapes=[
            pltpu.VMEM((depth, half), lwe_matrix.dtype),
            pltpu.VMEM((min(2, chunks) * half // chunks, depth), lwe_matrix.dtype),
            pltpu.VMEM((max(chunks - 2, 1) * half // chunks, depth), lwe_matrix.dtype),
            pltpu.VMEM((blocks, BLOCK, depth), database.dtype),
            flow,
            flow,
            flow,
            pltpu.VMEM((rows, places, UNIT, row_dev), jnp.float32),
            pltpu.VMEM((2, 2, units + shared, UNIT, row_dev), jnp.float32),
            pltpu.VMEM(table.shape[1:], jnp.float32),
            pltpu.VMEM(w.shape, jnp.bfloat16),
            pltpu.VMEM((2, 2, UNIT, row_dev), jnp.float32),
            pltpu.VMEM((2, 8, row_dev // 4), jnp.float32),
            pltpu.VMEM((8, row_dev // 4), jnp.float32),
            pltpu.VMEM((cols, 8, row_dev // 4), jnp.float32),
            pltpu.VMEM((2, 8, row_dev // 4), jnp.float32),
            dma((3,)),
            dma((chunks,)),
            dma((AHEAD,)),
            dma((2, cols)),
            dma((cols if shared and cols == 4 else cols + 1, units // couple)),
            dma((max(rows - 1, 1),)),
            dma((max(rows - 1, 1), places)),
            dma((1,)),
            dma((lots,)),
            dma((1,)),
            dma((lots,)),
            dma((2,)),
            dma((2,)),
            dma((1,)),
            dma((cols,)),
            dma((1,)),
            dma((max(units - 1 - shared, 1), PIECES)),
            dma((max(rows - 1, 1), max(units - 1 - shared, 1), PIECES)),
            dma((1,)),
            dma((rows,)),
            dma((2, blocks)),
        ],
        compiler_params=pltpu.CompilerParams(
            collective_id=0, has_side_effects=True, vmem_limit_bytes=55168 << 10
        ),
    )(
        lwe_matrix[:, 0, :],
        database,
        secret_ct[:, :, 0].reshape(2, 2, units, UNIT, row_dev),
        jnp.asarray(table),
        jnp.asarray(w),
    )


def solution(mesh):
    placed = (P(("grp", "row"), "col"), P("col", "limb", None), P(None, None, "limb", "col", "row"))
    return jax.shard_map(
        body, mesh=mesh, in_specs=placed, out_specs=P("grp", None, "row"), check_vma=False
    )
```

```python
import functools
import math

import jax
import jax.numpy as jnp
import numpy as np
from jax import lax
from jax.experimental import pallas as pl
from jax.experimental.pallas import tpu as pltpu
from jax.sharding import PartitionSpec as P

MESH = pl.DeviceIdType.MESH
UNIT = 8
LANES = 128
BLOCK = 256
LEAD = 6
AHEAD = 4
HEAD = 5
PAIR = 2
EARLY = 6
NEXT = 0
DELAY = 4
PIECES = 2
LAG = 3
END_LAG = 5
HOLD = 3


def fft(values):
    count = len(values)
    if count == 1:
        return values
    even, odd = fft(values[0::2]), fft(values[1::2])
    low, high = [], []
    for k in range(count // 2):
        (er, ei), (r, i) = even[k], odd[k]
        if k == 0:
            tr, ti = r, i
        elif 4 * k == count:
            tr, ti = i, -r
        elif 8 * k == count:
            half = math.sqrt(0.5)
            tr, ti = (r + i) * half, (i - r) * half
        elif 8 * k == 3 * count:
            half = math.sqrt(0.5)
            tr, ti = (i - r) * half, -(r + i) * half
        else:
            c, s = math.cos(2 * math.pi * k / count), math.sin(2 * math.pi * k / count)
            tr, ti = r * c + i * s, i * c - r * s
        low.append((er + tr, ei + ti))
        high.append((er - tr, ei - ti))
    return low + high


def swap_bits(blocks):
    blocks = list(blocks)
    lane = lax.broadcasted_iota(jnp.int32, blocks[0].shape, 1)
    step = 1
    while step < len(blocks):
        clear = (lane & step) == 0
        for b in range(len(blocks)):
            if not b & step:
                x, y = blocks[b], blocks[b + step]
                blocks[b] = jnp.where(clear, x, pltpu.roll(y, step, 1))
                blocks[b + step] = jnp.where(clear, pltpu.roll(x, LANES - step, 1), y)
        step *= 2
    return blocks


def kernel(cols, rows, grps, shared, l_hbm, d_hbm, s_hbm, table_hbm, w_hbm, out_ref,
           l_buf, lt_outer, lt_inner, d_buf, part, from_left, from_right, land, cipher, table, w, acc,
           half_sum, half_in, z_in, whole_sum,
           load_sem, l_sem, d_sem, send_sem, recv_sem, row_send, row_recv, s_send, y_send,
           limb_send, limb_recv, z_send, z_recv, near_send, near_recv, bit_recv, pair_send, pair_recv, early_recv):
    me, row = lax.axis_index("col"), lax.axis_index("row")
    grp, limb = lax.axis_index("grp"), lax.axis_index("limb")
    units, row_dev = part.shape[1], part.shape[3]
    slow = row_dev // LANES
    blocks = d_buf.shape[0]
    first, last = me == 0, me == cols - 1
    end = first | last
    beside = jnp.where(first, 1, cols - 2)
    giver = ((me == 1) | (me == cols - 2)) if shared else None
    head = max(min(HEAD, shared), shared - units // 2)
    late = units - shared if shared else 0
    right_hold = HOLD * jnp.maximum(me - 1, 0)
    left_hold = HOLD * jnp.maximum(cols - 2 - me, 0)
    lag = lambda d, side: LEAD * (cols - 1 - d) if side > 0 else LEAD * d
    by_left, by_right = right_hold + lag(me, 1), left_hold + lag(me, -1)
    if shared:
        by_left, by_right = jnp.where(me == 1, 0, by_left), jnp.where(me == cols - 2, 0, by_right)
    own_hold = jnp.where(end, 0, jnp.maximum(by_left, by_right))
    final = units + shared

    loads = [
        pltpu.make_async_copy(table_hbm.at[row], table, load_sem.at[0]),
        pltpu.make_async_copy(w_hbm, w, load_sem.at[1]),
        pltpu.make_async_copy(s_hbm, cipher.at[:, :, pl.ds(0, units)], load_sem.at[2]),
    ]
    chunks = l_sem.shape[0]
    chunk = l_buf.shape[1] // chunks
    outer = [0, chunks - 1] if chunks > 1 else [0]
    inner = list(range(1, chunks - 1))
    held = chunk * cols // l_buf.shape[1]

    def l_load(c):
        there = pl.ds(c * chunk, chunk)
        return pltpu.make_async_copy(l_hbm.at[:, there], l_buf.at[:, there], l_sem.at[c])

    def turn_over(c, lt, at):
        l_load(c).wait()
        lt[at * chunk : (at + 1) * chunk, :] = l_buf[:, c * chunk : (c + 1) * chunk].T

    def d_load(b):
        return pltpu.make_async_copy(
            d_hbm.at[pl.ds(b * BLOCK, BLOCK)], d_buf.at[b], d_sem.at[lax.rem(b, AHEAD)]
        )

    for c in outer:
        l_load(c).start()
    for b in range(min(AHEAD, blocks)):
        d_load(b).start()
    for c in inner:
        l_load(c).start()
    for load in loads[:-1]:
        load.start()

    barrier = pltpu.get_barrier_semaphore()
    greeted = 0
    peers = [{"row": lax.rem(row + step, rows)} for step in range(1, rows)]
    peers += [{"limb": 1 - limb}]
    if shared:
        peers += [{"grp": 1 - grp}]
    for peer in peers:
        pl.semaphore_signal(barrier, inc=1, device_id=peer, device_id_type=MESH)
        greeted += 1
    for there, side in ((me > 0, -1), (me < cols - 1, 1)):
        @pl.when(there)
        def _():
            pl.semaphore_signal(barrier, inc=1, device_id={"col": me + side}, device_id_type=MESH)

    acc[...] = jnp.zeros_like(acc)
    for at, c in enumerate(outer):
        turn_over(c, lt_outer, at)

    @pl.when(end)
    def _():
        pl.semaphore_wait(barrier, greeted + min(cols - 1, 1))

    @pl.when(jnp.logical_not(end))
    def _():
        pl.semaphore_wait(barrier, greeted + 2)

    def remote(src, dst, send, recv, where):
        return pltpu.make_async_remote_copy(
            src_ref=src, dst_ref=dst, send_sem=send, recv_sem=recv, device_id=where, device_id_type=MESH
        )

    early, ahead_of_rest = min(EARLY, units), min(EARLY + NEXT, units)
    couple = units // recv_sem.shape[1]
    starts = lambda t: lax.rem(t, couple) == 0
    farthest = lambda side: cols - 1 if side > 0 else 0

    def early_hop(b, side):
        landing, lane = (from_left, 0) if side > 0 else (from_right, 1)
        lanes = pl.ds(pl.multiple_of(b * BLOCK, BLOCK), BLOCK)
        d = farthest(side)
        return remote(
            part.at[d, pl.ds(0, early), :, lanes], landing.at[d, pl.ds(0, early), :, lanes],
            send_sem.at[lane, d], early_recv.at[lane, b], {"col": me + side},
        )

    def hop(d, t, side, to=None):
        landing, lane = (from_left, 0) if side > 0 else (from_right, 1)
        src, dst = part.at[d, pl.ds(t, couple)], landing.at[d, pl.ds(t, couple)]
        to = me + side if to is None else to
        slot = d if side > 0 or recv_sem.shape[0] == cols else jnp.where(d == to, cols, d)
        return remote(src, dst, send_sem.at[lane, d], recv_sem.at[slot, t // couple], {"col": me + side})

    def arrived(d, t, side):
        hop(d, t, side, to=me).wait_recv()

    def sent(src, sem):
        remote(src, src, sem, sem, {"col": me}).wait_send()

    def across(u, step):
        return remote(
            land.at[row, u], land.at[row, u], row_send.at[step - 1], row_recv.at[step - 1, u],
            {"row": lax.rem(row + step, rows)},
        )

    span = row_dev // PIECES
    piece = lambda p: slice(p * span, (p + 1) * span)

    def near_hop(t, p, side):
        landing, d = (from_left, 1) if side > 0 else (from_right, cols - 2)
        return remote(
            part.at[d, t, :, piece(p)], landing.at[d, t, :, piece(p)],
            near_send.at[0], near_recv.at[t - shared, p], {"col": me + side},
        )

    def bit_across(u, step, p):
        here = land.at[row, u, :, piece(p)]
        return remote(
            here, here, row_send.at[step - 1], bit_recv.at[step - 1, u - shared, p],
            {"row": lax.rem(row + step, rows)},
        )

    def give(u):
        there = jnp.where(me == 1, 0, cols - 1)
        return remote(
            s_hbm.at[grp, :, u], cipher.at[grp, :, units + u], s_send.at[0], near_recv.at[u // PIECES, lax.rem(u, PIECES)], {"col": there}
        )

    def swap(u):
        here = cipher.at[grp, :, units + u]
        return remote(here, here, y_send.at[0], bit_recv.at[0, u // PIECES, lax.rem(u, PIECES)], {"grp": 1 - grp})

    if shared:
        @pl.when(giver)
        def _():
            @pl.loop(0, head)
            def _(u):
                give(u).start()

    far = lambda side: range(cols - 1, 0, -1) if side > 0 else range(cols - 1)
    near = lambda side: (1 if side > 0 else cols - 2) if shared else None

    def product(lt, b):
        found = lax.dot_general(
            lt[...], d_buf[b], (((1,), (1,)), ((), ())), preferred_element_type=jnp.float32
        )
        return found.reshape(-1, units, UNIT, BLOCK)

    def block(b, carry):
        @pl.when(b < blocks)
        def _():
            d_load(b).wait()

            @pl.when(b + AHEAD < blocks)
            def _():
                d_load(b + AHEAD).start()

            lanes = pl.ds(pl.multiple_of(b * BLOCK, BLOCK), BLOCK)
            found = product(lt_outer, b)
            for at, c in enumerate(outer):
                part[c * held : (c + 1) * held, :, :, lanes] = found[at * held : (at + 1) * held]
            if cols > 1:
                for there, side in ((first, 1), (last, -1)):
                    @pl.when(there)
                    def _():
                        early_hop(b, side).start()

        @pl.when(b == blocks)
        def _():
            if cols > 1:
                for there, side in ((first, 1), (last, -1)):
                    @pl.when(there)
                    def _():
                        for t in range(early, ahead_of_rest, couple):
                            hop(farthest(side), t, side).start()

            loads[-1].start()
            for at, c in enumerate(inner):
                turn_over(c, lt_inner, at)

        if inner:
            @pl.when((b >= blocks) & (b < 2 * blocks))
            def _():
                lanes = pl.ds(pl.multiple_of((b - blocks) * BLOCK, BLOCK), BLOCK)
                part[held : cols - held, :, :, lanes] = product(lt_inner, b - blocks)

        for side, hops, landing in ((1, me, from_left), (-1, cols - 1 - me, from_right)):
            c = b - DELAY * hops

            @pl.when(jnp.logical_not(end) & (c >= 0) & (c < blocks))
            def _():
                early_hop(c, side).wait_recv()
                d, lanes = farthest(side), pl.ds(pl.multiple_of(c * BLOCK, BLOCK), BLOCK)
                part[d, 0:early, :, lanes] += landing[d, 0:early, :, lanes]
                early_hop(c, side).start()

        return carry

    follow = jnp.where(end, 0, DELAY * jnp.maximum(me, cols - 1 - me))
    lax.fori_loop(0, blocks + jnp.maximum(follow, blocks), block, 0)

    for there, side in ((first, 1), (last, -1)):
        @pl.when(there)
        def _():
            @pl.loop(min(early, LEAD), units + LEAD * (cols - 1))
            def _(i):
                for d in far(side):
                    if d != near(side):
                        t = i - lag(d, side)

                        @pl.when((t >= (ahead_of_rest if d == farthest(side) else 0)) & (t < units) & starts(t))
                        def _():
                            hop(d, t, side).start()

            if shared:
                @pl.loop(shared, units - 1)
                def _(t):
                    for p in range(PIECES):
                        near_hop(t, p, side).start()

    for load in loads:
        load.wait()

    def pair(m):
        here = land.at[m, final]
        return remote(here, here, pair_send.at[0], pair_recv.at[m], {"col": beside})

    def consume(u, secret):
        real, imag = [], []
        for s in range(slow):
            lanes = slice(s * LANES, (s + 1) * LANES)
            x = [land[m, u, :, lanes] for m in range(rows)]
            real.append(sum(x[m] * table[2 * m + 2, s : s + 1] for m in range(rows)))
            imag.append(sum(x[m] * table[2 * m + 3, s : s + 1] for m in range(rows)))
        real, imag = swap_bits(real), swap_bits(imag)
        both = jnp.concatenate([jnp.concatenate(real, 0), jnp.concatenate(imag, 0)], 1)
        high = both.astype(jnp.bfloat16)
        low = (both - high.astype(jnp.float32)).astype(jnp.bfloat16)
        mixed = jnp.dot(
            jnp.concatenate([high, low, high], 1), w[...], preferred_element_type=jnp.float32
        )
        spread = []
        for s in range(slow):
            r = mixed[s * UNIT : (s + 1) * UNIT, :LANES]
            i = mixed[s * UNIT : (s + 1) * UNIT, LANES:]
            c, n = table[0, s : s + 1], table[1, s : s + 1]
            spread.append((r * c - i * n, r * n + i * c) if s else (r, i))
        for v, (r, i) in enumerate(fft(spread)):
            lanes = slice(v * LANES, (v + 1) * LANES)
            for k in range(2):
                a, b = cipher[k, 0, secret, :, lanes], cipher[k, 1, secret, :, lanes]
                acc[k, 0, :, lanes] += r * a - i * b
                acc[k, 1, :, lanes] += r * b + i * a

    extra = jnp.where(giver, 1, 0) if shared else 0
    late_from = jnp.maximum(units + LEAD - 2, shared + own_hold)

    def place(i):
        k = i - head
        group, r = k // 3, lax.rem(k, 3)
        mixed = jnp.where(r == 2, units + head + group, 2 * group + r)
        at_end = jnp.where(k < 0, units + i, jnp.where(group < shared - head, mixed, i - shared))
        m = i - late_from
        inside = jnp.where(m < 0, i - own_hold, shared + m)
        if late > 1:
            inside = jnp.where(m == late - 2, units - 1, jnp.where(m == late - 1, units - 2, inside))
        if late:
            inside = jnp.where(m == late, final, inside)
        early_ones = (i >= own_hold) & (i < own_hold + units - late)
        busy = jnp.where(
            end, (i >= 0) & (i < shared + units), early_ones | ((m >= 0) & (m < late + extra))
        )
        return busy, jnp.where(end, at_end, inside)

    def in_pieces(u):
        return jnp.logical_not(end) & (u >= shared) & (u < units - 1) if shared else False

    wait = jnp.where(end, END_LAG, LAG)
    rest = jnp.maximum(
        right_hold + LEAD * jnp.maximum(cols - 2 - me, 0), left_hold + LEAD * jnp.maximum(me - 1, 0)
    )
    rest = jnp.maximum(units + rest, own_hold + units - late + LAG)
    if late:
        rest = jnp.maximum(rest, late_from + late + extra + LAG)
    steps = jnp.where(end, shared + units + END_LAG, rest)

    def forward(d, side, i):
        beyond, hold, landing = (
            (d > me, right_hold, from_left) if side > 0 else (d < me, left_hold, from_right)
        )
        t = i - hold - lag(d, side)

        first_one = early if d == farthest(side) else 0

        @pl.when(jnp.logical_not(end) & beyond & (t >= first_one) & (t < units) & starts(t))
        def _():
            arrived(d, t, side)
            part[d, pl.ds(t, couple)] += landing[d, pl.ds(t, couple)]
            hop(d, t, side).start()

    def step_of(i, carry):
        for d in range(cols - 1, 1, -1):
            forward(d, 1, i)
        for d in range(cols - 2):
            forward(d, -1, i)
        if shared > head:
            g = i - HOLD * (cols - 3) - 1

            @pl.when(giver & (g >= 0) & (g < 2 * (shared - head)) & (lax.rem(g, 2) == 0))
            def _():
                give(head + g // 2).start()

        busy, u = place(i)

        if shared:
            @pl.when(end & (i == 0))
            def _():
                land[row, final] = part[beside, units - 1]
                for step in range(1, rows):
                    across(final, step).start()

            @pl.when(end & (i == LAG))
            def _():
                for step in range(1, rows):
                    across(final, step).wait_recv()
                for m in range(rows):
                    pair(m).start()

        @pl.when(busy & (u != final))
        def _():
            lent = u >= units
            d = jnp.where(lent, beside, me)
            t = jnp.where(lent, u - units, u)
            whole_left, whole_right = me > 0, me < cols - 1
            if shared:
                whole_left, whole_right = whole_left & (me != 1), whole_right & (me != cols - 2)

            @pl.when(end & (u == 0) & (cols > 1))
            def _():
                for there, side in ((last, 1), (first, -1)):
                    @pl.when(there)
                    def _():
                        @pl.loop(0, blocks)
                        def _(b):
                            early_hop(b, side).wait_recv()

            awaited, lead = starts(t), t
            if late > 1 and couple > 1:
                awaited = jnp.where(
                    jnp.logical_not(end) & (t >= units - 2), t == units - 1, awaited
                )
                lead = t - lax.rem(t, couple)
            awaited = awaited & jnp.logical_not(end & (t < early))

            @pl.when(whole_left & jnp.logical_not(lent))
            def _():
                @pl.when(awaited)
                def _():
                    arrived(me, lead, 1)

                part[me, t] += from_left[me, t]

            @pl.when(whole_right & jnp.logical_not(lent))
            def _():
                @pl.when(awaited)
                def _():
                    arrived(me, lead, -1)

                part[me, t] += from_right[me, t]

            @pl.when(jnp.logical_not(in_pieces(u)))
            def _():
                land[row, u] = part[d, t]
                for step in range(1, rows):
                    across(u, step).start()

            if shared:
                @pl.when(in_pieces(u))
                def _():
                    for p in range(PIECES):
                        for there, side, landing in ((me == 1, 1, from_left), (me == cols - 2, -1, from_right)):
                            @pl.when(there)
                            def _():
                                near_hop(u, p, side).wait_recv()
                                part[me, u, :, piece(p)] += landing[me, u, :, piece(p)]
                        land[row, u, :, piece(p)] = part[me, u, :, piece(p)]
                        for step in range(1, rows):
                            bit_across(u, step, p).start()

            if shared:
                @pl.when(lent)
                def _():
                    give(t).wait_recv()
                    swap(t).start()

        ready, v = place(i - wait)

        @pl.when(ready)
        def _():
            @pl.when(jnp.logical_not(in_pieces(v)) & (v != final))
            def _():
                for step in range(1, rows):
                    across(v, step).wait_recv()

            if shared:
                @pl.when(in_pieces(v))
                def _():
                    for step in range(1, rows):
                        for p in range(PIECES):
                            bit_across(v, step, p).wait_recv()

                @pl.when((v >= units) & (v != final))
                def _():
                    swap(v - units).wait_recv()

                @pl.when(v == final)
                def _():
                    for m in range(rows):
                        pair(m).wait_recv()
            consume(v, jnp.where(v == final, units - 1, v) if shared else v)

        return carry

    lax.fori_loop(0, steps, step_of, 0)

    width = half_sum.shape[2]
    for k in range(2):
        for p in range(2):
            total = jnp.sum(acc[k, p], axis=0, keepdims=True)
            for q in range(4):
                r = (2 * k + p) * 2 + q % 2
                half_sum[q // 2, r : r + 1, :] = total[:, q * width : (q + 1) * width]
    other = {"limb": 1 - limb}
    trade = remote(half_sum.at[1 - limb], half_in, limb_send.at[0], limb_recv.at[0], other)
    trade.start()
    trade.wait_recv()
    z_in[me] = half_sum[limb] + half_in[...]

    def tell(src, dst):
        return remote(z_in.at[src], z_in.at[src], z_send.at[0], z_recv.at[src], {"col": dst})

    tellers = range(1, cols - 1) if cols > 3 else range(cols)
    ahead = [(me + side * step) for step in range(cols - 1, 0, -1) for side in (1, -1)]
    if cols > 3:
        @pl.when(end)
        def _():
            tell(me, beside).start()

        for there, src in ((me == 1, 0), (me == cols - 2, cols - 1)):
            @pl.when(there)
            def _():
                tell(src, me).wait_recv()
                z_in[me] += z_in[src]

    for dst in ahead:
        @pl.when((jnp.logical_not(end) | (cols <= 3)) & (dst >= 0) & (dst < cols))
        def _():
            tell(me, dst).start()
    for there, side in ((first, 1), (last, -1)):
        @pl.when(there)
        def _():
            lane = 0 if side > 0 else 1
            for d in far(side):
                if d != near(side):
                    sent(part.at[d], send_sem.at[lane, d])
            for step in range(1, rows):
                sent(land.at[row, pl.ds(0, final + 1 if shared else units)], row_send.at[step - 1])
            if shared:
                if units - 1 > shared:
                    sent(part.at[near(side), pl.ds(shared, units - 1 - shared)], near_send.at[0])
                sent(land.at[:, final], pair_send.at[0])
                sent(cipher.at[grp, :, pl.ds(units, shared)], y_send.at[0])

    @pl.when(jnp.logical_not(end))
    def _():
        for d in range(cols - 1, 1, -1):
            @pl.when(d > me)
            def _():
                sent(part.at[d], send_sem.at[0, d])
        for d in range(cols - 2):
            @pl.when(d < me)
            def _():
                sent(part.at[d], send_sem.at[1, d])
        for step in range(1, rows):
            sent(land.at[row, pl.ds(0, units)], row_send.at[step - 1])

    if shared:
        @pl.when(giver)
        def _():
            sent(cipher.at[grp, :, pl.ds(units, shared)], s_send.at[0])

    for src in tellers:
        @pl.when(me != src)
        def _():
            tell(src, me).wait_recv()
    total = z_in[tellers[0]]
    for c in tellers[1:]:
        total = total + z_in[c]
    whole_sum[limb] = total
    gather = remote(whole_sum.at[limb], whole_sum.at[limb], limb_send.at[1], limb_recv.at[1], other)
    gather.start()
    gather.wait_recv()
    for k in range(2):
        for p in range(2):
            for q in range(4):
                r = (2 * k + p) * 2 + q % 2
                out_ref[k, p : p + 1, q * width : (q + 1) * width] = whole_sum[q // 2, r : r + 1, :]

    trade.wait_send()
    gather.wait_send()
    if cols > 3:
        @pl.when(end)
        def _():
            sent(z_in.at[0], z_send.at[0])

        @pl.when(jnp.logical_not(end))
        def _():
            sent(z_in.at[pl.ds(0, cols - 1)], z_send.at[0])
    elif cols > 1:
        sent(z_in.at[pl.ds(0, cols - 1)], z_send.at[0])


def tables(rows, row_dev, half):
    slow = row_dev // LANES
    degree = rows * row_dev
    scale = 1.0 / (math.sqrt(degree) * math.sqrt(2 * half))
    lane = np.arange(LANES)
    at = LANES // slow * (lane % slow) + lane // slow
    n = LANES * np.arange(slow)[:, None] + lane[None, :]
    a, m = np.arange(rows)[:, None, None, None], np.arange(rows)[None, :, None, None]
    turn = -np.pi * ((n + m * row_dev) * (2 * a + 1) % (2 * degree)) / degree
    turn = np.exp(1j * turn) * scale
    turn = np.stack([turn.real, turn.imag], 2).reshape(rows, 2 * rows, slow, LANES)
    twiddle = np.exp(-2j * np.pi * np.arange(slow)[:, None] * lane[None, :] / row_dev)
    twiddle = np.stack([twiddle.real, twiddle.imag], 0)
    twiddle = np.broadcast_to(twiddle, (rows,) + twiddle.shape)
    table = np.concatenate([twiddle, turn], 1).astype(np.float32)
    w = np.exp(-2j * np.pi * (at[:, None] * lane[None, :] % LANES) / LANES)
    w = np.block([[w.real, w.imag], [-w.imag, w.real]]).astype(np.float32)
    high = w.astype(jnp.bfloat16)
    low = (w - high.astype(np.float32)).astype(jnp.bfloat16)
    return table, np.concatenate([high, high, low], 0)


def body(database, lwe_matrix, secret_ct):
    rows, cols = lax.axis_size("row"), lax.axis_size("col")
    grps = lax.axis_size("grp")
    row_dev, depth = database.shape
    half = lwe_matrix.shape[2]
    own = half // cols
    units = own // UNIT
    slow = row_dev // LANES
    shared = units * 10 // 16 if cols > 3 and grps == 2 else 0
    places = units + shared + 1
    blocks = row_dev // BLOCK
    chunks = half // max(own, LANES)
    couple = PAIR if units % PAIR == 0 and EARLY % PAIR == 0 and NEXT % PAIR == 0 else 1
    table, w = tables(rows, row_dev, half)
    dma = pltpu.SemaphoreType.DMA
    flow = pltpu.VMEM((cols, units, UNIT, row_dev), jnp.float32)
    tail = max(units - 1 - shared, -(-shared // PIECES), 1)
    hbm = pl.BlockSpec(memory_space=pl.ANY)
    return pl.pallas_call(
        functools.partial(kernel, cols, rows, grps, shared),
        out_shape=jax.ShapeDtypeStruct((2, 2, row_dev), jnp.float32),
        in_specs=[hbm] * 5,
        out_specs=pl.BlockSpec(memory_space=pltpu.VMEM),
        scratch_shapes=[
            pltpu.VMEM((depth, half), lwe_matrix.dtype),
            pltpu.VMEM((min(2, chunks) * half // chunks, depth), lwe_matrix.dtype),
            pltpu.VMEM((max(chunks - 2, 1) * half // chunks, depth), lwe_matrix.dtype),
            pltpu.VMEM((blocks, BLOCK, depth), database.dtype),
            flow,
            flow,
            flow,
            pltpu.VMEM((rows, places, UNIT, row_dev), jnp.float32),
            pltpu.VMEM((2, 2, units + shared, UNIT, row_dev), jnp.float32),
            pltpu.VMEM(table.shape[1:], jnp.float32),
            pltpu.VMEM(w.shape, jnp.bfloat16),
            pltpu.VMEM((2, 2, UNIT, row_dev), jnp.float32),
            pltpu.VMEM((2, 8, row_dev // 4), jnp.float32),
            pltpu.VMEM((8, row_dev // 4), jnp.float32),
            pltpu.VMEM((cols, 8, row_dev // 4), jnp.float32),
            pltpu.VMEM((2, 8, row_dev // 4), jnp.float32),
            dma((3,)),
            dma((chunks,)),
            dma((AHEAD,)),
            dma((2, cols)),
            dma((cols if shared and cols == 4 else cols + 1, units // couple)),
            dma((max(rows - 1, 1),)),
            dma((max(rows - 1, 1), places)),
            dma((1,)),
            dma((1,)),
            dma((2,)),
            dma((2,)),
            dma((1,)),
            dma((cols,)),
            dma((1,)),
            dma((tail, PIECES)),
            dma((max(rows - 1, 1), tail, PIECES)),
            dma((1,)),
            dma((rows,)),
            dma((2, blocks)),
        ],
        compiler_params=pltpu.CompilerParams(
            collective_id=0, has_side_effects=True, vmem_limit_bytes=55168 << 10
        ),
    )(
        lwe_matrix[:, 0, :],
        database,
        secret_ct[:, :, 0].reshape(2, 2, units, UNIT, row_dev),
        jnp.asarray(table),
        jnp.asarray(w),
    )


def solution(mesh):
    placed = (P(("grp", "row"), "col"), P("col", "limb", None), P(None, None, "limb", "col", "row"))
    return jax.shard_map(
        body, mesh=mesh, in_specs=placed, out_specs=P("grp", None, "row"), check_vma=False
    )
```
